32 devices in a mesh: dp: 8 (over y, x, core), seq: 4 (over z).
Axes of the slice: x: 2, y: 2, z: 4, core: 2. Of those that a mesh axis runs over, the one named last changes fastest.
Arguments:
- block_in: bfloat16 [8, 1024, 1024], P('dp', 'seq'), may hold values from -6 to 6
- segment_ids: int32 [8, 1024], P('dp'), may hold values from 0 to 2, never falling along the last dimension, each value on 1 to 512 neighbouring positions
- mamba_z: bfloat16 [1024, 1536], P(('dp', 'seq')), may hold values from -0.1875 to 0.1875
- mamba_x: bfloat16 [1024, 1536], P(('dp', 'seq')), may hold values from -0.1875 to 0.1875
- mamba_bc: bfloat16 [1024, 256], P(('dp', 'seq')), may hold values from -0.1875 to 0.1875
- mamba_dt: bfloat16 [1024, 24], P(('dp', 'seq')), may hold values from -0.1875 to 0.1875
- mamba_out: bfloat16 [1024, 1536], P(('dp', 'seq')), may hold values from -0.15625 to 0.15625
- attn_q: bfloat16 [1024, 512], P(('dp', 'seq')), may hold values from -0.1875 to 0.1875
- attn_kv: bfloat16 [1024, 256], P(('dp', 'seq')), may hold values from -0.1875 to 0.1875
- attn_out: bfloat16 [1024, 512], P(('dp', 'seq')), may hold values from -2 to 2
- ffn_gate: bfloat16 [1024, 2048], P(('dp', 'seq')), may hold values from -0.1875 to 0.1875
- ffn_up: bfloat16 [1024, 2048], P(('dp', 'seq')), may hold values from -0.1875 to 0.1875
- ffn_down: bfloat16 [1024, 2048], P(('dp', 'seq')), may hold values from -0.125 to 0.125
- mixer_norm: bfloat16 [1024], P(('dp', 'seq')), may hold values from 0.5 to 1.5
- ffn_norm: bfloat16 [1024], P(('dp', 'seq')), may hold values from 0.5 to 1.5
- conv_weight: float32 [4, 1792], replicated, may hold values from -3 to 3
- conv_bias: float32 [1792], replicated, may hold values from -0.5 to 0.5
- dt_bias: float32 [24], replicated, may hold values from -1 to 1
- a_log: float32 [24], replicated, may hold values from -6.5 to -3
- d_skip: float32 [24], replicated, may hold values from 0.5 to 1.5
- inner_norm: float32 [1536], replicated, may hold values from 0.5 to 1.5
- grad_out: bfloat16 [8, 1024, 1024], P('dp', 'seq'), may hold values from -6 to 6
Outputs:
- block_out: bfloat16 [8, 1024, 1024], P('dp', 'seq')
- grad_in: bfloat16 [8, 1024, 1024], P('dp', 'seq')
- grad_mamba_z: float32 [1024, 1536], P(('dp', 'seq'))
- grad_mamba_x: float32 [1024, 1536], P(('dp', 'seq'))
- grad_mamba_bc: float32 [1024, 256], P(('dp', 'seq'))
- grad_mamba_dt: float32 [1024, 24], P(('dp', 'seq'))
- grad_mamba_out: float32 [1024, 1536], P(('dp', 'seq'))
- grad_attn_q: float32 [1024, 512], P(('dp', 'seq'))
- grad_attn_kv: float32 [1024, 256], P(('dp', 'seq'))
- grad_attn_out: float32 [1024, 512], P(('dp', 'seq'))
- grad_ffn_gate: float32 [1024, 2048], P(('dp', 'seq'))
- grad_ffn_up: float32 [1024, 2048], P(('dp', 'seq'))
- grad_ffn_down: float32 [1024, 2048], P(('dp', 'seq'))
- grad_mixer_norm: float32 [1024], P(('dp', 'seq'))
- grad_ffn_norm: float32 [1024], P(('dp', 'seq'))
- grad_conv_weight: float32 [4, 1792], replicated
- grad_conv_bias: float32 [1792], replicated
- grad_dt_bias: float32 [24], replicated
- grad_a_log: float32 [24], replicated
- grad_d_skip: float32 [24], replicated
- grad_inner_norm: float32 [1536], replicated
The draws below stay inside these ranges and needn't reach their ends.
Inputs may be any that keep to these rules, and one draw needn't show every extreme that they name: `segment_ids`: along each sequence the ids start at 0 and never fall, so that equal ids form one run of tokens; a document has at most 512 tokens.
All inputs are finite; a program needn't handle non-finite values.
Results may differ from the reference program's by a relative error of at most 0.013.
Values may be sent and summed in bfloat16 or wider, within the bound.
No kernel may reach another device: no remote copies, remote signals or barrier semaphores. Data moves between devices by JAX's collectives and lax.ppermute only.
A program may use at most 256 MiB of HBM per device.

```python
import math
import jax
import jax.numpy as jnp
import numpy as np
from jax import lax

D = 1024
SSM_HEADS = 24
SSM_HEAD = 64
STATE = 128
Q_HEADS = 8
KV_HEADS = 2
HEAD = 64
FF = 2048
CONV = 4
LEN = 1024
BATCH = 8
INNER = 1536
CHANNELS = 1792
N_SEQ = 4


def strengthened(drawn, own_key, source, target, blocks, factor):
    owner, partner = [(jnp.arange(drawn.shape[dim]) // (drawn.shape[dim] // blocks)).reshape([-1 if axis == dim else 1 for axis in range(drawn.ndim)]) for dim in (source, target)]
    chosen = jax.random.permutation(own_key, blocks)[partner]
    strong = (owner == chosen) | (owner == (partner + blocks // 2) % blocks)
    return jnp.where(strong, factor * drawn, drawn)


def shard_levels(key, dims, split, smallest, high):
    loudness, own = 1.0, jax.random.fold_in(key, 6)
    for axis_at, blocks in split:
        steps = jnp.exp(jax.random.uniform(jax.random.fold_in(own, axis_at), (blocks,), jnp.float32, smallest / len(split), high / len(split)))
        loudness = loudness * jnp.repeat(steps, dims[axis_at] // blocks).reshape([-1 if axis == axis_at else 1 for axis in range(len(dims))])
    return loudness


def split_up(number_of, total, bound, lean):
    portions = [(1 << 20) // math.isqrt(standing ** lean) + 1 for standing in range(2, number_of + 1)]
    surplus, counts = total - bound - (number_of - 1), [1] * (number_of - 1)
    while surplus > 0:
        candidates = [i for i in range(number_of - 1) if counts[i] < bound]
        mass, budget = sum([portions[i] for i in candidates]), surplus
        for i in candidates:
            extra = min(bound - counts[i], max(1, budget * portions[i] // mass), surplus)
            counts[i] = counts[i] + extra
            surplus = surplus - extra
    return np.array([bound] + counts)


def uneven(own_key, count, total, limit, skew):
    if count == 2:
        one = jax.random.randint(own_key, (), max(1, total - limit), min(limit, total - 1) + 1)
        return jnp.stack([one, total - one])
    lengths = jnp.asarray(split_up(count, total, limit, skew), jnp.int32)
    couples = (count - 1) // 2
    source_of, receiver = lengths[1:1 + 2 * couples:2], lengths[2:2 + 2 * couples:2]
    margin = jnp.minimum(source_of - 1, limit - receiver)
    passed = jax.random.randint(jax.random.fold_in(own_key, 1), (couples,), 0, 1 << 20) % (margin + 1)
    lengths = lengths.at[1:1 + 2 * couples:2].set(source_of - passed).at[2:2 + 2 * couples:2].set(receiver + passed)
    return lengths[jax.random.permutation(jax.random.fold_in(own_key, 2), count)]


def gaussian(own_key, extent, scale, limit, cuts=(), kind=jnp.bfloat16):
    values = scale * jax.random.normal(own_key, extent, jnp.float32)
    if cuts:
        values = values * shard_levels(own_key, extent, cuts, -0.22, 0.18)
    return jnp.clip(values, -limit, limit).astype(kind)


def bell_draw_with(key, extent, deviation, bound, pieces, heavy, kind=jnp.bfloat16):
    values = deviation * jax.random.normal(key, extent, jnp.float32)
    if pieces:
        values = values * shard_levels(key, extent, pieces, -0.22, 0.18)
    return jnp.clip(strengthened(values, jax.random.fold_in(key, 3), *heavy), -bound, bound).astype(kind)


def setup_inputs(seed: int = 0) -> dict:
    arg_keys = jax.random.split(jax.random.key(seed), 23)
    block_in = gaussian(arg_keys[0], (BATCH, LEN, D), 1.0, 6.0, ((0, 8), (1, 4)))
    segment_ids = jax.vmap(lambda own: jnp.searchsorted(jnp.cumsum(uneven(own, 3, LEN, LEN // 2, 2)), jnp.arange(LEN), side="right"))(jax.random.split(arg_keys[1], BATCH)).reshape((BATCH, LEN)).astype(jnp.int32)
    mamba_z = gaussian(arg_keys[2], (D, INNER), D ** -0.5, 0.1875, ((0, 32),))
    mamba_x = gaussian(arg_keys[3], (D, INNER), D ** -0.5, 0.1875, ((0, 32),))
    mamba_bc = gaussian(arg_keys[4], (D, 2 * STATE), D ** -0.5, 0.1875, ((0, 32),))
    mamba_dt = gaussian(arg_keys[5], (D, SSM_HEADS), D ** -0.5, 0.1875, ((0, 32),))
    mamba_out = gaussian(arg_keys[6], (D, INNER), INNER ** -0.5, 0.15625, ((0, 32),))
    attn_q = gaussian(arg_keys[7], (D, Q_HEADS * HEAD), D ** -0.5, 0.1875, ((0, 32),))
    attn_kv = gaussian(arg_keys[8], (D, 2 * KV_HEADS * HEAD), D ** -0.5, 0.1875, ((0, 32),))
    attn_out = gaussian(arg_keys[9], (D, Q_HEADS * HEAD), (max(Q_HEADS * HEAD // 64, 1)) ** -0.5, 2.0, ((0, 32),))
    ffn_gate = gaussian(arg_keys[10], (D, FF), D ** -0.5, 0.1875, ((0, 32),))
    ffn_up = gaussian(arg_keys[11], (D, FF), D ** -0.5, 0.1875, ((0, 32),))
    ffn_down = gaussian(arg_keys[12], (D, FF), FF ** -0.5, 0.125, ((0, 32),))
    mixer_norm = jnp.clip(1.0 + 0.1 * jax.random.normal(arg_keys[13], (D,), jnp.float32), 0.5, 1.5).astype(jnp.bfloat16)
    ffn_norm = jnp.clip(1.0 + 0.1 * jax.random.normal(arg_keys[14], (D,), jnp.float32), 0.5, 1.5).astype(jnp.bfloat16)
    conv_weight = gaussian(arg_keys[15], (CONV, CHANNELS), CONV ** -0.5, 3.0, (), jnp.float32)
    conv_bias = jnp.clip(jax.random.uniform(arg_keys[16], (CHANNELS,), jnp.float32, -0.5, 0.5), -0.5, 0.5)
    dt_bias = jnp.clip(jax.random.uniform(arg_keys[17], (SSM_HEADS,), jnp.float32, -1.0, 1.0), -1.0, 1.0)
    a_log = jnp.clip(jax.random.uniform(arg_keys[18], (SSM_HEADS,), jnp.float32, -6.5, -3.0), -6.5, -3.0)
    d_skip = jnp.clip(jax.random.uniform(arg_keys[19], (SSM_HEADS,), jnp.float32, 0.5, 1.5), 0.5, 1.5)
    inner_norm = jnp.clip(1.0 + 0.1 * jax.random.normal(arg_keys[20], (INNER,), jnp.float32), 0.5, 1.5)
    grad_out = bell_draw_with(arg_keys[21], (BATCH, LEN, D), 1.0, 6.0, ((0, 8), (1, 4)), (0, 2, 8, 2.0))
    return dict(block_in=block_in, segment_ids=segment_ids, mamba_z=mamba_z, mamba_x=mamba_x, mamba_bc=mamba_bc, mamba_dt=mamba_dt, mamba_out=mamba_out, attn_q=attn_q, attn_kv=attn_kv, attn_out=attn_out, ffn_gate=ffn_gate, ffn_up=ffn_up, ffn_down=ffn_down, mixer_norm=mixer_norm, ffn_norm=ffn_norm, conv_weight=conv_weight, conv_bias=conv_bias, dt_bias=dt_bias, a_log=a_log, d_skip=d_skip, inner_norm=inner_norm, grad_out=grad_out)


EPSILON = 1e-05
ROPE_BASE = 100000000000.0

def silu_grad(value):
    sigma = jax.nn.sigmoid(value)
    return sigma * (1.0 + value * (1.0 - sigma))

def rms_forward(value, gain):
    factor = lax.rsqrt(lax.optimization_barrier(jnp.mean(value * value, axis=-1, keepdims=True)) + EPSILON)
    return (value * factor * gain, factor)

def rms_backward(value, factor, gain, upstream):
    weighted = upstream * gain
    gain_grad = lax.optimization_barrier(jnp.sum(upstream * value * factor, axis=0))
    inward = factor * weighted - value * factor * factor * factor * lax.optimization_barrier(jnp.mean(weighted * value, axis=-1, keepdims=True))
    return (inward, gain_grad)

def matmul(left, right):
    return jnp.dot(left, right, preferred_element_type=jnp.float32)

def rope_tables(positions, head_size):
    half = head_size // 2
    freq_scale = ROPE_BASE ** (-jnp.arange(half, dtype=jnp.float32) / half)
    angles = positions.astype(jnp.float32)[:, None] * freq_scale[None, :]
    return (jnp.cos(angles), jnp.sin(angles))

def rotate(value, cosine, sine):
    half = value.shape[-1] // 2
    first = value[..., :half]
    second = value[..., half:]
    return jnp.concatenate([first * cosine - second * sine, second * cosine + first * sine], axis=-1)

def rotate_back(grad, cosine, sine):
    half = grad.shape[-1] // 2
    first = grad[..., :half]
    second = grad[..., half:]
    return jnp.concatenate([first * cosine + second * sine, second * cosine - first * sine], axis=-1)

def block_masks(local_ids, prior_id):
    count = local_ids.shape[1]
    order = jnp.arange(count)
    pair = (order[:, None] >= order[None, :])[None] & (local_ids[:, :, None] == local_ids[:, None, :])
    inbound = (local_ids == prior_id[:, None]).astype(jnp.float32)
    outbound = (local_ids == local_ids[:, -1:]).astype(jnp.float32)
    return (pair, inbound, outbound)

def block_summary(xs, bmat, step, a_log, inbound, outbound):
    decay = jnp.cumsum(step * -jnp.exp(a_log), axis=1)
    tail = jnp.exp(decay[:, -1:, :] - decay) * outbound[:, :, None] * step
    state_out = jnp.einsum('suh,suhp,sun->shpn', tail, xs, bmat, precision=lax.Precision.HIGHEST)
    carry = jnp.exp(decay[:, -1, :]) * inbound[:, -1:]
    return (state_out, carry)

def block_output(xs, bmat, cmat, step, a_log, d_skip, state_in, pair, inbound):
    decay = jnp.cumsum(step * -jnp.exp(a_log), axis=1)
    spread = decay[:, :, None, :] - decay[:, None, :, :]
    mask = pair[:, :, :, None]
    kernel = jnp.where(mask, jnp.exp(jnp.where(mask, spread, 0.0)), 0.0)
    intersection_cb = jnp.einsum('stn,sun->stu', cmat, bmat, precision=lax.Precision.HIGHEST)
    mixed = kernel * intersection_cb[:, :, :, None] * step[:, None, :, :]
    local_part = jnp.einsum('stuh,suhp->sthp', mixed, xs, precision=lax.Precision.HIGHEST)
    entry = jnp.exp(decay) * inbound[:, :, None]
    carried = entry[:, :, :, None] * jnp.einsum('stn,shpn->sthp', cmat, state_in, precision=lax.Precision.HIGHEST)
    return local_part + carried + d_skip[:, None] * xs

def reference(block_in, segment_ids, mamba_z, mamba_x, mamba_bc, mamba_dt, mamba_out, attn_q, attn_kv, attn_out, ffn_gate, ffn_up, ffn_down, mixer_norm, ffn_norm, conv_weight, conv_bias, dt_bias, a_log, d_skip, inner_norm, grad_out):
    taps = CONV
    group = Q_HEADS // KV_HEADS
    piece = LEN // N_SEQ
    parts = N_SEQ
    inv_root = HEAD ** (-0.5)
    gain_one = mixer_norm.astype(jnp.float32)
    gain_two = ffn_norm.astype(jnp.float32)
    positions = jnp.arange(LEN, dtype=jnp.int32)
    cosine, sine = rope_tables(positions, HEAD)
    cos_b = cosine[:, None, :]
    sin_b = sine[:, None, :]
    causal = positions[None, :] <= positions[:, None]

    def ssm_sequence(xs, bmat, cmat, step, alog_in, skip_in, ids):
        xs_p = xs.reshape(parts, 1, piece, SSM_HEADS, SSM_HEAD)
        bmat_p = bmat.reshape(parts, 1, piece, STATE)
        cmat_p = cmat.reshape(parts, 1, piece, STATE)
        step_p = step.reshape(parts, 1, piece, SSM_HEADS)
        ids_p = ids.reshape(parts, 1, piece)
        last_ids = ids_p[:, :, -1]
        prior_p = jnp.concatenate([jnp.full((1, 1), -1, jnp.int32), last_ids[:-1]], axis=0)

        def advance(state, items):
            xs_c, bmat_c, cmat_c, step_c, ids_c, prior_c = items
            pair, inbound, outbound = block_masks(ids_c, prior_c)
            result = block_output(xs_c, bmat_c, cmat_c, step_c, alog_in, skip_in, state, pair, inbound)
            summary, carry = block_summary(xs_c, bmat_c, step_c, alog_in, inbound, outbound)
            return (carry[:, :, None, None] * state + summary, result)
        start = jnp.zeros((1, SSM_HEADS, SSM_HEAD, STATE), jnp.float32)
        final_state, results = lax.scan(advance, start, (xs_p, bmat_p, cmat_p, step_p, ids_p, prior_p))
        return results.reshape(LEN, SSM_HEADS, SSM_HEAD)

    def one_sequence(totals, items):
        seq_in, ids, seq_grad = items
        x_in = seq_in.astype(jnp.float32)
        normed, factor_one = rms_forward(x_in, gain_one)
        normed_b = normed.astype(jnp.bfloat16)
        gate_z = matmul(normed_b, mamba_z)
        inner_u = jnp.concatenate([matmul(normed_b, mamba_x), matmul(normed_b, mamba_bc)], axis=1)
        step_raw = matmul(normed_b, mamba_dt)
        padded_u = jnp.pad(inner_u, ((taps - 1, 0), (0, 0)))
        padded_ids = jnp.concatenate([jnp.full((taps - 1,), -1, jnp.int32), ids])
        tap_masks = [(padded_ids[tap:tap + LEN] == ids).astype(jnp.float32)[:, None] for tap in range(taps)]
        conv_pre = jnp.zeros_like(inner_u) + conv_bias
        for tap in range(taps):
            conv_pre = conv_pre + conv_weight[tap] * padded_u[tap:tap + LEN] * tap_masks[tap]
        activated = jax.nn.silu(conv_pre)
        xs = activated[:, :INNER].reshape(LEN, SSM_HEADS, SSM_HEAD)
        bmat = activated[:, INNER:INNER + STATE]
        cmat = activated[:, INNER + STATE:]
        step = jax.nn.softplus(step_raw + dt_bias)

        def ssm_of(xs_a, bmat_a, cmat_a, step_a, alog_a, skip_a):
            return ssm_sequence(xs_a, bmat_a, cmat_a, step_a, alog_a, skip_a, ids)
        ssm_out, pullback = jax.vjp(ssm_of, xs, bmat, cmat, step, a_log, d_skip)
        silu_z = jax.nn.silu(gate_z)
        gated = ssm_out.reshape(LEN, INNER) * silu_z
        mixed_norm, factor_m = rms_forward(gated, inner_norm)
        mixed_b = mixed_norm.astype(jnp.bfloat16)
        mixer_a = matmul(mixed_b, mamba_out.T)
        query = matmul(normed_b, attn_q).reshape(LEN, Q_HEADS, HEAD)
        keyval = matmul(normed_b, attn_kv).reshape(LEN, 2 * KV_HEADS, HEAD)
        query_b = rotate(query, cos_b, sin_b).astype(jnp.bfloat16)
        keys = rotate(keyval[:, :KV_HEADS], cos_b, sin_b).astype(jnp.bfloat16)
        values = keyval[:, KV_HEADS:].astype(jnp.bfloat16)
        allowed = causal & (ids[None, :] == ids[:, None])
        query_g = query_b.reshape(LEN, KV_HEADS, group, HEAD)
        scores = jnp.einsum('tkgd,lkd->kgtl', query_g.astype(jnp.float32), keys.astype(jnp.float32)) * inv_root
        scores = jnp.where(allowed[None, None], scores, -1e+30)
        top = lax.optimization_barrier(jnp.max(scores, axis=-1, keepdims=True))
        lse = top + jnp.log(lax.optimization_barrier(jnp.sum(jnp.exp(scores - top), axis=-1, keepdims=True)))
        probs = jnp.exp(scores - lse)
        probs_b = probs.astype(jnp.bfloat16)
        attended = jnp.einsum('kgtl,lkd->tkgd', probs_b.astype(jnp.float32), values.astype(jnp.float32))
        attended_b = attended.reshape(LEN, Q_HEADS * HEAD).astype(jnp.bfloat16)
        attn_a = matmul(attended_b, attn_out.T)
        mid = x_in + mixer_a + attn_a
        fnormed, factor_two = rms_forward(mid, gain_two)
        fnormed_b = fnormed.astype(jnp.bfloat16)
        gate_h = matmul(fnormed_b, ffn_gate)
        up_h = matmul(fnormed_b, ffn_up)
        hidden_b = (jax.nn.silu(gate_h) * up_h).astype(jnp.bfloat16)
        seq_out = (mid + matmul(hidden_b, ffn_down.T)).astype(jnp.bfloat16)
        g_down = matmul(seq_grad.T, hidden_b)
        d_hidden = matmul(seq_grad, ffn_down)
        d_gate_b = (d_hidden * up_h * silu_grad(gate_h)).astype(jnp.bfloat16)
        d_up_b = (d_hidden * jax.nn.silu(gate_h)).astype(jnp.bfloat16)
        g_gate = matmul(fnormed_b.T, d_gate_b)
        g_up = matmul(fnormed_b.T, d_up_b)
        d_fnorm = matmul(d_gate_b, ffn_gate.T) + matmul(d_up_b, ffn_up.T)
        d_mid_norm, g_fnorm = rms_backward(mid, factor_two, gain_two, d_fnorm)
        d_mid = seq_grad.astype(jnp.float32) + d_mid_norm
        d_mid_b = d_mid.astype(jnp.bfloat16)
        g_mout = matmul(d_mid_b.T, mixed_b)
        d_mnorm = matmul(d_mid_b, mamba_out)
        d_gated, g_inner = rms_backward(gated, factor_m, inner_norm, d_mnorm)
        d_ssm = (d_gated * silu_z).reshape(LEN, SSM_HEADS, SSM_HEAD)
        d_z = d_gated * ssm_out.reshape(LEN, INNER) * silu_grad(gate_z)
        d_xs, d_bmat, d_cmat, d_step, g_alog, g_skip = pullback(d_ssm)
        d_act = jnp.concatenate([d_xs.reshape(LEN, INNER), d_bmat, d_cmat], axis=1)
        d_pre = d_act * silu_grad(conv_pre)
        g_cbias = lax.optimization_barrier(jnp.sum(d_pre, axis=0))
        g_cweight = jnp.stack([lax.optimization_barrier(jnp.sum(d_pre * padded_u[tap:tap + LEN] * tap_masks[tap], axis=0)) for tap in range(taps)])
        d_padded = jnp.zeros_like(padded_u)
        for tap in range(taps):
            d_padded = d_padded + jnp.pad(d_pre * tap_masks[tap] * conv_weight[tap], ((tap, taps - 1 - tap), (0, 0)))
        d_inner = d_padded[taps - 1:]
        d_step_raw = d_step * jax.nn.sigmoid(step_raw + dt_bias)
        g_dtb = lax.optimization_barrier(jnp.sum(d_step_raw, axis=0))
        d_att_b = matmul(d_mid_b, attn_out).astype(jnp.bfloat16)
        g_aout = matmul(d_mid_b.T, attended_b)
        d_att_g = d_att_b.reshape(LEN, KV_HEADS, group, HEAD).astype(jnp.float32)
        d_probs = jnp.einsum('tkgd,lkd->kgtl', d_att_g, values.astype(jnp.float32))
        d_scores = probs * (d_probs - lax.optimization_barrier(jnp.sum(probs * d_probs, axis=-1, keepdims=True)))
        d_scores_f = d_scores.astype(jnp.bfloat16).astype(jnp.float32)
        d_query = jnp.einsum('kgtl,lkd->tkgd', d_scores_f, keys.astype(jnp.float32)) * inv_root
        d_keys = jnp.einsum('kgtl,tkgd->lkd', d_scores_f, query_g.astype(jnp.float32)) * inv_root
        d_values = jnp.einsum('kgtl,tkgd->lkd', probs_b.astype(jnp.float32), d_att_g)
        d_q_b = rotate_back(d_query.reshape(LEN, Q_HEADS, HEAD), cos_b, sin_b).reshape(LEN, Q_HEADS * HEAD).astype(jnp.bfloat16)
        d_kv_b = jnp.concatenate([rotate_back(d_keys, cos_b, sin_b), d_values], axis=1).reshape(LEN, 2 * KV_HEADS * HEAD).astype(jnp.bfloat16)
        d_z_b = d_z.astype(jnp.bfloat16)
        d_x_b = d_inner[:, :INNER].astype(jnp.bfloat16)
        d_bc_b = d_inner[:, INNER:].astype(jnp.bfloat16)
        d_st_b = d_step_raw.astype(jnp.bfloat16)
        g_z = matmul(normed_b.T, d_z_b)
        g_x = matmul(normed_b.T, d_x_b)
        g_bc = matmul(normed_b.T, d_bc_b)
        g_dt = matmul(normed_b.T, d_st_b)
        g_q = matmul(normed_b.T, d_q_b)
        g_kv = matmul(normed_b.T, d_kv_b)
        d_norm = matmul(d_z_b, mamba_z.T) + matmul(d_x_b, mamba_x.T) + matmul(d_bc_b, mamba_bc.T)
        d_norm = d_norm + matmul(d_st_b, mamba_dt.T) + matmul(d_q_b, attn_q.T) + matmul(d_kv_b, attn_kv.T)
        d_in_norm, g_mnorm = rms_backward(x_in, factor_one, gain_one, d_norm)
        seq_grad_in = (d_mid + d_in_norm).astype(jnp.bfloat16)
        terms = (g_z, g_x, g_bc, g_dt, g_mout, g_q, g_kv, g_aout, g_gate, g_up, g_down, g_mnorm, g_fnorm, g_cweight, g_cbias, g_dtb, g_alog, g_skip, g_inner)
        return (jax.tree.map(jnp.add, totals, terms), (seq_out, seq_grad_in))
    zero_totals = (jnp.zeros((D, INNER), jnp.float32), jnp.zeros((D, INNER), jnp.float32), jnp.zeros((D, 2 * STATE), jnp.float32), jnp.zeros((D, SSM_HEADS), jnp.float32), jnp.zeros((D, INNER), jnp.float32), jnp.zeros((D, Q_HEADS * HEAD), jnp.float32), jnp.zeros((D, 2 * KV_HEADS * HEAD), jnp.float32), jnp.zeros((D, Q_HEADS * HEAD), jnp.float32), jnp.zeros((D, FF), jnp.float32), jnp.zeros((D, FF), jnp.float32), jnp.zeros((D, FF), jnp.float32), jnp.zeros((D,), jnp.float32), jnp.zeros((D,), jnp.float32), jnp.zeros((CONV, CHANNELS), jnp.float32), jnp.zeros((CHANNELS,), jnp.float32), jnp.zeros((SSM_HEADS,), jnp.float32), jnp.zeros((SSM_HEADS,), jnp.float32), jnp.zeros((SSM_HEADS,), jnp.float32), jnp.zeros((INNER,), jnp.float32))
    totals, stacked = lax.scan(one_sequence, zero_totals, (block_in, segment_ids, grad_out))
    return (stacked[0], stacked[1], totals[0], totals[1], totals[2], totals[3], totals[4], totals[5], totals[6], totals[7], totals[8], totals[9], totals[10], totals[11], totals[12], totals[13], totals[14], totals[15], totals[16], totals[17], totals[18])
```

```python
import jax
import jax.numpy as jnp
from jax import lax
from jax.sharding import PartitionSpec as P

SSM_HEADS = 24
SSM_HEAD = 64
STATE = 128
Q_HEADS = 8
KV_HEADS = 2
HEAD = 64


EPSILON = 1e-05
ROPE_BASE = 100000000000.0
MAX_DOC = 512
LANES = 128


def passed_along(block, axis, distance):
    devices = range(lax.axis_size(axis))
    route = [(i - distance, i) for i in devices if i - distance in devices]
    return lax.ppermute(block, axis, route)


def scattered(grad):
    part = lax.psum_scatter(grad, "dp", scatter_dimension=0, tiled=True)
    return lax.psum_scatter(part, "seq", scatter_dimension=0, tiled=True).astype(jnp.float32)


def silu_grad(value):
    sigma = jax.nn.sigmoid(value)
    return sigma * (1.0 + value * (1.0 - sigma))


def rms_forward(value, gain):
    factor = lax.rsqrt(jnp.mean(value * value, axis=-1, keepdims=True) + EPSILON)
    return (value * factor * gain, factor)


def rms_backward(value, factor, gain, upstream):
    weighted = upstream * gain
    gain_grad = jnp.sum(upstream * value * factor, axis=0)
    inward = factor * weighted - value * factor * factor * factor * jnp.mean(
        weighted * value, axis=-1, keepdims=True
    )
    return (inward, gain_grad)


def matmul(left, right):
    return jnp.dot(left, right, preferred_element_type=jnp.float32)


def matmul_nt(left, right):
    return lax.dot_general(
        left, right, (((1,), (1,)), ((), ())), preferred_element_type=jnp.float32
    )


def matmul_tn(left, right):
    return lax.dot_general(
        left, right, (((0,), (0,)), ((), ())), preferred_element_type=jnp.float32
    )


def rope_tables(positions, head_size):
    half = head_size // 2
    freq_scale = ROPE_BASE ** (-jnp.arange(half, dtype=jnp.float32) / half)
    angles = positions.astype(jnp.float32)[:, None] * freq_scale[None, :]
    return (jnp.cos(angles), jnp.sin(angles))


def rotate(value, cosine, sine):
    half = value.shape[-1] // 2
    first = value[..., :half]
    second = value[..., half:]
    return jnp.concatenate(
        [first * cosine - second * sine, second * cosine + first * sine], axis=-1
    )


def rotate_back(grad, cosine, sine):
    half = grad.shape[-1] // 2
    first = grad[..., :half]
    second = grad[..., half:]
    return jnp.concatenate(
        [first * cosine + second * sine, second * cosine - first * sine], axis=-1
    )


def block_masks(local_ids, prior_id):
    count = local_ids.shape[1]
    order = jnp.arange(count)
    pair = (order[:, None] >= order[None, :])[None] & (
        local_ids[:, :, None] == local_ids[:, None, :]
    )
    inbound = (local_ids == prior_id[:, None]).astype(jnp.float32)
    outbound = (local_ids == local_ids[:, -1:]).astype(jnp.float32)
    return (pair, inbound, outbound)


def block_summary(xs, bmat, step, a_log, inbound, outbound):
    decay = jnp.cumsum(step * -jnp.exp(a_log), axis=1)
    tail = jnp.exp(decay[:, -1:, :] - decay) * outbound[:, :, None] * step
    state_out = jnp.einsum("suh,suhp,sun->shpn", tail, xs, bmat, precision=lax.Precision.HIGHEST)
    carry = jnp.exp(decay[:, -1, :]) * inbound[:, -1:]
    return (state_out, carry)


def block_output(xs, bmat, cmat, step, a_log, d_skip, state_in, pair, inbound):
    decay = jnp.cumsum(step * -jnp.exp(a_log), axis=1)
    spread = decay[:, :, None, :] - decay[:, None, :, :]
    mask = pair[:, :, :, None]
    kernel = jnp.where(mask, jnp.exp(jnp.where(mask, spread, 0.0)), 0.0)
    intersection_cb = jnp.einsum("stn,sun->stu", cmat, bmat, precision=lax.Precision.HIGHEST)
    mixed = kernel * intersection_cb[:, :, :, None] * step[:, None, :, :]
    local_part = jnp.einsum("stuh,suhp->sthp", mixed, xs, precision=lax.Precision.HIGHEST)
    entry = jnp.exp(decay) * inbound[:, :, None]
    carried = entry[:, :, :, None] * jnp.einsum(
        "stn,shpn->sthp", cmat, state_in, precision=lax.Precision.HIGHEST
    )
    return local_part + carried + d_skip[:, None] * xs


def local(
    block_in,
    segment_ids,
    mamba_z,
    mamba_x,
    mamba_bc,
    mamba_dt,
    mamba_out,
    attn_q,
    attn_kv,
    attn_out,
    ffn_gate,
    ffn_up,
    ffn_down,
    mixer_norm,
    ffn_norm,
    conv_weight,
    conv_bias,
    dt_bias,
    a_log,
    d_skip,
    inner_norm,
    grad_out,
):
    sequences, rows, width = block_in.shape
    length = segment_ids.shape[1]
    taps = conv_weight.shape[0]
    group = Q_HEADS // KV_HEADS
    inner_width = SSM_HEADS * SSM_HEAD
    total_rows = sequences * rows
    inv_root = HEAD ** (-0.5)
    offset = lax.axis_index("seq") * rows
    positions = offset + jnp.arange(rows, dtype=jnp.int32)
    local_ids = lax.dynamic_slice_in_dim(segment_ids, offset, rows, 1)
    padded_ids = jnp.concatenate(
        [jnp.full((sequences, taps - 1), -1, jnp.int32), segment_ids], axis=1
    )
    window_ids = lax.dynamic_slice_in_dim(padded_ids, offset, rows + taps - 1, 1)
    prior_id = window_ids[:, taps - 2]
    tap_masks = [
        (window_ids[:, tap : tap + rows] == local_ids).astype(jnp.float32)[:, :, None]
        for tap in range(taps)
    ]
    cosine, sine = rope_tables(positions, HEAD)
    cos_b = cosine[:, None, :]
    sin_b = sine[:, None, :]
    behind = min(lax.axis_size("seq") - 1, (MAX_DOC - 2) // rows + 1) * rows
    key_ids = lax.dynamic_slice_in_dim(
        jnp.concatenate([jnp.full((sequences, behind), -1, jnp.int32), segment_ids], axis=1),
        offset,
        behind + rows,
        1,
    )
    key_order = jnp.arange(behind + rows, dtype=jnp.int32) - behind
    allowed = (key_order[None, None, :] <= jnp.arange(rows, dtype=jnp.int32)[None, :, None]) & (
        key_ids[:, None, :] == local_ids[:, :, None]
    )
    hops = min(lax.axis_size("seq") - 1, (MAX_DOC - 2) // rows + 1)
    spare = -(mamba_dt.shape[1] + 2) % LANES
    shard_in = jnp.concatenate(
        [
            mamba_z,
            mamba_x,
            mamba_bc,
            attn_q,
            attn_kv,
            mamba_dt,
            mixer_norm[:, None],
            ffn_norm[:, None],
            jnp.zeros((mixer_norm.shape[0], spare), jnp.bfloat16),
        ],
        axis=1,
    )
    shard_out = jnp.concatenate([mamba_out, attn_out, ffn_gate, ffn_up, ffn_down], axis=1)
    full_in = lax.all_gather(shard_in, ("dp", "seq"), axis=0, tiled=True)
    full_out = lax.all_gather(shard_out, ("dp", "seq"), axis=0, tiled=True)
    bc_width = mamba_bc.shape[1]
    q_width = attn_q.shape[1]
    kv_width = attn_kv.shape[1]
    hidden_width = ffn_gate.shape[1]
    at_u = inner_width
    at_q = at_u + inner_width + bc_width
    at_kv = at_q + q_width
    at_dt = at_kv + kv_width
    at_gain = at_dt + SSM_HEADS
    mixer_width = inner_width + q_width
    full_mixer = full_out[:, :mixer_width]
    full_gateup = full_out[:, mixer_width : mixer_width + 2 * hidden_width]
    full_down = full_out[:, mixer_width + 2 * hidden_width :]
    gain_one = full_in[:, at_gain].astype(jnp.float32)
    gain_two = full_in[:, at_gain + 1].astype(jnp.float32)
    x_in = block_in.reshape(total_rows, width).astype(jnp.float32)
    normed, factor_one = rms_forward(x_in, gain_one)
    normed_b = normed.astype(jnp.bfloat16)
    projected = matmul(normed_b, full_in)
    gate_z = projected[:, :at_u]
    inner_u = projected[:, at_u:at_q]
    step_raw = projected[:, at_dt:at_gain]
    channels = inner_u.shape[1]
    conv_in = inner_u.reshape(sequences, rows, channels)
    edge_in = passed_along(conv_in[:, rows - taps + 1 :, :], "seq", 1)
    extended = jnp.concatenate([edge_in, conv_in], axis=1)
    conv_pre = jnp.zeros_like(conv_in) + conv_bias
    for tap in range(taps):
        conv_pre = conv_pre + conv_weight[tap] * extended[:, tap : tap + rows] * tap_masks[tap]
    activated = jax.nn.silu(conv_pre)
    xs = activated[:, :, :inner_width].reshape(sequences, rows, SSM_HEADS, SSM_HEAD)
    bmat = activated[:, :, inner_width : inner_width + STATE]
    cmat = activated[:, :, inner_width + STATE :]
    step = jax.nn.softplus(step_raw + dt_bias).reshape(sequences, rows, SSM_HEADS)
    pair, inbound, outbound = block_masks(local_ids, prior_id)
    state_local, carry = block_summary(xs, bmat, step, a_log, inbound, outbound)
    outgoing = state_local
    incoming = jnp.zeros_like(state_local)
    for hop in range(hops):
        incoming = passed_along(outgoing.astype(jnp.bfloat16), "seq", 1).astype(outgoing.dtype)
        outgoing = carry[:, :, None, None] * incoming + state_local
    ssm_out = block_output(xs, bmat, cmat, step, a_log, d_skip, incoming, pair, inbound)
    silu_z = jax.nn.silu(gate_z)
    gated = ssm_out.reshape(total_rows, inner_width) * silu_z
    mixed_norm, factor_m = rms_forward(gated, inner_norm)
    mixed_b = mixed_norm.astype(jnp.bfloat16)
    query = projected[:, at_q:at_kv].reshape(sequences, rows, Q_HEADS, HEAD)
    keyval = projected[:, at_kv:at_dt].reshape(sequences, rows, 2 * KV_HEADS, HEAD)
    query_b = rotate(query, cos_b, sin_b).astype(jnp.bfloat16)
    keys_local = rotate(keyval[:, :, :KV_HEADS], cos_b, sin_b)
    kv_local = jnp.concatenate([keys_local, keyval[:, :, KV_HEADS:]], axis=2).astype(jnp.bfloat16)
    kv_flat = kv_local.reshape(sequences, rows, kv_width)
    kv_all = jnp.concatenate(
        [passed_along(kv_flat, "seq", far) for far in range(hops, 0, -1)] + [kv_flat], axis=1
    )
    window = kv_all.shape[1]
    kv_all = kv_all.reshape(sequences, window, 2 * KV_HEADS, HEAD)
    keys = kv_all[:, :, :KV_HEADS]
    values = kv_all[:, :, KV_HEADS:]
    query_g = query_b.reshape(sequences, rows, KV_HEADS, group, HEAD)

    def attention_scores():
        raw = (
            jnp.einsum("stkgd,slkd->skgtl", query_g, keys, preferred_element_type=jnp.float32)
            * inv_root
        )
        return jnp.where(allowed[:, None, None], raw, -1e30)

    scores = attention_scores()
    top = jnp.max(scores, axis=-1, keepdims=True)
    lse = top + jnp.log(jnp.sum(jnp.exp(scores - top), axis=-1, keepdims=True))
    probs_b = jnp.exp(scores - lse).astype(jnp.bfloat16)
    attended = jnp.einsum("skgtl,slkd->stkgd", probs_b, values, preferred_element_type=jnp.float32)
    attended_b = attended.reshape(total_rows, Q_HEADS * HEAD).astype(jnp.bfloat16)
    mixers_b = jnp.concatenate([mixed_b, attended_b], axis=1)
    mid = x_in + matmul_nt(mixers_b, full_mixer)
    fnormed, factor_two = rms_forward(mid, gain_two)
    fnormed_b = fnormed.astype(jnp.bfloat16)
    gateup_h = matmul(fnormed_b, full_gateup)
    gate_h = gateup_h[:, :hidden_width]
    up_h = gateup_h[:, hidden_width:]
    hidden_b = (jax.nn.silu(gate_h) * up_h).astype(jnp.bfloat16)
    block_out = (
        (mid + matmul_nt(hidden_b, full_down)).astype(jnp.bfloat16).reshape(sequences, rows, width)
    )
    grad_flat = grad_out.reshape(total_rows, width)
    g_down = matmul_tn(grad_flat, hidden_b).astype(jnp.bfloat16)
    d_hidden = matmul(grad_flat, full_down)
    d_gate_b = (d_hidden * up_h * silu_grad(gate_h)).astype(jnp.bfloat16)
    d_up_b = (d_hidden * jax.nn.silu(gate_h)).astype(jnp.bfloat16)
    d_gateup_b = jnp.concatenate([d_gate_b, d_up_b], axis=1)
    g_gateup = matmul_tn(fnormed_b, d_gateup_b).astype(jnp.bfloat16)
    owned_ffn = scattered(jnp.concatenate([g_gateup, g_down], axis=1))
    d_fnorm = matmul_nt(d_gateup_b, full_gateup)
    d_mid_norm, g_fnorm = rms_backward(mid, factor_two, gain_two, d_fnorm)
    d_mid = grad_flat.astype(jnp.float32) + d_mid_norm
    d_mid_b = d_mid.astype(jnp.bfloat16)
    g_mixers = matmul_tn(d_mid_b, mixers_b).astype(jnp.bfloat16)
    d_mixers = matmul(d_mid_b, full_mixer)
    d_mnorm = d_mixers[:, :inner_width]
    d_gated, g_inner = rms_backward(gated, factor_m, inner_norm, d_mnorm)
    d_ssm = (d_gated * silu_z).reshape(sequences, rows, SSM_HEADS, SSM_HEAD)
    d_z = d_gated * ssm_out.reshape(total_rows, inner_width) * silu_grad(gate_z)
    entry = jnp.exp(jnp.cumsum(step * -jnp.exp(a_log), axis=1)) * inbound[:, :, None]
    direct = jnp.einsum("sth,sthp,stn->shpn", entry, d_ssm, cmat, precision=lax.Precision.HIGHEST)
    backlog = direct
    later_grad = jnp.zeros_like(direct)
    for hop in range(hops):
        later_grad = passed_along(backlog.astype(jnp.bfloat16), "seq", -1).astype(backlog.dtype)
        backlog = direct + carry[:, :, None, None] * later_grad
    d_carry = jnp.sum(later_grad * incoming, axis=(2, 3))

    def local_ssm(xs_a, bmat_a, cmat_a, step_a, alog_a, skip_a):
        result = block_output(xs_a, bmat_a, cmat_a, step_a, alog_a, skip_a, incoming, pair, inbound)
        summary, carry_a = block_summary(xs_a, bmat_a, step_a, alog_a, inbound, outbound)
        return (result, summary, carry_a)

    primal, pullback = jax.vjp(local_ssm, xs, bmat, cmat, step, a_log, d_skip)
    d_xs, d_bmat, d_cmat, d_step, g_alog, g_skip = pullback((d_ssm, later_grad, d_carry))
    d_act = jnp.concatenate([d_xs.reshape(sequences, rows, inner_width), d_bmat, d_cmat], axis=2)
    d_pre = d_act * silu_grad(conv_pre)
    g_cbias = jnp.sum(d_pre, axis=(0, 1))
    g_cweight = jnp.stack(
        [
            jnp.sum(d_pre * extended[:, tap : tap + rows] * tap_masks[tap], axis=(0, 1))
            for tap in range(taps)
        ]
    )
    d_padded = jnp.zeros_like(extended)
    for tap in range(taps):
        d_padded = d_padded + jnp.pad(
            d_pre * tap_masks[tap] * conv_weight[tap], ((0, 0), (tap, taps - 1 - tap), (0, 0))
        )
    edge_grad = passed_along(d_padded[:, : taps - 1], "seq", -1)
    d_inner = d_padded[:, taps - 1 :] + jnp.pad(edge_grad, ((0, 0), (rows - taps + 1, 0), (0, 0)))
    d_inner = d_inner.reshape(total_rows, channels)
    d_step_raw = d_step.reshape(total_rows, SSM_HEADS) * jax.nn.sigmoid(step_raw + dt_bias)
    g_dtb = jnp.sum(d_step_raw, axis=0)
    d_att_b = d_mixers[:, inner_width:].astype(jnp.bfloat16)
    d_att_g = d_att_b.reshape(sequences, rows, KV_HEADS, group, HEAD)
    probs = jnp.exp(attention_scores() - lse)
    d_probs = jnp.einsum("stkgd,slkd->skgtl", d_att_g, values, preferred_element_type=jnp.float32)
    d_scores_b = (probs * (d_probs - jnp.sum(probs * d_probs, axis=-1, keepdims=True))).astype(
        jnp.bfloat16
    )
    d_query = (
        jnp.einsum("skgtl,slkd->stkgd", d_scores_b, keys, preferred_element_type=jnp.float32)
        * inv_root
    )
    d_keys = (
        jnp.einsum("skgtl,stkgd->slkd", d_scores_b, query_g, preferred_element_type=jnp.float32)
        * inv_root
    )
    d_values = jnp.einsum("skgtl,stkgd->slkd", probs_b, d_att_g, preferred_element_type=jnp.float32)
    d_kv_all = jnp.concatenate([d_keys, d_values], axis=2).reshape(sequences, window, kv_width)
    d_kv_local = d_kv_all[:, window - rows :]
    for far in range(1, hops + 1):
        start = window - (far + 1) * rows
        term = d_kv_all[:, start : start + rows].astype(jnp.bfloat16)
        d_kv_local = d_kv_local + passed_along(term, "seq", -far).astype(jnp.float32)
    d_kv_local = d_kv_local.reshape(sequences, rows, 2 * KV_HEADS, HEAD)
    d_key_local = rotate_back(d_kv_local[:, :, :KV_HEADS], cos_b, sin_b)
    d_kv_b = (
        jnp.concatenate([d_key_local, d_kv_local[:, :, KV_HEADS:]], axis=2)
        .reshape(total_rows, 2 * KV_HEADS * HEAD)
        .astype(jnp.bfloat16)
    )
    d_q_b = (
        rotate_back(d_query.reshape(sequences, rows, Q_HEADS, HEAD), cos_b, sin_b)
        .reshape(total_rows, Q_HEADS * HEAD)
        .astype(jnp.bfloat16)
    )
    d_z_b = d_z.astype(jnp.bfloat16)
    d_x_b = d_inner[:, :inner_width].astype(jnp.bfloat16)
    d_bc_b = d_inner[:, inner_width:].astype(jnp.bfloat16)
    d_st_b = d_step_raw.astype(jnp.bfloat16)
    d_projected = jnp.concatenate(
        [
            d_z_b,
            d_x_b,
            d_bc_b,
            d_q_b,
            d_kv_b,
            d_st_b,
            jnp.zeros((total_rows, spare + 2), jnp.bfloat16),
        ],
        axis=1,
    )
    g_projected = matmul_tn(normed_b, d_projected).astype(jnp.bfloat16)
    owned_rest = scattered(jnp.concatenate([g_projected, g_mixers], axis=1))
    d_norm = matmul_nt(d_projected, full_in)
    d_in_norm, g_mnorm = rms_backward(x_in, factor_one, gain_one, d_norm)
    grad_in = (d_mid + d_in_norm).astype(jnp.bfloat16).reshape(sequences, rows, width)
    summed = lax.psum(
        (g_cweight, g_cbias, g_dtb, g_alog, g_skip, g_inner, g_mnorm, g_fnorm), ("dp", "seq")
    )
    gain_rows = mixer_norm.shape[0]
    first_row = (lax.axis_index("dp") * lax.axis_size("seq") + lax.axis_index("seq")) * gain_rows
    g_mnorm_own = lax.dynamic_slice_in_dim(summed[6], first_row, gain_rows, 0)
    g_fnorm_own = lax.dynamic_slice_in_dim(summed[7], first_row, gain_rows, 0)
    at_mixers = shard_in.shape[1]
    return (
        block_out,
        grad_in,
        owned_rest[:, :at_u],
        owned_rest[:, at_u : at_u + inner_width],
        owned_rest[:, at_u + inner_width : at_q],
        owned_rest[:, at_dt:at_gain],
        owned_rest[:, at_mixers : at_mixers + inner_width],
        owned_rest[:, at_q:at_kv],
        owned_rest[:, at_kv:at_dt],
        owned_rest[:, at_mixers + inner_width :],
        owned_ffn[:, :hidden_width],
        owned_ffn[:, hidden_width : 2 * hidden_width],
        owned_ffn[:, 2 * hidden_width :],
        g_mnorm_own,
        g_fnorm_own,
        summed[0],
        summed[1],
        summed[2],
        summed[3],
        summed[4],
        summed[5],
    )


def solution(mesh):
    in_specs = (
        P("dp", "seq", None),
        P("dp", None),
        P(("dp", "seq"), None),
        P(("dp", "seq"), None),
        P(("dp", "seq"), None),
        P(("dp", "seq"), None),
        P(("dp", "seq"), None),
        P(("dp", "seq"), None),
        P(("dp", "seq"), None),
        P(("dp", "seq"), None),
        P(("dp", "seq"), None),
        P(("dp", "seq"), None),
        P(("dp", "seq"), None),
        P(("dp", "seq")),
        P(("dp", "seq")),
        P(),
        P(),
        P(),
        P(),
        P(),
        P(),
        P("dp", "seq", None),
    )
    out_specs = (
        P("dp", "seq", None),
        P("dp", "seq", None),
        P(("dp", "seq"), None),
        P(("dp", "seq"), None),
        P(("dp", "seq"), None),
        P(("dp", "seq"), None),
        P(("dp", "seq"), None),
        P(("dp", "seq"), None),
        P(("dp", "seq"), None),
        P(("dp", "seq"), None),
        P(("dp", "seq"), None),
        P(("dp", "seq"), None),
        P(("dp", "seq"), None),
        P(("dp", "seq")),
        P(("dp", "seq")),
        P(),
        P(),
        P(),
        P(),
        P(),
        P(),
    )
    return jax.shard_map(local, mesh=mesh, in_specs=in_specs, out_specs=out_specs, check_vma=False)
```

```python
import functools
import math

import jax
import jax.numpy as jnp
from jax import lax
from jax.experimental import pallas as pl
from jax.experimental.pallas import tpu as pltpu
from jax.sharding import PartitionSpec as P

SSM_HEADS = 24
SSM_HEAD = 64
STATE = 128
Q_HEADS = 8
KV_HEADS = 2
HEAD = 64


EPSILON = 1e-05
ROPE_BASE = 100000000000.0
MAX_DOC = 512
LANES = 128
SSM_PAIRS = SSM_HEADS * SSM_HEAD // LANES


def passed_along(block, axis, distance):
    devices = range(lax.axis_size(axis))
    route = [(i - distance, i) for i in devices if i - distance in devices]
    return lax.ppermute(block, axis, route)


def scattered_dp(grad):
    return lax.psum_scatter(grad, "dp", scatter_dimension=0, tiled=True)


def scattered_seq(part):
    return lax.psum_scatter(part, "seq", scatter_dimension=0, tiled=True).astype(jnp.float32)


def silu_grad(value):
    sigma = jax.nn.sigmoid(value)
    return sigma * (1.0 + value * (1.0 - sigma))


def rms_forward(value, gain):
    factor = lax.rsqrt(jnp.mean(value * value, axis=-1, keepdims=True) + EPSILON)
    return (value * factor * gain, factor)


def rms_backward(value, factor, gain, upstream):
    weighted = upstream * gain
    gain_grad = jnp.sum(upstream * value * factor, axis=0)
    inward = factor * weighted - value * factor * factor * factor * jnp.mean(
        weighted * value, axis=-1, keepdims=True
    )
    return (inward, gain_grad)


def matmul(left, right):
    return jnp.dot(left, right, preferred_element_type=jnp.float32)


def matmul_nt(left, right):
    return lax.dot_general(
        left, right, (((1,), (1,)), ((), ())), preferred_element_type=jnp.float32
    )


def matmul_tn(left, right):
    return lax.dot_general(
        left, right, (((0,), (0,)), ((), ())), preferred_element_type=jnp.float32
    )


def rope_tables(positions, head_size):
    half = head_size // 2
    freq_scale = ROPE_BASE ** (-jnp.arange(half, dtype=jnp.float32) / half)
    angles = positions.astype(jnp.float32)[:, None] * freq_scale[None, :]
    return (jnp.cos(angles), jnp.sin(angles))


def rotate(value, cosine, sine):
    half = value.shape[-1] // 2
    first = value[..., :half]
    second = value[..., half:]
    return jnp.concatenate(
        [first * cosine - second * sine, second * cosine + first * sine], axis=-1
    )


def rotate_back(grad, cosine, sine):
    half = grad.shape[-1] // 2
    first = grad[..., :half]
    second = grad[..., half:]
    return jnp.concatenate(
        [first * cosine + second * sine, second * cosine - first * sine], axis=-1
    )


def half_lanes(cols, first, shape):
    lane = lax.broadcasted_iota(jnp.int32, shape, 1)
    return jnp.where(lane < SSM_HEAD, cols[:, first : first + 1], cols[:, first + 1 : first + 2])


def dot_nn(left, right):
    return lax.dot_general(
        left, right, (((1,), (0,)), ((), ())), preferred_element_type=jnp.float32
    )


def ssm_local_kernel(xs_ref, b_ref, c_ref, cols_ref, rows_ref, bias_ref, out_ref, state_ref, cb_ref):
    bmat = b_ref[...]

    @pl.when(pl.program_id(0) == 0)
    def _():
        cb_ref[...] = lax.dot_general(
            c_ref[...],
            bmat,
            (((1,), (1,)), ((), ())),
            precision=lax.Precision.HIGHEST,
            preferred_element_type=jnp.float32,
        )

    xs = xs_ref[...]
    cols = cols_ref[0]
    rows = rows_ref[0]
    scaled = xs * half_lanes(cols, 2, xs.shape)
    scaled_b = scaled.astype(jnp.bfloat16)
    parts = []
    for k in range(2):
        kernel = jnp.exp(cols[:, k : k + 1] - rows[k : k + 1, :] + bias_ref[...])
        parts.append(dot_nn((kernel * cb_ref[...]).astype(jnp.bfloat16), scaled_b))
    lane = lax.broadcasted_iota(jnp.int32, xs.shape, 1)
    out_ref[...] = jnp.where(lane < SSM_HEAD, parts[0], parts[1])
    tailed = (scaled * half_lanes(cols, 6, xs.shape)).astype(jnp.bfloat16)
    state_ref[0] = lax.dot_general(
        tailed,
        bmat.astype(jnp.bfloat16),
        (((0,), (0,)), ((), ())),
        preferred_element_type=jnp.float32,
    )


def ssm_carry_kernel(local_ref, xs_ref, c_ref, cols_ref, state_ref, skip_ref, z_ref, out_ref, gated_ref):
    xs = xs_ref[...]
    carried = lax.dot_general(
        c_ref[...].astype(jnp.bfloat16),
        state_ref[0],
        (((1,), (1,)), ((), ())),
        preferred_element_type=jnp.float32,
    )
    entry = half_lanes(cols_ref[0], 4, xs.shape)
    out = local_ref[...] + entry * carried + skip_ref[...] * xs
    out_ref[...] = out
    gate = z_ref[...]
    gated_ref[...] = out * (gate * jax.nn.sigmoid(gate))


def ssm_direct_kernel(g_ref, c_ref, cols_ref, direct_ref):
    g = g_ref[...]
    entered = (g * half_lanes(cols_ref[0], 4, g.shape)).astype(jnp.bfloat16)
    direct_ref[0] = lax.dot_general(
        entered,
        c_ref[...].astype(jnp.bfloat16),
        (((0,), (0,)), ((), ())),
        preferred_element_type=jnp.float32,
    )


def ssm_backward_kernel(
    g_ref,
    xs_ref,
    out_ref,
    b_ref,
    c_ref,
    cols_ref,
    rows_ref,
    bias_ref,
    state_ref,
    later_ref,
    skip_ref,
    dxs_ref,
    db_ref,
    dc_ref,
    dcols_ref,
    drows_ref,
    cb_ref,
    dcb_ref,
):
    pair = pl.program_id(0)
    bmat = b_ref[...]
    cmat = c_ref[...]
    b_low = bmat.astype(jnp.bfloat16)
    c_low = cmat.astype(jnp.bfloat16)

    @pl.when(pair == 0)
    def _():
        cb_ref[...] = lax.dot_general(
            bmat,
            cmat,
            (((1,), (1,)), ((), ())),
            precision=lax.Precision.HIGHEST,
            preferred_element_type=jnp.float32,
        )
        dcb_ref[...] = jnp.zeros_like(dcb_ref)
        db_ref[...] = jnp.zeros_like(db_ref)
        dc_ref[...] = jnp.zeros_like(dc_ref)

    g = g_ref[...]
    xs = xs_ref[...]
    skip = skip_ref[...]
    cols = cols_ref[0]
    rows = rows_ref[0]
    step = half_lanes(cols, 2, xs.shape)
    tail = half_lanes(cols, 6, xs.shape)
    lane = lax.broadcasted_iota(jnp.int32, xs.shape, 1)
    first = lane < SSM_HEAD
    g_low = g.astype(jnp.bfloat16)
    scaled = xs * step
    parts = []
    total = dcb_ref[...]
    for k in range(2):
        mine = first if k == 0 else jnp.logical_not(first)
        kernel = jnp.exp(rows[k : k + 1, :] - cols[:, k : k + 1] + bias_ref[...])
        parts.append(dot_nn((kernel * cb_ref[...]).astype(jnp.bfloat16), g_low))
        crossed = lax.dot_general(
            jnp.where(mine, scaled, 0.0).astype(jnp.bfloat16),
            g_low,
            (((1,), (1,)), ((), ())),
            preferred_element_type=jnp.float32,
        )
        total = total + crossed * kernel
    dcb_ref[...] = total
    later = later_ref[0]
    swept = tail * lax.dot_general(
        b_low, later, (((1,), (1,)), ((), ())), preferred_element_type=jnp.float32
    )
    inner = jnp.where(first, parts[0], parts[1]) + swept
    dxs_ref[...] = step * inner + skip * g
    db_ref[...] += dot_nn((scaled * tail).astype(jnp.bfloat16), later)
    entered = (g * half_lanes(cols, 4, g.shape)).astype(jnp.bfloat16)
    dc_ref[...] += dot_nn(entered, state_ref[0])
    rose = g_low.astype(jnp.float32) * (out_ref[...] - skip * xs)
    stepped = xs * inner
    kept = scaled.astype(jnp.bfloat16).astype(jnp.float32)
    fell = kept * (inner - swept) + scaled * swept
    columns = [
        jnp.sum(jnp.where(first, value, 0.0), axis=1, keepdims=True)
        if k == 0
        else jnp.sum(jnp.where(first, 0.0, value), axis=1, keepdims=True)
        for value in (rose, stepped, fell)
        for k in range(2)
    ]
    spot = lax.broadcasted_iota(jnp.int32, cols.shape, 1)
    packed = jnp.zeros_like(cols)
    for index, column in enumerate(columns):
        packed = jnp.where(spot == index, column, packed)
    dcols_ref[0] = packed
    drows_ref[0, 0:1, :] = jnp.sum(scaled * swept, axis=0, keepdims=True)
    drows_ref[0, 1:2, :] = jnp.sum(g * xs, axis=0, keepdims=True)

    @pl.when(pair == pl.num_programs(0) - 1)
    def _():
        low = dcb_ref[...].astype(jnp.bfloat16)
        db_ref[...] += dot_nn(low, c_low)
        dc_ref[...] += lax.dot_general(
            low, b_low, (((0,), (0,)), ((), ())), preferred_element_type=jnp.float32
        )


def ssm_specs(count):
    rows = count
    block = pl.BlockSpec((rows, LANES), lambda p: (0, p))
    bmat = pl.BlockSpec((rows, LANES), lambda p: (0, SSM_PAIRS))
    cmat = pl.BlockSpec((rows, LANES), lambda p: (0, SSM_PAIRS + 1))
    cols = pl.BlockSpec((1, rows, 8), lambda p: (p, 0, 0))
    turned = pl.BlockSpec((1, 2, rows), lambda p: (p, 0, 0))
    bias = pl.BlockSpec((rows, rows), lambda p: (0, 0))
    state = pl.BlockSpec((1, LANES, STATE), lambda p: (p, 0, 0))
    skip = pl.BlockSpec((1, LANES), lambda p: (0, p))
    whole = pl.BlockSpec((rows, LANES), lambda p: (0, 0))
    return block, bmat, cmat, cols, turned, bias, state, skip, whole


def ssm_local(act, cols, turned, bias):
    rows = act.shape[0]
    block, bmat, cmat, col, turn, square, state, skip, whole = ssm_specs(rows)
    return pl.pallas_call(
        ssm_local_kernel,
        grid=(SSM_PAIRS,),
        in_specs=[block, bmat, cmat, col, turn, square],
        out_specs=[block, state],
        out_shape=[
            jax.ShapeDtypeStruct((rows, SSM_PAIRS * LANES), jnp.float32),
            jax.ShapeDtypeStruct((SSM_PAIRS, LANES, STATE), jnp.float32),
        ],
        scratch_shapes=[pltpu.VMEM((rows, rows), jnp.float32)],
        name="ssm_local",
        cost_estimate=pl.CostEstimate(flops=10**9, transcendentals=24 * rows * rows, bytes_accessed=6 * 10**6),
    )(act, act, act, cols, turned, bias)


def ssm_carried(local_part, act, cols, state, skip_row, projected):
    rows = act.shape[0]
    block, bmat, cmat, col, turn, square, states, skip, whole = ssm_specs(rows)
    shape = jax.ShapeDtypeStruct((rows, SSM_PAIRS * LANES), jnp.float32)
    return pl.pallas_call(
        ssm_carry_kernel,
        grid=(SSM_PAIRS,),
        in_specs=[block, block, cmat, col, states, skip, block],
        out_specs=[block, block],
        out_shape=[shape, shape],
        name="ssm_carried",
        cost_estimate=pl.CostEstimate(flops=10**8, transcendentals=rows * 1536, bytes_accessed=9 * 10**6),
    )(local_part, act, act, cols, state, skip_row, projected)


def ssm_direct(g, act, cols):
    rows = act.shape[0]
    block, bmat, cmat, col, turn, square, states, skip, whole = ssm_specs(rows)
    return pl.pallas_call(
        ssm_direct_kernel,
        grid=(SSM_PAIRS,),
        in_specs=[block, cmat, col],
        out_specs=states,
        out_shape=jax.ShapeDtypeStruct((SSM_PAIRS, LANES, STATE), jnp.float32),
        name="ssm_direct",
        cost_estimate=pl.CostEstimate(flops=10**8, transcendentals=0, bytes_accessed=4 * 10**6),
    )(g, act, cols)


def ssm_backward(g, act, out, cols, turned, bias_turned, state, later, skip_row):
    rows = act.shape[0]
    block, bmat, cmat, col, turn, square, states, skip, whole = ssm_specs(rows)
    return pl.pallas_call(
        ssm_backward_kernel,
        grid=(SSM_PAIRS,),
        in_specs=[block, block, block, bmat, cmat, col, turn, square, states, states, skip],
        out_specs=[block, whole, whole, col, pl.BlockSpec((1, 2, LANES), lambda p: (p, 0, 0))],
        out_shape=[
            jax.ShapeDtypeStruct((rows, SSM_PAIRS * LANES), jnp.float32),
            jax.ShapeDtypeStruct((rows, STATE), jnp.float32),
            jax.ShapeDtypeStruct((rows, STATE), jnp.float32),
            jax.ShapeDtypeStruct((SSM_PAIRS, rows, 8), jnp.float32),
            jax.ShapeDtypeStruct((SSM_PAIRS, 2, LANES), jnp.float32),
        ],
        scratch_shapes=[pltpu.VMEM((rows, rows), jnp.float32)] * 2,
        name="ssm_backward",
        cost_estimate=pl.CostEstimate(flops=2 * 10**9, transcendentals=24 * rows * rows, bytes_accessed=12 * 10**6),
    )(g, act, out, act, act, cols, turned, bias_turned, state, later, skip_row)


def outer_kernel(split, left_a_ref, right_a_ref, left_b_ref, right_b_ref, out_ref, turned_ref):
    step = pl.program_id(0)

    @pl.when(step == 0)
    def _():
        turned_ref[...] = left_a_ref[...].T

    @pl.when(step == split)
    def _():
        turned_ref[...] = left_b_ref[...].T

    @pl.when(step < split)
    def _():
        out_ref[...] = dot_nn(turned_ref[...], right_a_ref[...]).astype(jnp.bfloat16)

    @pl.when(step >= split)
    def _():
        out_ref[...] = dot_nn(turned_ref[...], right_b_ref[...]).astype(jnp.bfloat16)


def outer_pair(left_a, right_a, left_b, right_b):
    rows, width = left_a.shape
    wide_a = right_a.shape[1]
    wide_b = right_b.shape[1]
    wide = math.gcd(math.gcd(wide_a, wide_b), 512)
    split = wide_a // wide
    total = split + wide_b // wide
    held = pl.BlockSpec((rows, width), lambda j: (0, 0))
    return pl.pallas_call(
        functools.partial(outer_kernel, split),
        grid=(total,),
        in_specs=[
            held,
            pl.BlockSpec((rows, wide), lambda j: (0, jnp.minimum(j, split - 1))),
            held,
            pl.BlockSpec((rows, wide), lambda j: (0, jnp.maximum(j - split, 0))),
        ],
        out_specs=pl.BlockSpec((width, wide), lambda j: (0, j)),
        out_shape=jax.ShapeDtypeStruct((width, wide_a + wide_b), jnp.bfloat16),
        scratch_shapes=[pltpu.VMEM((width, rows), jnp.bfloat16)],
        name="outer_pair",
        cost_estimate=pl.CostEstimate(
            flops=2 * rows * width * (wide_a + wide_b),
            transcendentals=0,
            bytes_accessed=2 * width * (wide_a + wide_b),
        ),
    )(left_a, right_a, left_b, right_b)


def local(
    block_in,
    segment_ids,
    mamba_z,
    mamba_x,
    mamba_bc,
    mamba_dt,
    mamba_out,
    attn_q,
    attn_kv,
    attn_out,
    ffn_gate,
    ffn_up,
    ffn_down,
    mixer_norm,
    ffn_norm,
    conv_weight,
    conv_bias,
    dt_bias,
    a_log,
    d_skip,
    inner_norm,
    grad_out,
):
    sequences, rows, width = block_in.shape
    length = segment_ids.shape[1]
    taps = conv_weight.shape[0]
    group = Q_HEADS // KV_HEADS
    inner_width = SSM_HEADS * SSM_HEAD
    total_rows = sequences * rows
    inv_root = HEAD ** (-0.5)
    offset = lax.axis_index("seq") * rows
    positions = offset + jnp.arange(rows, dtype=jnp.int32)
    local_ids = lax.dynamic_slice_in_dim(segment_ids, offset, rows, 1)
    padded_ids = jnp.concatenate(
        [jnp.full((sequences, taps - 1), -1, jnp.int32), segment_ids], axis=1
    )
    window_ids = lax.dynamic_slice_in_dim(padded_ids, offset, rows + taps - 1, 1)
    prior_id = window_ids[:, taps - 2]
    tap_masks = [
        (window_ids[:, tap : tap + rows] == local_ids).astype(jnp.float32)[:, :, None]
        for tap in range(taps)
    ]
    cosine, sine = rope_tables(positions, HEAD)
    cos_b = cosine[:, None, :]
    sin_b = sine[:, None, :]
    behind = min(lax.axis_size("seq") - 1, (MAX_DOC - 2) // rows + 1) * rows
    key_ids = lax.dynamic_slice_in_dim(
        jnp.concatenate([jnp.full((sequences, behind), -1, jnp.int32), segment_ids], axis=1),
        offset,
        behind + rows,
        1,
    )
    key_order = jnp.arange(behind + rows, dtype=jnp.int32) - behind
    allowed = (key_order[None, None, :] <= jnp.arange(rows, dtype=jnp.int32)[None, :, None]) & (
        key_ids[:, None, :] == local_ids[:, :, None]
    )
    hops = min(lax.axis_size("seq") - 1, (MAX_DOC - 2) // rows + 1)
    spare = -(mamba_dt.shape[1] + 2) % (2 * LANES)
    shard_in = jnp.concatenate(
        [
            mamba_z,
            mamba_x,
            mamba_bc,
            attn_q,
            attn_kv,
            mamba_dt,
            mixer_norm[:, None],
            ffn_norm[:, None],
            jnp.zeros((mixer_norm.shape[0], spare), jnp.bfloat16),
        ],
        axis=1,
    )
    shard_out = jnp.concatenate([mamba_out, attn_out, ffn_gate, ffn_up, ffn_down], axis=1)
    full_in = lax.all_gather(shard_in, ("dp", "seq"), axis=0, tiled=True)
    full_out = lax.all_gather(shard_out, ("dp", "seq"), axis=0, tiled=True)
    bc_width = mamba_bc.shape[1]
    q_width = attn_q.shape[1]
    kv_width = attn_kv.shape[1]
    hidden_width = ffn_gate.shape[1]
    at_u = inner_width
    at_q = at_u + inner_width + bc_width
    at_kv = at_q + q_width
    at_dt = at_kv + kv_width
    at_gain = at_dt + SSM_HEADS
    mixer_width = inner_width + q_width
    full_mixer = full_out[:, :mixer_width]
    full_gateup = full_out[:, mixer_width : mixer_width + 2 * hidden_width]
    full_down = full_out[:, mixer_width + 2 * hidden_width :]
    gain_one = full_in[:, at_gain].astype(jnp.float32)
    gain_two = full_in[:, at_gain + 1].astype(jnp.float32)
    x_in = block_in.reshape(total_rows, width).astype(jnp.float32)
    normed, factor_one = rms_forward(x_in, gain_one)
    normed_b = normed.astype(jnp.bfloat16)
    projected = matmul(normed_b, full_in)
    gate_z = projected[:, :at_u]
    inner_u = projected[:, at_u:at_q]
    step_raw = projected[:, at_dt:at_gain]
    channels = inner_u.shape[1]
    conv_in = inner_u.reshape(sequences, rows, channels)
    edge_in = passed_along(conv_in[:, rows - taps + 1 :, :], "seq", 1)
    extended = jnp.concatenate([edge_in, conv_in], axis=1)
    conv_pre = jnp.zeros_like(conv_in) + conv_bias
    for tap in range(taps):
        conv_pre = conv_pre + conv_weight[tap] * extended[:, tap : tap + rows] * tap_masks[tap]
    activated = jax.nn.silu(conv_pre)
    act = activated.reshape(total_rows, channels)
    step = jax.nn.softplus(step_raw + dt_bias)
    ids = local_ids.reshape(total_rows)
    order = jnp.arange(rows)
    pair = (order[:, None] >= order[None, :]) & (ids[:, None] == ids[None, :])
    bias = jnp.where(pair, 0.0, -1e30).astype(jnp.float32)
    bias_turned = jnp.where(
        (order[:, None] <= order[None, :]) & (ids[:, None] == ids[None, :]), 0.0, -1e30
    ).astype(jnp.float32)
    inbound = (ids == prior_id[0]).astype(jnp.float32)[:, None]
    outbound = (ids == ids[-1]).astype(jnp.float32)[:, None]
    rate = -jnp.exp(a_log)
    ladder = (order[:, None] >= order[None, :]).astype(jnp.float32)
    decay = jnp.dot(ladder, step * rate, precision=lax.Precision.HIGHEST)
    entry = jnp.exp(decay) * inbound
    tail = jnp.exp(decay[-1:] - decay) * outbound
    carry = jnp.exp(decay[-1]) * inbound[-1, 0]
    cols = jnp.stack([decay, step, entry, tail], axis=1)
    cols = cols.reshape(rows, 4, SSM_PAIRS, 2).transpose(2, 0, 1, 3).reshape(SSM_PAIRS, rows, 8)
    turned = decay.T.reshape(SSM_PAIRS, 2, rows)
    skip_row = jnp.repeat(d_skip, SSM_HEAD)[None, :]
    carry_rows = jnp.repeat(carry, SSM_HEAD).reshape(SSM_PAIRS, LANES, 1)
    local_part, state_local = ssm_local(act, cols, turned, bias)
    outgoing = state_local
    for hop in range(hops):
        incoming = passed_along(outgoing.astype(jnp.bfloat16), "seq", 1)
        outgoing = carry_rows * incoming.astype(jnp.float32) + state_local
    ssm_out, gated = ssm_carried(local_part, act, cols, incoming, skip_row, projected)
    silu_z = jax.nn.silu(gate_z)
    mixed_norm, factor_m = rms_forward(gated, inner_norm)
    mixed_b = mixed_norm.astype(jnp.bfloat16)
    query = projected[:, at_q:at_kv].reshape(sequences, rows, Q_HEADS, HEAD)
    keyval = projected[:, at_kv:at_dt].reshape(sequences, rows, 2 * KV_HEADS, HEAD)
    query_b = rotate(query, cos_b, sin_b).astype(jnp.bfloat16)
    keys_local = rotate(keyval[:, :, :KV_HEADS], cos_b, sin_b)
    kv_local = jnp.concatenate([keys_local, keyval[:, :, KV_HEADS:]], axis=2).astype(jnp.bfloat16)
    kv_flat = kv_local.reshape(sequences, rows, kv_width)
    kv_all = jnp.concatenate(
        [passed_along(kv_flat, "seq", far) for far in range(hops, 0, -1)] + [kv_flat], axis=1
    )
    window = kv_all.shape[1]
    kv_all = kv_all.reshape(sequences, window, 2 * KV_HEADS, HEAD)
    keys = kv_all[:, :, :KV_HEADS]
    values = kv_all[:, :, KV_HEADS:]
    query_g = query_b.reshape(sequences, rows, KV_HEADS, group, HEAD)

    def attention_scores():
        raw = (
            jnp.einsum("stkgd,slkd->skgtl", query_g, keys, preferred_element_type=jnp.float32)
            * inv_root
        )
        return jnp.where(allowed[:, None, None], raw, -1e30)

    scores = attention_scores()
    top = jnp.max(scores, axis=-1, keepdims=True)
    lse = top + jnp.log(jnp.sum(jnp.exp(scores - top), axis=-1, keepdims=True))
    probs_b = jnp.exp(scores - lse).astype(jnp.bfloat16)
    attended = jnp.einsum("skgtl,slkd->stkgd", probs_b, values, preferred_element_type=jnp.float32)
    attended_b = attended.reshape(total_rows, Q_HEADS * HEAD).astype(jnp.bfloat16)
    mixers_b = jnp.concatenate([mixed_b, attended_b], axis=1)
    mid = x_in + matmul_nt(mixers_b, full_mixer)
    fnormed, factor_two = rms_forward(mid, gain_two)
    fnormed_b = fnormed.astype(jnp.bfloat16)
    gateup_h = matmul(fnormed_b, full_gateup)
    gate_h = gateup_h[:, :hidden_width]
    up_h = gateup_h[:, hidden_width:]
    hidden_b = (jax.nn.silu(gate_h) * up_h).astype(jnp.bfloat16)
    block_out = (
        (mid + matmul_nt(hidden_b, full_down)).astype(jnp.bfloat16).reshape(sequences, rows, width)
    )
    grad_flat = grad_out.reshape(total_rows, width)
    d_hidden = matmul(grad_flat, full_down)
    d_gate_b = (d_hidden * up_h * silu_grad(gate_h)).astype(jnp.bfloat16)
    d_up_b = (d_hidden * jax.nn.silu(gate_h)).astype(jnp.bfloat16)
    d_gateup_b = jnp.concatenate([d_gate_b, d_up_b], axis=1)
    part_ffn = scattered_dp(outer_pair(fnormed_b, d_gateup_b, grad_flat, hidden_b))
    d_fnorm = matmul_nt(d_gateup_b, full_gateup)
    d_mid_norm, g_fnorm = rms_backward(mid, factor_two, gain_two, d_fnorm)
    d_mid = grad_flat.astype(jnp.float32) + d_mid_norm
    d_mid_b = d_mid.astype(jnp.bfloat16)
    d_mixers = matmul(d_mid_b, full_mixer)
    d_mnorm = d_mixers[:, :inner_width]
    d_gated, g_inner = rms_backward(gated, factor_m, inner_norm, d_mnorm)
    d_ssm = d_gated * silu_z
    d_z = d_gated * ssm_out * silu_grad(gate_z)
    direct = ssm_direct(d_ssm, act, cols)
    backlog = direct
    for hop in range(hops):
        later_grad = passed_along(backlog.astype(jnp.bfloat16), "seq", -1)
        backlog = direct + carry_rows * later_grad.astype(jnp.float32)
    d_carry = jnp.sum(
        (later_grad.astype(jnp.float32) * incoming.astype(jnp.float32)).reshape(
            SSM_HEADS, SSM_HEAD, STATE
        ),
        axis=(1, 2),
    )
    d_xs, d_bmat, d_cmat, d_cols, d_rows = ssm_backward(
        d_ssm, act, ssm_out, cols, turned, bias_turned, incoming, later_grad, skip_row
    )
    d_pairs = d_cols[:, :, :6].reshape(SSM_PAIRS, rows, 3, 2).transpose(2, 1, 0, 3)
    d_pairs = d_pairs.reshape(3, rows, SSM_HEADS)
    d_sums = jnp.sum(d_rows.reshape(SSM_PAIRS, 2, 2, SSM_HEAD), axis=3).transpose(1, 0, 2)
    d_sums = d_sums.reshape(2, SSM_HEADS)
    g_skip = d_sums[1]
    d_decay = d_pairs[0] - d_pairs[2]
    d_rise = jnp.dot(ladder.T, d_decay, precision=lax.Precision.HIGHEST)
    d_rise = d_rise + (d_sums[0] + d_carry * carry)
    d_step = d_pairs[1] + d_rise * rate
    g_alog = jnp.sum(d_rise * step, axis=0) * rate
    d_act = jnp.concatenate([d_xs, d_bmat, d_cmat], axis=1).reshape(sequences, rows, channels)
    d_act, part_ffn = lax.optimization_barrier((d_act, part_ffn))
    owned_ffn = scattered_seq(part_ffn)
    d_pre = d_act * silu_grad(conv_pre)
    g_cbias = jnp.sum(d_pre, axis=(0, 1))
    g_cweight = jnp.stack(
        [
            jnp.sum(d_pre * extended[:, tap : tap + rows] * tap_masks[tap], axis=(0, 1))
            for tap in range(taps)
        ]
    )
    d_padded = jnp.zeros_like(extended)
    for tap in range(taps):
        d_padded = d_padded + jnp.pad(
            d_pre * tap_masks[tap] * conv_weight[tap], ((0, 0), (tap, taps - 1 - tap), (0, 0))
        )
    edge_grad = passed_along(d_padded[:, : taps - 1], "seq", -1)
    d_inner = d_padded[:, taps - 1 :] + jnp.pad(edge_grad, ((0, 0), (rows - taps + 1, 0), (0, 0)))
    d_inner = d_inner.reshape(total_rows, channels)
    d_step_raw = d_step.reshape(total_rows, SSM_HEADS) * jax.nn.sigmoid(step_raw + dt_bias)
    g_dtb = jnp.sum(d_step_raw, axis=0)
    d_att_b = d_mixers[:, inner_width:].astype(jnp.bfloat16)
    d_att_g = d_att_b.reshape(sequences, rows, KV_HEADS, group, HEAD)
    probs = jnp.exp(attention_scores() - lse)
    d_probs = jnp.einsum("stkgd,slkd->skgtl", d_att_g, values, preferred_element_type=jnp.float32)
    d_scores_b = (probs * (d_probs - jnp.sum(probs * d_probs, axis=-1, keepdims=True))).astype(
        jnp.bfloat16
    )
    d_query = (
        jnp.einsum("skgtl,slkd->stkgd", d_scores_b, keys, preferred_element_type=jnp.float32)
        * inv_root
    )
    d_keys = (
        jnp.einsum("skgtl,stkgd->slkd", d_scores_b, query_g, preferred_element_type=jnp.float32)
        * inv_root
    )
    d_values = jnp.einsum("skgtl,stkgd->slkd", probs_b, d_att_g, preferred_element_type=jnp.float32)
    d_kv_all = jnp.concatenate([d_keys, d_values], axis=2).reshape(sequences, window, kv_width)
    d_kv_local = d_kv_all[:, window - rows :]
    for far in range(1, hops + 1):
        start = window - (far + 1) * rows
        term = d_kv_all[:, start : start + rows].astype(jnp.bfloat16)
        d_kv_local = d_kv_local + passed_along(term, "seq", -far).astype(jnp.float32)
    d_kv_local = d_kv_local.reshape(sequences, rows, 2 * KV_HEADS, HEAD)
    d_key_local = rotate_back(d_kv_local[:, :, :KV_HEADS], cos_b, sin_b)
    d_kv_b = (
        jnp.concatenate([d_key_local, d_kv_local[:, :, KV_HEADS:]], axis=2)
        .reshape(total_rows, 2 * KV_HEADS * HEAD)
        .astype(jnp.bfloat16)
    )
    d_q_b = (
        rotate_back(d_query.reshape(sequences, rows, Q_HEADS, HEAD), cos_b, sin_b)
        .reshape(total_rows, Q_HEADS * HEAD)
        .astype(jnp.bfloat16)
    )
    d_z_b = d_z.astype(jnp.bfloat16)
    d_x_b = d_inner[:, :inner_width].astype(jnp.bfloat16)
    d_bc_b = d_inner[:, inner_width:].astype(jnp.bfloat16)
    d_st_b = d_step_raw.astype(jnp.bfloat16)
    d_projected = jnp.concatenate(
        [
            d_z_b,
            d_x_b,
            d_bc_b,
            d_q_b,
            d_kv_b,
            d_st_b,
            jnp.zeros((total_rows, spare + 2), jnp.bfloat16),
        ],
        axis=1,
    )
    g_rest = outer_pair(normed_b, d_projected, d_mid_b, mixers_b)
    g_rest, owned_ffn = lax.optimization_barrier((g_rest, owned_ffn))
    owned_rest = scattered_seq(scattered_dp(g_rest))
    d_norm = matmul_nt(d_projected, full_in)
    d_in_norm, g_mnorm = rms_backward(x_in, factor_one, gain_one, d_norm)
    grad_in = (d_mid + d_in_norm).astype(jnp.bfloat16).reshape(sequences, rows, width)
    summed = lax.psum(
        (g_cweight, g_cbias, g_dtb, g_alog, g_skip, g_inner, g_mnorm, g_fnorm), ("dp", "seq")
    )
    gain_rows = mixer_norm.shape[0]
    first_row = (lax.axis_index("dp") * lax.axis_size("seq") + lax.axis_index("seq")) * gain_rows
    g_mnorm_own = lax.dynamic_slice_in_dim(summed[6], first_row, gain_rows, 0)
    g_fnorm_own = lax.dynamic_slice_in_dim(summed[7], first_row, gain_rows, 0)
    at_mixers = shard_in.shape[1]
    return (
        block_out,
        grad_in,
        owned_rest[:, :at_u],
        owned_rest[:, at_u : at_u + inner_width],
        owned_rest[:, at_u + inner_width : at_q],
        owned_rest[:, at_dt:at_gain],
        owned_rest[:, at_mixers : at_mixers + inner_width],
        owned_rest[:, at_q:at_kv],
        owned_rest[:, at_kv:at_dt],
        owned_rest[:, at_mixers + inner_width :],
        owned_ffn[:, :hidden_width],
        owned_ffn[:, hidden_width : 2 * hidden_width],
        owned_ffn[:, 2 * hidden_width :],
        g_mnorm_own,
        g_fnorm_own,
        summed[0],
        summed[1],
        summed[2],
        summed[3],
        summed[4],
        summed[5],
    )


def solution(mesh):
    in_specs = (
        P("dp", "seq", None),
        P("dp", None),
        P(("dp", "seq"), None),
        P(("dp", "seq"), None),
        P(("dp", "seq"), None),
        P(("dp", "seq"), None),
        P(("dp", "seq"), None),
        P(("dp", "seq"), None),
        P(("dp", "seq"), None),
        P(("dp", "seq"), None),
        P(("dp", "seq"), None),
        P(("dp", "seq"), None),
        P(("dp", "seq"), None),
        P(("dp", "seq")),
        P(("dp", "seq")),
        P(),
        P(),
        P(),
        P(),
        P(),
        P(),
        P("dp", "seq", None),
    )
    out_specs = (
        P("dp", "seq", None),
        P("dp", "seq", None),
        P(("dp", "seq"), None),
        P(("dp", "seq"), None),
        P(("dp", "seq"), None),
        P(("dp", "seq"), None),
        P(("dp", "seq"), None),
        P(("dp", "seq"), None),
        P(("dp", "seq"), None),
        P(("dp", "seq"), None),
        P(("dp", "seq"), None),
        P(("dp", "seq"), None),
        P(("dp", "seq"), None),
        P(("dp", "seq")),
        P(("dp", "seq")),
        P(),
        P(),
        P(),
        P(),
        P(),
        P(),
    )
    return jax.shard_map(local, mesh=mesh, in_specs=in_specs, out_specs=out_specs, check_vma=False)
```

```python
import functools
import math

import jax
import jax.numpy as jnp
from jax import lax
from jax.experimental import pallas as pl
from jax.experimental.pallas import tpu as pltpu
from jax.sharding import PartitionSpec as P

SSM_HEADS = 24
SSM_HEAD = 64
STATE = 128
Q_HEADS = 8
KV_HEADS = 2
HEAD = 64


EPSILON = 1e-05
ROPE_BASE = 100000000000.0
MAX_DOC = 512
LANES = 128
SSM_PAIRS = SSM_HEADS * SSM_HEAD // LANES
PAIR_GROUP = 4


def passed_along(block, axis, distance):
    devices = range(lax.axis_size(axis))
    route = [(i - distance, i) for i in devices if i - distance in devices]
    return lax.ppermute(block, axis, route)


def scattered_dp(grad):
    return lax.psum_scatter(grad, "dp", scatter_dimension=0, tiled=True)


def scattered_seq(part):
    return lax.psum_scatter(part, "seq", scatter_dimension=0, tiled=True).astype(jnp.float32)


def gathered_seq(shard):
    index = lax.axis_index("seq")
    count = lax.axis_size("seq")
    held = shard
    bit = 1
    while bit < count:
        got = lax.ppermute(held, "seq", [(i, i ^ bit) for i in range(count)])
        odd = (index // bit) % 2 == 1
        held = jnp.concatenate([jnp.where(odd, got, held), jnp.where(odd, held, got)], axis=0)
        bit *= 2
    return held


def hopped_seq(part, rider):
    index = lax.axis_index("seq")
    count = lax.axis_size("seq")
    held = part.reshape(count, part.shape[0] // count, part.shape[1])
    bit = 1
    while bit < count:
        halves = held.reshape(held.shape[0] // 2, 2, *held.shape[1:])
        odd = (index // bit) % 2 == 1
        mine = jnp.where(odd, halves[:, 1], halves[:, 0])
        other = jnp.where(odd, halves[:, 0], halves[:, 1])
        got = lax.ppermute(other, "seq", [(i, i ^ bit) for i in range(count)])
        held = mine.astype(jnp.float32) + got.astype(jnp.float32)
        bit *= 2
        if bit < count:
            held = held.astype(jnp.bfloat16)
        if bit == 2 and rider is not None:
            held, rider = lax.optimization_barrier((held, rider))
    return held[0].astype(jnp.float32), rider


def silu_grad(value):
    sigma = jax.nn.sigmoid(value)
    return sigma * (1.0 + value * (1.0 - sigma))


def rms_forward(value, gain):
    factor = lax.rsqrt(jnp.mean(value * value, axis=-1, keepdims=True) + EPSILON)
    return (value * factor * gain, factor)


def rms_backward(value, factor, gain, upstream):
    weighted = upstream * gain
    gain_grad = jnp.sum(upstream * value * factor, axis=0)
    inward = factor * weighted - value * factor * factor * factor * jnp.mean(
        weighted * value, axis=-1, keepdims=True
    )
    return (inward, gain_grad)


def matmul(left, right):
    return jnp.dot(left, right, preferred_element_type=jnp.float32)


def matmul_nt(left, right):
    return lax.dot_general(
        left, right, (((1,), (1,)), ((), ())), preferred_element_type=jnp.float32
    )


def matmul_tn(left, right):
    return lax.dot_general(
        left, right, (((0,), (0,)), ((), ())), preferred_element_type=jnp.float32
    )


def rope_tables(positions, head_size):
    half = head_size // 2
    freq_scale = ROPE_BASE ** (-jnp.arange(half, dtype=jnp.float32) / half)
    angles = positions.astype(jnp.float32)[:, None] * freq_scale[None, :]
    return (jnp.cos(angles), jnp.sin(angles))


def rotate(value, cosine, sine):
    half = value.shape[-1] // 2
    first = value[..., :half]
    second = value[..., half:]
    return jnp.concatenate(
        [first * cosine - second * sine, second * cosine + first * sine], axis=-1
    )


def rotate_back(grad, cosine, sine):
    half = grad.shape[-1] // 2
    first = grad[..., :half]
    second = grad[..., half:]
    return jnp.concatenate(
        [first * cosine + second * sine, second * cosine - first * sine], axis=-1
    )


def half_lanes(cols, first, shape):
    lane = lax.broadcasted_iota(jnp.int32, shape, 1)
    return jnp.where(lane < SSM_HEAD, cols[:, first : first + 1], cols[:, first + 1 : first + 2])


def dot_nn(left, right):
    return lax.dot_general(
        left, right, (((1,), (0,)), ((), ())), preferred_element_type=jnp.float32
    )


def each_pair(body):
    for k in range(PAIR_GROUP):
        body(k, pl.ds(k * LANES, LANES))


def ssm_state_kernel(xs_ref, b_ref, cols_ref, state_ref):
    b_low = b_ref[...].astype(jnp.bfloat16)

    def one(k, lanes):
        xs = xs_ref[:, lanes]
        cols = cols_ref[k]
        scaled = xs * half_lanes(cols, 2, xs.shape)
        tailed = (scaled * half_lanes(cols, 6, xs.shape)).astype(jnp.bfloat16)
        state_ref[k] = lax.dot_general(
            tailed, b_low, (((0,), (0,)), ((), ())), preferred_element_type=jnp.float32
        )

    each_pair(one)


def ssm_local_kernel(xs_ref, b_ref, c_ref, cols_ref, rows_ref, bias_ref, out_ref, cb_ref):
    bmat = b_ref[...]

    @pl.when(pl.program_id(0) == 0)
    def _():
        cb_ref[...] = lax.dot_general(
            c_ref[...],
            bmat,
            (((1,), (1,)), ((), ())),
            precision=lax.Precision.HIGHEST,
            preferred_element_type=jnp.float32,
        )

    def one(k, lanes):
        xs = xs_ref[:, lanes]
        cols = cols_ref[k]
        rows = rows_ref[k]
        scaled_b = (xs * half_lanes(cols, 2, xs.shape)).astype(jnp.bfloat16)
        parts = []
        for h in range(2):
            kernel = jnp.exp(cols[:, h : h + 1] - rows[h : h + 1, :] + bias_ref[...])
            parts.append(dot_nn((kernel * cb_ref[...]).astype(jnp.bfloat16), scaled_b))
        lane = lax.broadcasted_iota(jnp.int32, xs.shape, 1)
        out_ref[:, lanes] = jnp.where(lane < SSM_HEAD, parts[0], parts[1])

    each_pair(one)


def ssm_carry_kernel(local_ref, xs_ref, c_ref, cols_ref, state_ref, skip_ref, z_ref, out_ref, gated_ref):
    c_low = c_ref[...].astype(jnp.bfloat16)

    def one(k, lanes):
        xs = xs_ref[:, lanes]
        carried = lax.dot_general(
            c_low, state_ref[k], (((1,), (1,)), ((), ())), preferred_element_type=jnp.float32
        )
        entry = half_lanes(cols_ref[k], 4, xs.shape)
        out = local_ref[:, lanes] + entry * carried + skip_ref[:, lanes] * xs
        out_ref[:, lanes] = out
        gate = z_ref[:, lanes]
        gated_ref[:, lanes] = out * (gate * jax.nn.sigmoid(gate))

    each_pair(one)


def ssm_direct_kernel(g_ref, c_ref, cols_ref, direct_ref):
    c_low = c_ref[...].astype(jnp.bfloat16)

    def one(k, lanes):
        g = g_ref[:, lanes]
        entered = (g * half_lanes(cols_ref[k], 4, g.shape)).astype(jnp.bfloat16)
        direct_ref[k] = lax.dot_general(
            entered, c_low, (((0,), (0,)), ((), ())), preferred_element_type=jnp.float32
        )

    each_pair(one)


def ssm_backward_kernel(
    g_ref,
    xs_ref,
    out_ref,
    b_ref,
    c_ref,
    cols_ref,
    rows_ref,
    bias_ref,
    state_ref,
    later_ref,
    skip_ref,
    dxs_ref,
    db_ref,
    dc_ref,
    dcols_ref,
    drows_ref,
    cb_ref,
    dcb_ref,
):
    pair = pl.program_id(0)
    bmat = b_ref[...]
    cmat = c_ref[...]
    b_low = bmat.astype(jnp.bfloat16)
    c_low = cmat.astype(jnp.bfloat16)

    @pl.when(pair == 0)
    def _():
        cb_ref[...] = lax.dot_general(
            bmat,
            cmat,
            (((1,), (1,)), ((), ())),
            precision=lax.Precision.HIGHEST,
            preferred_element_type=jnp.float32,
        )
        dcb_ref[...] = jnp.zeros_like(dcb_ref)
        db_ref[...] = jnp.zeros_like(db_ref)
        dc_ref[...] = jnp.zeros_like(dc_ref)

    def one(at, lanes):
        g = g_ref[:, lanes]
        xs = xs_ref[:, lanes]
        skip = skip_ref[:, lanes]
        cols = cols_ref[at]
        rows = rows_ref[at]
        step = half_lanes(cols, 2, xs.shape)
        tail = half_lanes(cols, 6, xs.shape)
        lane = lax.broadcasted_iota(jnp.int32, xs.shape, 1)
        first = lane < SSM_HEAD
        g_low = g.astype(jnp.bfloat16)
        scaled = xs * step
        parts = []
        total = dcb_ref[...]
        for k in range(2):
            mine = first if k == 0 else jnp.logical_not(first)
            kernel = jnp.exp(rows[k : k + 1, :] - cols[:, k : k + 1] + bias_ref[...])
            parts.append(dot_nn((kernel * cb_ref[...]).astype(jnp.bfloat16), g_low))
            crossed = lax.dot_general(
                jnp.where(mine, scaled, 0.0).astype(jnp.bfloat16),
                g_low,
                (((1,), (1,)), ((), ())),
                preferred_element_type=jnp.float32,
            )
            total = total + crossed * kernel
        dcb_ref[...] = total
        later = later_ref[at]
        swept = tail * lax.dot_general(
            b_low, later, (((1,), (1,)), ((), ())), preferred_element_type=jnp.float32
        )
        inner = jnp.where(first, parts[0], parts[1]) + swept
        dxs_ref[:, lanes] = step * inner + skip * g
        db_ref[...] += dot_nn((scaled * tail).astype(jnp.bfloat16), later)
        entered = (g * half_lanes(cols, 4, g.shape)).astype(jnp.bfloat16)
        dc_ref[...] += dot_nn(entered, state_ref[at])
        rose = g_low.astype(jnp.float32) * (out_ref[:, lanes] - skip * xs)
        stepped = xs * inner
        kept = scaled.astype(jnp.bfloat16).astype(jnp.float32)
        fell = kept * (inner - swept) + scaled * swept
        columns = [
            jnp.sum(jnp.where(first, value, 0.0), axis=1, keepdims=True)
            if k == 0
            else jnp.sum(jnp.where(first, 0.0, value), axis=1, keepdims=True)
            for value in (rose, stepped, fell)
            for k in range(2)
        ]
        spot = lax.broadcasted_iota(jnp.int32, cols.shape, 1)
        packed = jnp.zeros_like(cols)
        for index, column in enumerate(columns):
            packed = jnp.where(spot == index, column, packed)
        dcols_ref[at] = packed
        drows_ref[at, 0:1, :] = jnp.sum(scaled * swept, axis=0, keepdims=True)
        drows_ref[at, 1:2, :] = jnp.sum(g * xs, axis=0, keepdims=True)

    each_pair(one)

    @pl.when(pair == pl.num_programs(0) - 1)
    def _():
        low = dcb_ref[...].astype(jnp.bfloat16)
        db_ref[...] += dot_nn(low, c_low)
        dc_ref[...] += lax.dot_general(
            low, b_low, (((0,), (0,)), ((), ())), preferred_element_type=jnp.float32
        )


def ssm_specs(rows):
    wide = PAIR_GROUP * LANES
    block = pl.BlockSpec((rows, wide), lambda p: (0, p))
    bmat = pl.BlockSpec((rows, LANES), lambda p: (0, SSM_PAIRS))
    cmat = pl.BlockSpec((rows, LANES), lambda p: (0, SSM_PAIRS + 1))
    cols = pl.BlockSpec((PAIR_GROUP, rows, 8), lambda p: (p, 0, 0))
    turned = pl.BlockSpec((PAIR_GROUP, 2, rows), lambda p: (p, 0, 0))
    bias = pl.BlockSpec((rows, rows), lambda p: (0, 0))
    state = pl.BlockSpec((PAIR_GROUP, LANES, STATE), lambda p: (p, 0, 0))
    skip = pl.BlockSpec((1, wide), lambda p: (0, p))
    whole = pl.BlockSpec((rows, LANES), lambda p: (0, 0))
    return block, bmat, cmat, cols, turned, bias, state, skip, whole


def ssm_state(act, cols):
    rows = act.shape[0]
    block, bmat, cmat, col, turn, square, state, skip, whole = ssm_specs(rows)
    return pl.pallas_call(
        ssm_state_kernel,
        grid=(SSM_PAIRS // PAIR_GROUP,),
        in_specs=[block, bmat, col],
        out_specs=state,
        out_shape=jax.ShapeDtypeStruct((SSM_PAIRS, LANES, STATE), jnp.float32),
        name="ssm_state",
        cost_estimate=pl.CostEstimate(flops=10**8, transcendentals=0, bytes_accessed=4 * 10**6),
    )(act, act, cols)


def ssm_local(act, cols, turned, bias):
    rows = act.shape[0]
    block, bmat, cmat, col, turn, square, state, skip, whole = ssm_specs(rows)
    return pl.pallas_call(
        ssm_local_kernel,
        grid=(SSM_PAIRS // PAIR_GROUP,),
        in_specs=[block, bmat, cmat, col, turn, square],
        out_specs=block,
        out_shape=jax.ShapeDtypeStruct((rows, SSM_PAIRS * LANES), jnp.float32),
        scratch_shapes=[pltpu.VMEM((rows, rows), jnp.float32)],
        name="ssm_local",
        cost_estimate=pl.CostEstimate(flops=10**9, transcendentals=24 * rows * rows, bytes_accessed=6 * 10**6),
    )(act, act, act, cols, turned, bias)


def ssm_carried(local_part, act, cols, state, skip_row, projected):
    rows = act.shape[0]
    block, bmat, cmat, col, turn, square, states, skip, whole = ssm_specs(rows)
    shape = jax.ShapeDtypeStruct((rows, SSM_PAIRS * LANES), jnp.float32)
    return pl.pallas_call(
        ssm_carry_kernel,
        grid=(SSM_PAIRS // PAIR_GROUP,),
        in_specs=[block, block, cmat, col, states, skip, block],
        out_specs=[block, block],
        out_shape=[shape, shape],
        name="ssm_carried",
        cost_estimate=pl.CostEstimate(flops=10**8, transcendentals=rows * 1536, bytes_accessed=9 * 10**6),
    )(local_part, act, act, cols, state, skip_row, projected)


def ssm_direct(g, act, cols):
    rows = act.shape[0]
    block, bmat, cmat, col, turn, square, states, skip, whole = ssm_specs(rows)
    return pl.pallas_call(
        ssm_direct_kernel,
        grid=(SSM_PAIRS // PAIR_GROUP,),
        in_specs=[block, cmat, col],
        out_specs=states,
        out_shape=jax.ShapeDtypeStruct((SSM_PAIRS, LANES, STATE), jnp.float32),
        name="ssm_direct",
        cost_estimate=pl.CostEstimate(flops=10**8, transcendentals=0, bytes_accessed=4 * 10**6),
    )(g, act, cols)


def ssm_backward(g, act, out, cols, turned, bias_turned, state, later, skip_row):
    rows = act.shape[0]
    block, bmat, cmat, col, turn, square, states, skip, whole = ssm_specs(rows)
    return pl.pallas_call(
        ssm_backward_kernel,
        grid=(SSM_PAIRS // PAIR_GROUP,),
        in_specs=[block, block, block, bmat, cmat, col, turn, square, states, states, skip],
        out_specs=[block, whole, whole, col, pl.BlockSpec((PAIR_GROUP, 2, LANES), lambda p: (p, 0, 0))],
        out_shape=[
            jax.ShapeDtypeStruct((rows, SSM_PAIRS * LANES), jnp.float32),
            jax.ShapeDtypeStruct((rows, STATE), jnp.float32),
            jax.ShapeDtypeStruct((rows, STATE), jnp.float32),
            jax.ShapeDtypeStruct((SSM_PAIRS, rows, 8), jnp.float32),
            jax.ShapeDtypeStruct((SSM_PAIRS, 2, LANES), jnp.float32),
        ],
        scratch_shapes=[pltpu.VMEM((rows, rows), jnp.float32)] * 2,
        name="ssm_backward",
        cost_estimate=pl.CostEstimate(flops=2 * 10**9, transcendentals=24 * rows * rows, bytes_accessed=12 * 10**6),
    )(g, act, out, act, act, cols, turned, bias_turned, state, later, skip_row)


def outer_kernel(split, left_a_ref, right_a_ref, left_b_ref, right_b_ref, out_ref, turned_ref):
    step = pl.program_id(0)

    @pl.when(step == 0)
    def _():
        turned_ref[...] = left_a_ref[...].T

    @pl.when(step == split)
    def _():
        turned_ref[...] = left_b_ref[...].T

    def filled(right_ref):
        wide = right_ref.shape[1]
        piece = math.gcd(wide, 256)
        for at in range(0, wide, piece):
            lanes = pl.ds(at, piece)
            out_ref[:, lanes] = dot_nn(turned_ref[...], right_ref[:, lanes]).astype(jnp.bfloat16)

    @pl.when(step < split)
    def _():
        filled(right_a_ref)

    @pl.when(step >= split)
    def _():
        filled(right_b_ref)


def outer_pair(left_a, right_a, left_b, right_b):
    rows, width = left_a.shape
    wide_a = right_a.shape[1]
    wide_b = right_b.shape[1]
    wide = math.gcd(math.gcd(wide_a, wide_b), 1024)
    split = wide_a // wide
    total = split + wide_b // wide
    held = pl.BlockSpec((rows, width), lambda j: (0, 0))
    return pl.pallas_call(
        functools.partial(outer_kernel, split),
        grid=(total,),
        in_specs=[
            held,
            pl.BlockSpec((rows, wide), lambda j: (0, jnp.minimum(j, split - 1))),
            held,
            pl.BlockSpec((rows, wide), lambda j: (0, jnp.maximum(j - split, 0))),
        ],
        out_specs=pl.BlockSpec((width, wide), lambda j: (0, j)),
        out_shape=jax.ShapeDtypeStruct((width, wide_a + wide_b), jnp.bfloat16),
        scratch_shapes=[pltpu.VMEM((width, rows), jnp.bfloat16)],
        name="outer_pair",
        cost_estimate=pl.CostEstimate(
            flops=2 * rows * width * (wide_a + wide_b),
            transcendentals=0,
            bytes_accessed=2 * width * (wide_a + wide_b),
        ),
    )(left_a, right_a, left_b, right_b)


def local(
    block_in,
    segment_ids,
    mamba_z,
    mamba_x,
    mamba_bc,
    mamba_dt,
    mamba_out,
    attn_q,
    attn_kv,
    attn_out,
    ffn_gate,
    ffn_up,
    ffn_down,
    mixer_norm,
    ffn_norm,
    conv_weight,
    conv_bias,
    dt_bias,
    a_log,
    d_skip,
    inner_norm,
    grad_out,
):
    sequences, rows, width = block_in.shape
    length = segment_ids.shape[1]
    taps = conv_weight.shape[0]
    group = Q_HEADS // KV_HEADS
    inner_width = SSM_HEADS * SSM_HEAD
    total_rows = sequences * rows
    inv_root = HEAD ** (-0.5)
    offset = lax.axis_index("seq") * rows
    positions = offset + jnp.arange(rows, dtype=jnp.int32)
    local_ids = lax.dynamic_slice_in_dim(segment_ids, offset, rows, 1)
    padded_ids = jnp.concatenate(
        [jnp.full((sequences, taps - 1), -1, jnp.int32), segment_ids], axis=1
    )
    window_ids = lax.dynamic_slice_in_dim(padded_ids, offset, rows + taps - 1, 1)
    prior_id = window_ids[:, taps - 2]
    tap_masks = [
        (window_ids[:, tap : tap + rows] == local_ids).astype(jnp.float32)[:, :, None]
        for tap in range(taps)
    ]
    cosine, sine = rope_tables(positions, HEAD)
    cos_b = cosine[:, None, :]
    sin_b = sine[:, None, :]
    behind = min(lax.axis_size("seq") - 1, (MAX_DOC - 2) // rows + 1) * rows
    key_ids = lax.dynamic_slice_in_dim(
        jnp.concatenate([jnp.full((sequences, behind), -1, jnp.int32), segment_ids], axis=1),
        offset,
        behind + rows,
        1,
    )
    key_order = jnp.arange(behind + rows, dtype=jnp.int32) - behind
    allowed = (key_order[None, None, :] <= jnp.arange(rows, dtype=jnp.int32)[None, :, None]) & (
        key_ids[:, None, :] == local_ids[:, :, None]
    )
    hops = min(lax.axis_size("seq") - 1, (MAX_DOC - 2) // rows + 1)
    spare = -(mamba_dt.shape[1] + 2) % LANES
    shard_in = jnp.concatenate(
        [
            mamba_z,
            attn_q,
            mamba_x,
            mamba_bc,
            attn_kv,
            mamba_dt,
            mixer_norm[:, None],
            ffn_norm[:, None],
            jnp.zeros((mixer_norm.shape[0], spare), jnp.bfloat16),
        ],
        axis=1,
    )
    shard_out = jnp.concatenate([mamba_out, attn_out, ffn_gate, ffn_up, ffn_down], axis=1)
    full_in = lax.all_gather(shard_in, ("dp", "seq"), axis=0, tiled=True)
    full_out = lax.all_gather(gathered_seq(shard_out), "dp", axis=0, tiled=True)
    bc_width = mamba_bc.shape[1]
    q_width = attn_q.shape[1]
    kv_width = attn_kv.shape[1]
    hidden_width = ffn_gate.shape[1]
    at_q = inner_width
    at_u = at_q + q_width
    at_kv = at_u + inner_width + bc_width
    at_dt = at_kv + kv_width
    at_gain = at_dt + SSM_HEADS
    mixer_width = inner_width + q_width
    full_mixer = full_out[:, :mixer_width]
    full_gateup = full_out[:, mixer_width : mixer_width + 2 * hidden_width]
    full_down = full_out[:, mixer_width + 2 * hidden_width :]
    gain_one = full_in[:, at_gain].astype(jnp.float32)
    gain_two = full_in[:, at_gain + 1].astype(jnp.float32)
    x_in = block_in.reshape(total_rows, width).astype(jnp.float32)
    normed, factor_one = rms_forward(x_in, gain_one)
    normed_b = normed.astype(jnp.bfloat16)
    projected = matmul(normed_b, full_in)
    gate_z = projected[:, :at_q]
    inner_u = projected[:, at_u:at_kv]
    step_raw = projected[:, at_dt:at_gain]
    channels = inner_u.shape[1]
    conv_in = inner_u.reshape(sequences, rows, channels)
    edge_in = passed_along(conv_in[:, rows - taps + 1 :, :], "seq", 1)
    extended = jnp.concatenate([edge_in, conv_in], axis=1)
    conv_pre = jnp.zeros_like(conv_in) + conv_bias
    for tap in range(taps):
        conv_pre = conv_pre + conv_weight[tap] * extended[:, tap : tap + rows] * tap_masks[tap]
    activated = jax.nn.silu(conv_pre)
    act = activated.reshape(total_rows, channels)
    step = jax.nn.softplus(step_raw + dt_bias)
    ids = local_ids.reshape(total_rows)
    order = jnp.arange(rows)
    pair = (order[:, None] >= order[None, :]) & (ids[:, None] == ids[None, :])
    bias = jnp.where(pair, 0.0, -1e30).astype(jnp.float32)
    bias_turned = jnp.where(
        (order[:, None] <= order[None, :]) & (ids[:, None] == ids[None, :]), 0.0, -1e30
    ).astype(jnp.float32)
    inbound = (ids == prior_id[0]).astype(jnp.float32)[:, None]
    outbound = (ids == ids[-1]).astype(jnp.float32)[:, None]
    rate = -jnp.exp(a_log)
    ladder = (order[:, None] >= order[None, :]).astype(jnp.float32)
    decay = jnp.dot(ladder, step * rate, precision=lax.Precision.HIGHEST)
    entry = jnp.exp(decay) * inbound
    tail = jnp.exp(decay[-1:] - decay) * outbound
    carry = jnp.exp(decay[-1]) * inbound[-1, 0]
    cols = jnp.stack([decay, step, entry, tail], axis=1)
    cols = cols.reshape(rows, 4, SSM_PAIRS, 2).transpose(2, 0, 1, 3).reshape(SSM_PAIRS, rows, 8)
    turned = decay.T.reshape(SSM_PAIRS, 2, rows)
    skip_row = jnp.repeat(d_skip, SSM_HEAD)[None, :]
    carry_rows = jnp.repeat(carry, SSM_HEAD).reshape(SSM_PAIRS, LANES, 1)
    state_local = ssm_state(act, cols)
    outgoing = state_local
    for hop in range(hops):
        incoming = passed_along(outgoing.astype(jnp.bfloat16), "seq", 1)
        outgoing = carry_rows * incoming.astype(jnp.float32) + state_local
    local_part = ssm_local(act, cols, turned, bias)
    ssm_out, gated = ssm_carried(local_part, act, cols, incoming, skip_row, projected)
    silu_z = jax.nn.silu(gate_z)
    mixed_norm, factor_m = rms_forward(gated, inner_norm)
    mixed_b = mixed_norm.astype(jnp.bfloat16)
    query = projected[:, at_q:at_u].reshape(sequences, rows, Q_HEADS, HEAD)
    keyval = projected[:, at_kv:at_dt].reshape(sequences, rows, 2 * KV_HEADS, HEAD)
    query_b = rotate(query, cos_b, sin_b).astype(jnp.bfloat16)
    keys_local = rotate(keyval[:, :, :KV_HEADS], cos_b, sin_b)
    kv_local = jnp.concatenate([keys_local, keyval[:, :, KV_HEADS:]], axis=2).astype(jnp.bfloat16)
    kv_flat = kv_local.reshape(sequences, rows, kv_width)
    kv_all = jnp.concatenate(
        [passed_along(kv_flat, "seq", far) for far in range(hops, 0, -1)] + [kv_flat], axis=1
    )
    window = kv_all.shape[1]
    kv_all = kv_all.reshape(sequences, window, 2 * KV_HEADS, HEAD)
    keys = kv_all[:, :, :KV_HEADS]
    values = kv_all[:, :, KV_HEADS:]
    query_g = query_b.reshape(sequences, rows, KV_HEADS, group, HEAD)

    def attention_scores():
        raw = (
            jnp.einsum("stkgd,slkd->skgtl", query_g, keys, preferred_element_type=jnp.float32)
            * inv_root
        )
        return jnp.where(allowed[:, None, None], raw, -1e30)

    scores = attention_scores()
    top = jnp.max(scores, axis=-1, keepdims=True)
    lse = top + jnp.log(jnp.sum(jnp.exp(scores - top), axis=-1, keepdims=True))
    probs_b = jnp.exp(scores - lse).astype(jnp.bfloat16)
    attended = jnp.einsum("skgtl,slkd->stkgd", probs_b, values, preferred_element_type=jnp.float32)
    attended_b = attended.reshape(total_rows, Q_HEADS * HEAD).astype(jnp.bfloat16)
    mixers_b = jnp.concatenate([mixed_b, attended_b], axis=1)
    mid = x_in + matmul_nt(mixers_b, full_mixer)
    fnormed, factor_two = rms_forward(mid, gain_two)
    fnormed_b = fnormed.astype(jnp.bfloat16)
    gateup_h = matmul(fnormed_b, full_gateup)
    gate_h = gateup_h[:, :hidden_width]
    up_h = gateup_h[:, hidden_width:]
    hidden_b = (jax.nn.silu(gate_h) * up_h).astype(jnp.bfloat16)
    block_out = (
        (mid + matmul_nt(hidden_b, full_down)).astype(jnp.bfloat16).reshape(sequences, rows, width)
    )
    grad_flat = grad_out.reshape(total_rows, width)
    d_hidden = matmul(grad_flat, full_down)
    d_gate_b = (d_hidden * up_h * silu_grad(gate_h)).astype(jnp.bfloat16)
    d_up_b = (d_hidden * jax.nn.silu(gate_h)).astype(jnp.bfloat16)
    d_gateup_b = jnp.concatenate([d_gate_b, d_up_b], axis=1)
    part_ffn = scattered_dp(outer_pair(fnormed_b, d_gateup_b, grad_flat, hidden_b))
    d_fnorm = matmul_nt(d_gateup_b, full_gateup)
    d_mid_norm, g_fnorm = rms_backward(mid, factor_two, gain_two, d_fnorm)
    d_mid = grad_flat.astype(jnp.float32) + d_mid_norm
    d_mid_b = d_mid.astype(jnp.bfloat16)
    d_mixers = matmul(d_mid_b, full_mixer)
    d_mnorm = d_mixers[:, :inner_width]
    d_gated, g_inner = rms_backward(gated, factor_m, inner_norm, d_mnorm)
    d_ssm = d_gated * silu_z
    d_z = d_gated * ssm_out * silu_grad(gate_z)
    direct = ssm_direct(d_ssm, act, cols)
    backlog = direct
    for hop in range(hops):
        later_grad = passed_along(backlog.astype(jnp.bfloat16), "seq", -1)
        backlog = direct + carry_rows * later_grad.astype(jnp.float32)
    d_carry = jnp.sum(
        (later_grad.astype(jnp.float32) * incoming.astype(jnp.float32)).reshape(
            SSM_HEADS, SSM_HEAD, STATE
        ),
        axis=(1, 2),
    )
    d_att_b = d_mixers[:, inner_width:].astype(jnp.bfloat16)
    d_att_g = d_att_b.reshape(sequences, rows, KV_HEADS, group, HEAD)
    probs = jnp.exp(attention_scores() - lse)
    d_probs = jnp.einsum("stkgd,slkd->skgtl", d_att_g, values, preferred_element_type=jnp.float32)
    d_scores_b = (probs * (d_probs - jnp.sum(probs * d_probs, axis=-1, keepdims=True))).astype(
        jnp.bfloat16
    )
    d_query = (
        jnp.einsum("skgtl,slkd->stkgd", d_scores_b, keys, preferred_element_type=jnp.float32)
        * inv_root
    )
    d_keys = (
        jnp.einsum("skgtl,stkgd->slkd", d_scores_b, query_g, preferred_element_type=jnp.float32)
        * inv_root
    )
    d_values = jnp.einsum("skgtl,stkgd->slkd", probs_b, d_att_g, preferred_element_type=jnp.float32)
    d_kv_all = jnp.concatenate([d_keys, d_values], axis=2).reshape(sequences, window, kv_width)
    d_kv_local = d_kv_all[:, window - rows :]
    for far in range(1, hops + 1):
        start = window - (far + 1) * rows
        term = d_kv_all[:, start : start + rows].astype(jnp.bfloat16)
        d_kv_local = d_kv_local + passed_along(term, "seq", -far).astype(jnp.float32)
    d_kv_local = d_kv_local.reshape(sequences, rows, 2 * KV_HEADS, HEAD)
    d_key_local = rotate_back(d_kv_local[:, :, :KV_HEADS], cos_b, sin_b)
    d_kv_b = (
        jnp.concatenate([d_key_local, d_kv_local[:, :, KV_HEADS:]], axis=2)
        .reshape(total_rows, 2 * KV_HEADS * HEAD)
        .astype(jnp.bfloat16)
    )
    d_q_b = (
        rotate_back(d_query.reshape(sequences, rows, Q_HEADS, HEAD), cos_b, sin_b)
        .reshape(total_rows, Q_HEADS * HEAD)
        .astype(jnp.bfloat16)
    )
    d_early = jnp.concatenate([d_z.astype(jnp.bfloat16), d_q_b], axis=1)
    g_early = outer_pair(normed_b, d_early, d_mid_b, mixers_b)
    later_grad, g_early = lax.optimization_barrier((later_grad, g_early))
    part_early = scattered_dp(g_early)
    d_xs, d_bmat, d_cmat, d_cols, d_rows = ssm_backward(
        d_ssm, act, ssm_out, cols, turned, bias_turned, incoming, later_grad, skip_row
    )
    d_pairs = d_cols[:, :, :6].reshape(SSM_PAIRS, rows, 3, 2).transpose(2, 1, 0, 3)
    d_pairs = d_pairs.reshape(3, rows, SSM_HEADS)
    d_sums = jnp.sum(d_rows.reshape(SSM_PAIRS, 2, 2, SSM_HEAD), axis=3).transpose(1, 0, 2)
    d_sums = d_sums.reshape(2, SSM_HEADS)
    g_skip = d_sums[1]
    d_decay = d_pairs[0] - d_pairs[2]
    d_rise = jnp.dot(ladder.T, d_decay, precision=lax.Precision.HIGHEST)
    d_rise = d_rise + (d_sums[0] + d_carry * carry)
    d_step = d_pairs[1] + d_rise * rate
    g_alog = jnp.sum(d_rise * step, axis=0) * rate
    d_act = jnp.concatenate([d_xs, d_bmat, d_cmat], axis=1).reshape(sequences, rows, channels)
    d_act, part_ffn = lax.optimization_barrier((d_act, part_ffn))
    owned_ffn, _ = hopped_seq(part_ffn, None)
    d_pre = d_act * silu_grad(conv_pre)
    g_cbias = jnp.sum(d_pre, axis=(0, 1))
    g_cweight = jnp.stack(
        [
            jnp.sum(d_pre * extended[:, tap : tap + rows] * tap_masks[tap], axis=(0, 1))
            for tap in range(taps)
        ]
    )
    d_padded = jnp.zeros_like(extended)
    for tap in range(taps):
        d_padded = d_padded + jnp.pad(
            d_pre * tap_masks[tap] * conv_weight[tap], ((0, 0), (tap, taps - 1 - tap), (0, 0))
        )
    edge_grad = passed_along(d_padded[:, : taps - 1], "seq", -1)
    d_inner = d_padded[:, taps - 1 :] + jnp.pad(edge_grad, ((0, 0), (rows - taps + 1, 0), (0, 0)))
    d_inner = d_inner.reshape(total_rows, channels)
    d_step_raw = d_step.reshape(total_rows, SSM_HEADS) * jax.nn.sigmoid(step_raw + dt_bias)
    g_dtb = jnp.sum(d_step_raw, axis=0)
    d_x_b = d_inner[:, :inner_width].astype(jnp.bfloat16)
    d_bc_b = d_inner[:, inner_width:].astype(jnp.bfloat16)
    d_st_b = d_step_raw.astype(jnp.bfloat16)
    d_late = jnp.concatenate(
        [
            d_x_b,
            d_bc_b,
            d_kv_b,
            d_st_b,
            jnp.zeros((total_rows, spare + 2), jnp.bfloat16),
        ],
        axis=1,
    )
    part_late = scattered_dp(matmul_tn(normed_b, d_late).astype(jnp.bfloat16))
    d_norm = matmul_nt(d_early, full_in[:, :at_u]) + matmul_nt(d_late, full_in[:, at_u:])
    d_in_norm, g_mnorm = rms_backward(x_in, factor_one, gain_one, d_norm)
    grad_in = (d_mid + d_in_norm).astype(jnp.bfloat16).reshape(sequences, rows, width)
    summed = lax.psum(
        (g_cweight, g_cbias, g_dtb, g_alog, g_skip, g_inner, g_mnorm, g_fnorm), ("dp", "seq")
    )
    gain_rows = mixer_norm.shape[0]
    part_early, summed, grad_in = lax.optimization_barrier((part_early, summed, grad_in))
    owned_early, part_late = hopped_seq(part_early, part_late)
    owned_late = scattered_seq(part_late)
    first_row = (lax.axis_index("dp") * lax.axis_size("seq") + lax.axis_index("seq")) * gain_rows
    g_mnorm_own = lax.dynamic_slice_in_dim(summed[6], first_row, gain_rows, 0)
    g_fnorm_own = lax.dynamic_slice_in_dim(summed[7], first_row, gain_rows, 0)
    at_mixers = at_u
    late_kv = at_kv - at_u
    late_dt = at_dt - at_u
    return (
        block_out,
        grad_in,
        owned_early[:, :at_q],
        owned_late[:, :inner_width],
        owned_late[:, inner_width:late_kv],
        owned_late[:, late_dt : late_dt + SSM_HEADS],
        owned_early[:, at_mixers : at_mixers + inner_width],
        owned_early[:, at_q:at_u],
        owned_late[:, late_kv:late_dt],
        owned_early[:, at_mixers + inner_width :],
        owned_ffn[:, :hidden_width],
        owned_ffn[:, hidden_width : 2 * hidden_width],
        owned_ffn[:, 2 * hidden_width :],
        g_mnorm_own,
        g_fnorm_own,
        summed[0],
        summed[1],
        summed[2],
        summed[3],
        summed[4],
        summed[5],
    )


def solution(mesh):
    in_specs = (
        P("dp", "seq", None),
        P("dp", None),
        P(("dp", "seq"), None),
        P(("dp", "seq"), None),
        P(("dp", "seq"), None),
        P(("dp", "seq"), None),
        P(("dp", "seq"), None),
        P(("dp", "seq"), None),
        P(("dp", "seq"), None),
        P(("dp", "seq"), None),
        P(("dp", "seq"), None),
        P(("dp", "seq"), None),
        P(("dp", "seq"), None),
        P(("dp", "seq")),
        P(("dp", "seq")),
        P(),
        P(),
        P(),
        P(),
        P(),
        P(),
        P("dp", "seq", None),
    )
    out_specs = (
        P("dp", "seq", None),
        P("dp", "seq", None),
        P(("dp", "seq"), None),
        P(("dp", "seq"), None),
        P(("dp", "seq"), None),
        P(("dp", "seq"), None),
        P(("dp", "seq"), None),
        P(("dp", "seq"), None),
        P(("dp", "seq"), None),
        P(("dp", "seq"), None),
        P(("dp", "seq"), None),
        P(("dp", "seq"), None),
        P(("dp", "seq"), None),
        P(("dp", "seq")),
        P(("dp", "seq")),
        P(),
        P(),
        P(),
        P(),
        P(),
        P(),
    )
    return jax.shard_map(local, mesh=mesh, in_specs=in_specs, out_specs=out_specs, check_vma=False)
```

```python
import functools
import math

import jax
import jax.numpy as jnp
from jax import lax
from jax.experimental import pallas as pl
from jax.experimental.pallas import tpu as pltpu
from jax.sharding import Mesh
from jax.sharding import PartitionSpec as P

SSM_HEADS = 24
SSM_HEAD = 64
STATE = 128
Q_HEADS = 8
KV_HEADS = 2
HEAD = 64


EPSILON = 1e-05
ROPE_BASE = 100000000000.0
MAX_DOC = 512
LANES = 128
SSM_PAIRS = SSM_HEADS * SSM_HEAD // LANES
PAIR_GROUP = 4
DP = ("dpo", "core")


def passed_along(block, axis, distance):
    devices = range(lax.axis_size(axis))
    route = [(i - distance, i) for i in devices if i - distance in devices]
    return lax.ppermute(block, axis, route)


def scattered_dp(grad):
    return lax.psum_scatter(grad, ("dpo", "core"), scatter_dimension=0, tiled=True)


def swapped(block):
    return lax.ppermute(block, "core", [(0, 1), (1, 0)])


def paired_cores(own, other):
    return (own.astype(jnp.float32) + swapped(other).astype(jnp.float32)).astype(jnp.bfloat16)


def scattered_own(paired):
    return lax.psum_scatter(paired, "dpo", scatter_dimension=0, tiled=True)


def split_by_core(block):
    rows, width = block.shape
    views = block.reshape(rows, lax.axis_size("dpo"), 2, -1)
    low = views[:, :, 0].reshape(rows, width // 2)
    high = views[:, :, 1].reshape(rows, width // 2)
    second = lax.axis_index("core") == 1
    return jnp.where(second, high, low), jnp.where(second, low, high)


def summed_everywhere(block):
    for axis in ("core", "dpo", "seq"):
        count = lax.axis_size(axis)
        bit = 1
        while bit < count:
            block = block + lax.ppermute(block, axis, [(i, i ^ bit) for i in range(count)])
            bit *= 2
    return block


def scattered_seq(part):
    return lax.psum_scatter(part, "seq", scatter_dimension=0, tiled=True).astype(jnp.float32)


def gathered_seq(shard):
    index = lax.axis_index("seq")
    count = lax.axis_size("seq")
    held = shard
    bit = 1
    while bit < count:
        got = lax.ppermute(held, "seq", [(i, i ^ bit) for i in range(count)])
        odd = (index // bit) % 2 == 1
        held = jnp.concatenate([jnp.where(odd, got, held), jnp.where(odd, held, got)], axis=0)
        bit *= 2
    return held


def hopped_seq(part, rider):
    index = lax.axis_index("seq")
    count = lax.axis_size("seq")
    held = part.reshape(count, part.shape[0] // count, part.shape[1])
    bit = 1
    while bit < count:
        halves = held.reshape(held.shape[0] // 2, 2, *held.shape[1:])
        odd = (index // bit) % 2 == 1
        mine = jnp.where(odd, halves[:, 1], halves[:, 0])
        other = jnp.where(odd, halves[:, 0], halves[:, 1])
        got = lax.ppermute(other, "seq", [(i, i ^ bit) for i in range(count)])
        held = mine.astype(jnp.float32) + got.astype(jnp.float32)
        bit *= 2
        if bit < count:
            held = held.astype(jnp.bfloat16)
        if bit == 2 and rider is not None:
            held, rider = lax.optimization_barrier((held, rider))
    return held[0].astype(jnp.float32), rider


def silu_grad(value):
    sigma = jax.nn.sigmoid(value)
    return sigma * (1.0 + value * (1.0 - sigma))


def rms_forward(value, gain):
    factor = lax.rsqrt(jnp.mean(value * value, axis=-1, keepdims=True) + EPSILON)
    return (value * factor * gain, factor)


def rms_backward(value, factor, gain, upstream):
    weighted = upstream * gain
    gain_grad = jnp.sum(upstream * value * factor, axis=0)
    inward = factor * weighted - value * factor * factor * factor * jnp.mean(
        weighted * value, axis=-1, keepdims=True
    )
    return (inward, gain_grad)


def matmul(left, right):
    return jnp.dot(left, right, preferred_element_type=jnp.float32)


def matmul_nt(left, right):
    return lax.dot_general(
        left, right, (((1,), (1,)), ((), ())), preferred_element_type=jnp.float32
    )


def matmul_tn(left, right):
    return lax.dot_general(
        left, right, (((0,), (0,)), ((), ())), preferred_element_type=jnp.float32
    )


def rope_tables(positions, head_size):
    half = head_size // 2
    freq_scale = ROPE_BASE ** (-jnp.arange(half, dtype=jnp.float32) / half)
    angles = positions.astype(jnp.float32)[:, None] * freq_scale[None, :]
    return (jnp.cos(angles), jnp.sin(angles))


def rotate(value, cosine, sine):
    half = value.shape[-1] // 2
    first = value[..., :half]
    second = value[..., half:]
    return jnp.concatenate(
        [first * cosine - second * sine, second * cosine + first * sine], axis=-1
    )


def rotate_back(grad, cosine, sine):
    half = grad.shape[-1] // 2
    first = grad[..., :half]
    second = grad[..., half:]
    return jnp.concatenate(
        [first * cosine + second * sine, second * cosine - first * sine], axis=-1
    )


def half_lanes(cols, first, shape):
    lane = lax.broadcasted_iota(jnp.int32, shape, 1)
    return jnp.where(lane < SSM_HEAD, cols[:, first : first + 1], cols[:, first + 1 : first + 2])


def dot_nn(left, right):
    return lax.dot_general(
        left, right, (((1,), (0,)), ((), ())), preferred_element_type=jnp.float32
    )


def each_pair(body):
    def turn(k, carry):
        body(k, pl.ds(pl.multiple_of(k * LANES, LANES), LANES))
        return carry

    lax.fori_loop(0, PAIR_GROUP, turn, 0)


def ssm_state_kernel(xs_ref, b_ref, cols_ref, state_ref):
    b_low = b_ref[...].astype(jnp.bfloat16)

    def one(k, lanes):
        xs = xs_ref[:, lanes]
        cols = cols_ref[k]
        scaled = xs * half_lanes(cols, 2, xs.shape)
        tailed = (scaled * half_lanes(cols, 6, xs.shape)).astype(jnp.bfloat16)
        state_ref[k] = lax.dot_general(
            tailed, b_low, (((0,), (0,)), ((), ())), preferred_element_type=jnp.float32
        )

    each_pair(one)


def ssm_local_kernel(xs_ref, b_ref, c_ref, cols_ref, rows_ref, bias_ref, out_ref, cb_ref):
    bmat = b_ref[...]

    @pl.when(pl.program_id(0) == 0)
    def _():
        cb_ref[...] = lax.dot_general(
            c_ref[...],
            bmat,
            (((1,), (1,)), ((), ())),
            precision=lax.Precision.HIGHEST,
            preferred_element_type=jnp.float32,
        )

    def one(k, lanes):
        xs = xs_ref[:, lanes]
        cols = cols_ref[k]
        rows = rows_ref[k]
        scaled_b = (xs * half_lanes(cols, 2, xs.shape)).astype(jnp.bfloat16)
        parts = []
        for h in range(2):
            kernel = jnp.exp(cols[:, h : h + 1] - rows[h : h + 1, :] + bias_ref[...])
            parts.append(dot_nn((kernel * cb_ref[...]).astype(jnp.bfloat16), scaled_b))
        lane = lax.broadcasted_iota(jnp.int32, xs.shape, 1)
        out_ref[:, lanes] = jnp.where(lane < SSM_HEAD, parts[0], parts[1])

    each_pair(one)


def ssm_carry_kernel(local_ref, xs_ref, c_ref, cols_ref, state_ref, skip_ref, z_ref, out_ref, gated_ref):
    c_low = c_ref[...].astype(jnp.bfloat16)

    def one(k, lanes):
        xs = xs_ref[:, lanes]
        carried = lax.dot_general(
            c_low, state_ref[k], (((1,), (1,)), ((), ())), preferred_element_type=jnp.float32
        )
        entry = half_lanes(cols_ref[k], 4, xs.shape)
        out = local_ref[:, lanes] + entry * carried + skip_ref[:, lanes] * xs
        out_ref[:, lanes] = out
        gate = z_ref[:, lanes]
        gated_ref[:, lanes] = out * (gate * jax.nn.sigmoid(gate))

    each_pair(one)


def ssm_direct_kernel(g_ref, c_ref, cols_ref, direct_ref):
    c_low = c_ref[...].astype(jnp.bfloat16)

    def one(k, lanes):
        g = g_ref[:, lanes]
        entered = (g * half_lanes(cols_ref[k], 4, g.shape)).astype(jnp.bfloat16)
        direct_ref[k] = lax.dot_general(
            entered, c_low, (((0,), (0,)), ((), ())), preferred_element_type=jnp.float32
        )

    each_pair(one)


def ssm_backward_kernel(
    g_ref,
    xs_ref,
    out_ref,
    b_ref,
    c_ref,
    cols_ref,
    rows_ref,
    bias_ref,
    state_ref,
    later_ref,
    skip_ref,
    dxs_ref,
    db_ref,
    dc_ref,
    dcols_ref,
    drows_ref,
    cb_ref,
    dcb_ref,
):
    pair = pl.program_id(0)
    bmat = b_ref[...]
    cmat = c_ref[...]
    b_low = bmat.astype(jnp.bfloat16)
    c_low = cmat.astype(jnp.bfloat16)

    @pl.when(pair == 0)
    def _():
        cb_ref[...] = lax.dot_general(
            bmat,
            cmat,
            (((1,), (1,)), ((), ())),
            precision=lax.Precision.HIGHEST,
            preferred_element_type=jnp.float32,
        )
        dcb_ref[...] = jnp.zeros_like(dcb_ref)
        db_ref[...] = jnp.zeros_like(db_ref)
        dc_ref[...] = jnp.zeros_like(dc_ref)

    def one(at, lanes):
        g = g_ref[:, lanes]
        xs = xs_ref[:, lanes]
        skip = skip_ref[:, lanes]
        cols = cols_ref[at]
        rows = rows_ref[at]
        step = half_lanes(cols, 2, xs.shape)
        tail = half_lanes(cols, 6, xs.shape)
        lane = lax.broadcasted_iota(jnp.int32, xs.shape, 1)
        first = lane < SSM_HEAD
        g_low = g.astype(jnp.bfloat16)
        scaled = xs * step
        parts = []
        total = dcb_ref[...]
        for k in range(2):
            mine = first if k == 0 else jnp.logical_not(first)
            kernel = jnp.exp(rows[k : k + 1, :] - cols[:, k : k + 1] + bias_ref[...])
            parts.append(dot_nn((kernel * cb_ref[...]).astype(jnp.bfloat16), g_low))
            crossed = lax.dot_general(
                jnp.where(mine, scaled, 0.0).astype(jnp.bfloat16),
                g_low,
                (((1,), (1,)), ((), ())),
                preferred_element_type=jnp.float32,
            )
            total = total + crossed * kernel
        dcb_ref[...] = total
        later = later_ref[at]
        swept = tail * lax.dot_general(
            b_low, later, (((1,), (1,)), ((), ())), preferred_element_type=jnp.float32
        )
        inner = jnp.where(first, parts[0], parts[1]) + swept
        dxs_ref[:, lanes] = step * inner + skip * g
        db_ref[...] += dot_nn((scaled * tail).astype(jnp.bfloat16), later)
        entered = (g * half_lanes(cols, 4, g.shape)).astype(jnp.bfloat16)
        dc_ref[...] += dot_nn(entered, state_ref[at])
        rose = g_low.astype(jnp.float32) * (out_ref[:, lanes] - skip * xs)
        stepped = xs * inner
        kept = scaled.astype(jnp.bfloat16).astype(jnp.float32)
        fell = kept * (inner - swept) + scaled * swept
        columns = [
            jnp.sum(jnp.where(first, value, 0.0), axis=1, keepdims=True)
            if k == 0
            else jnp.sum(jnp.where(first, 0.0, value), axis=1, keepdims=True)
            for value in (rose, stepped, fell)
            for k in range(2)
        ]
        spot = lax.broadcasted_iota(jnp.int32, cols.shape, 1)
        packed = jnp.zeros_like(cols)
        for index, column in enumerate(columns):
            packed = jnp.where(spot == index, column, packed)
        dcols_ref[at] = packed
        drows_ref[at, 0:1, :] = jnp.sum(scaled * swept, axis=0, keepdims=True)
        drows_ref[at, 1:2, :] = jnp.sum(g * xs, axis=0, keepdims=True)

    each_pair(one)

    @pl.when(pair == pl.num_programs(0) - 1)
    def _():
        low = dcb_ref[...].astype(jnp.bfloat16)
        db_ref[...] += dot_nn(low, c_low)
        dc_ref[...] += lax.dot_general(
            low, b_low, (((0,), (0,)), ((), ())), preferred_element_type=jnp.float32
        )


def ssm_specs(rows):
    wide = PAIR_GROUP * LANES
    block = pl.BlockSpec((rows, wide), lambda p: (0, p))
    bmat = pl.BlockSpec((rows, LANES), lambda p: (0, SSM_PAIRS))
    cmat = pl.BlockSpec((rows, LANES), lambda p: (0, SSM_PAIRS + 1))
    cols = pl.BlockSpec((PAIR_GROUP, rows, 8), lambda p: (p, 0, 0))
    turned = pl.BlockSpec((PAIR_GROUP, 2, rows), lambda p: (p, 0, 0))
    bias = pl.BlockSpec((rows, rows), lambda p: (0, 0))
    state = pl.BlockSpec((PAIR_GROUP, LANES, STATE), lambda p: (p, 0, 0))
    skip = pl.BlockSpec((1, wide), lambda p: (0, p))
    whole = pl.BlockSpec((rows, LANES), lambda p: (0, 0))
    return block, bmat, cmat, cols, turned, bias, state, skip, whole


def ssm_state(act, cols):
    rows = act.shape[0]
    block, bmat, cmat, col, turn, square, state, skip, whole = ssm_specs(rows)
    return pl.pallas_call(
        ssm_state_kernel,
        grid=(SSM_PAIRS // PAIR_GROUP,),
        in_specs=[block, bmat, col],
        out_specs=state,
        out_shape=jax.ShapeDtypeStruct((SSM_PAIRS, LANES, STATE), jnp.float32),
        name="ssm_state",
        cost_estimate=pl.CostEstimate(flops=10**8, transcendentals=0, bytes_accessed=4 * 10**6),
    )(act, act, cols)


def ssm_local(act, cols, turned, bias):
    rows = act.shape[0]
    block, bmat, cmat, col, turn, square, state, skip, whole = ssm_specs(rows)
    return pl.pallas_call(
        ssm_local_kernel,
        grid=(SSM_PAIRS // PAIR_GROUP,),
        in_specs=[block, bmat, cmat, col, turn, square],
        out_specs=block,
        out_shape=jax.ShapeDtypeStruct((rows, SSM_PAIRS * LANES), jnp.float32),
        scratch_shapes=[pltpu.VMEM((rows, rows), jnp.float32)],
        name="ssm_local",
        cost_estimate=pl.CostEstimate(flops=10**9, transcendentals=24 * rows * rows, bytes_accessed=6 * 10**6),
    )(act, act, act, cols, turned, bias)


def ssm_carried(local_part, act, cols, state, skip_row, projected):
    rows = act.shape[0]
    block, bmat, cmat, col, turn, square, states, skip, whole = ssm_specs(rows)
    shape = jax.ShapeDtypeStruct((rows, SSM_PAIRS * LANES), jnp.float32)
    return pl.pallas_call(
        ssm_carry_kernel,
        grid=(SSM_PAIRS // PAIR_GROUP,),
        in_specs=[block, block, cmat, col, states, skip, block],
        out_specs=[block, block],
        out_shape=[shape, shape],
        name="ssm_carried",
        cost_estimate=pl.CostEstimate(flops=10**8, transcendentals=rows * 1536, bytes_accessed=9 * 10**6),
    )(local_part, act, act, cols, state, skip_row, projected)


def ssm_direct(g, act, cols):
    rows = act.shape[0]
    block, bmat, cmat, col, turn, square, states, skip, whole = ssm_specs(rows)
    return pl.pallas_call(
        ssm_direct_kernel,
        grid=(SSM_PAIRS // PAIR_GROUP,),
        in_specs=[block, cmat, col],
        out_specs=states,
        out_shape=jax.ShapeDtypeStruct((SSM_PAIRS, LANES, STATE), jnp.float32),
        name="ssm_direct",
        cost_estimate=pl.CostEstimate(flops=10**8, transcendentals=0, bytes_accessed=4 * 10**6),
    )(g, act, cols)


def ssm_backward(g, act, out, cols, turned, bias_turned, state, later, skip_row):
    rows = act.shape[0]
    block, bmat, cmat, col, turn, square, states, skip, whole = ssm_specs(rows)
    return pl.pallas_call(
        ssm_backward_kernel,
        grid=(SSM_PAIRS // PAIR_GROUP,),
        in_specs=[block, block, block, bmat, cmat, col, turn, square, states, states, skip],
        out_specs=[block, whole, whole, col, pl.BlockSpec((PAIR_GROUP, 2, LANES), lambda p: (p, 0, 0))],
        out_shape=[
            jax.ShapeDtypeStruct((rows, SSM_PAIRS * LANES), jnp.float32),
            jax.ShapeDtypeStruct((rows, STATE), jnp.float32),
            jax.ShapeDtypeStruct((rows, STATE), jnp.float32),
            jax.ShapeDtypeStruct((SSM_PAIRS, rows, 8), jnp.float32),
            jax.ShapeDtypeStruct((SSM_PAIRS, 2, LANES), jnp.float32),
        ],
        scratch_shapes=[pltpu.VMEM((rows, rows), jnp.float32)] * 2,
        name="ssm_backward",
        cost_estimate=pl.CostEstimate(flops=2 * 10**9, transcendentals=24 * rows * rows, bytes_accessed=12 * 10**6),
    )(g, act, out, act, act, cols, turned, bias_turned, state, later, skip_row)


def outer_kernel(split, left_a_ref, right_a_ref, left_b_ref, right_b_ref, *rest):
    outs, turned_ref = rest[:-1], rest[-1]
    step = pl.program_id(0)

    @pl.when(step == 0)
    def _():
        turned_ref[...] = left_a_ref[...].T

    @pl.when(step == split)
    def _():
        turned_ref[...] = left_b_ref[...].T

    def filled(right_ref):
        wide = right_ref.shape[1]
        piece = math.gcd(wide, 256)
        for at in range(0, wide, piece):
            lanes = pl.ds(at, piece)
            product = dot_nn(turned_ref[...], right_ref[:, lanes]).astype(jnp.bfloat16)
            for place, out_ref in enumerate(outs):
                tall = out_ref.shape[0]
                out_ref[:, lanes] = product[place * tall : (place + 1) * tall]

    @pl.when(step < split)
    def _():
        filled(right_a_ref)

    @pl.when(step >= split)
    def _():
        filled(right_b_ref)


def outer_pair(left_a, right_a, left_b, right_b, outputs=1):
    rows, width = left_a.shape
    wide_a = right_a.shape[1]
    wide_b = right_b.shape[1]
    wide = math.gcd(math.gcd(wide_a, wide_b), 1024)
    split = wide_a // wide
    total = split + wide_b // wide
    held = pl.BlockSpec((rows, width), lambda j: (0, 0))
    return pl.pallas_call(
        functools.partial(outer_kernel, split),
        grid=(total,),
        in_specs=[
            held,
            pl.BlockSpec((rows, wide), lambda j: (0, jnp.minimum(j, split - 1))),
            held,
            pl.BlockSpec((rows, wide), lambda j: (0, jnp.maximum(j - split, 0))),
        ],
        out_specs=[pl.BlockSpec((width // outputs, wide), lambda j: (0, j))] * outputs,
        out_shape=[jax.ShapeDtypeStruct((width // outputs, wide_a + wide_b), jnp.bfloat16)]
        * outputs,
        scratch_shapes=[pltpu.VMEM((width, rows), jnp.bfloat16)],
        name="outer_pair",
        cost_estimate=pl.CostEstimate(
            flops=2 * rows * width * (wide_a + wide_b),
            transcendentals=0,
            bytes_accessed=2 * width * (wide_a + wide_b),
        ),
    )(left_a, right_a, left_b, right_b)


def local(
    block_in,
    segment_ids,
    mamba_z,
    mamba_x,
    mamba_bc,
    mamba_dt,
    mamba_out,
    attn_q,
    attn_kv,
    attn_out,
    ffn_gate,
    ffn_up,
    ffn_down,
    mixer_norm,
    ffn_norm,
    conv_weight,
    conv_bias,
    dt_bias,
    a_log,
    d_skip,
    inner_norm,
    grad_out,
):
    sequences, rows, width = block_in.shape
    length = segment_ids.shape[1]
    taps = conv_weight.shape[0]
    group = Q_HEADS // KV_HEADS
    inner_width = SSM_HEADS * SSM_HEAD
    total_rows = sequences * rows
    inv_root = HEAD ** (-0.5)
    offset = lax.axis_index("seq") * rows
    positions = offset + jnp.arange(rows, dtype=jnp.int32)
    local_ids = lax.dynamic_slice_in_dim(segment_ids, offset, rows, 1)
    padded_ids = jnp.concatenate(
        [jnp.full((sequences, taps - 1), -1, jnp.int32), segment_ids], axis=1
    )
    window_ids = lax.dynamic_slice_in_dim(padded_ids, offset, rows + taps - 1, 1)
    prior_id = window_ids[:, taps - 2]
    tap_masks = [
        (window_ids[:, tap : tap + rows] == local_ids).astype(jnp.float32)[:, :, None]
        for tap in range(taps)
    ]
    cosine, sine = rope_tables(positions, HEAD)
    cos_b = cosine[:, None, :]
    sin_b = sine[:, None, :]
    behind = min(lax.axis_size("seq") - 1, (MAX_DOC - 2) // rows + 1) * rows
    key_ids = lax.dynamic_slice_in_dim(
        jnp.concatenate([jnp.full((sequences, behind), -1, jnp.int32), segment_ids], axis=1),
        offset,
        behind + rows,
        1,
    )
    key_order = jnp.arange(behind + rows, dtype=jnp.int32) - behind
    allowed = (key_order[None, None, :] <= jnp.arange(rows, dtype=jnp.int32)[None, :, None]) & (
        key_ids[:, None, :] == local_ids[:, :, None]
    )
    hops = min(lax.axis_size("seq") - 1, (MAX_DOC - 2) // rows + 1)
    spare = -(mamba_dt.shape[1] + 2) % LANES
    shard_in = jnp.concatenate(
        [
            mamba_z,
            attn_q,
            mamba_x,
            mamba_bc,
            attn_kv,
            mamba_dt,
            mixer_norm[:, None],
            ffn_norm[:, None],
            jnp.zeros((mixer_norm.shape[0], spare), jnp.bfloat16),
        ],
        axis=1,
    )
    shard_out = jnp.concatenate([mamba_out, attn_out, ffn_gate, ffn_up, ffn_down], axis=1)
    held_in, shard_out = lax.optimization_barrier((gathered_seq(shard_in), shard_out))
    full_in = lax.all_gather(held_in, ("dpo", "core"), axis=0, tiled=True)
    full_out = lax.all_gather(gathered_seq(shard_out), ("dpo", "core"), axis=0, tiled=True)
    bc_width = mamba_bc.shape[1]
    q_width = attn_q.shape[1]
    kv_width = attn_kv.shape[1]
    hidden_width = ffn_gate.shape[1]
    at_q = inner_width
    at_u = at_q + q_width
    at_kv = at_u + inner_width + bc_width
    at_dt = at_kv + kv_width
    at_gain = at_dt + SSM_HEADS
    mixer_width = inner_width + q_width
    full_mixer = full_out[:, :mixer_width]
    full_gateup = full_out[:, mixer_width : mixer_width + 2 * hidden_width]
    full_down = full_out[:, mixer_width + 2 * hidden_width :]
    gain_one = full_in[:, at_gain].astype(jnp.float32)
    gain_two = full_in[:, at_gain + 1].astype(jnp.float32)
    x_in = block_in.reshape(total_rows, width).astype(jnp.float32)
    normed, factor_one = rms_forward(x_in, gain_one)
    normed_b = normed.astype(jnp.bfloat16)
    projected = matmul(normed_b, full_in)
    gate_z = projected[:, :at_q]
    inner_u = projected[:, at_u:at_kv]
    step_raw = projected[:, at_dt:at_gain]
    channels = inner_u.shape[1]
    conv_in = inner_u.reshape(sequences, rows, channels)
    edge_in = passed_along(conv_in[:, rows - taps + 1 :, :], "seq", 1)
    extended = jnp.concatenate([edge_in, conv_in], axis=1)
    conv_pre = jnp.zeros_like(conv_in) + conv_bias
    for tap in range(taps):
        conv_pre = conv_pre + conv_weight[tap] * extended[:, tap : tap + rows] * tap_masks[tap]
    activated = jax.nn.silu(conv_pre)
    act = activated.reshape(total_rows, channels)
    step = jax.nn.softplus(step_raw + dt_bias)
    ids = local_ids.reshape(total_rows)
    order = jnp.arange(rows)
    pair = (order[:, None] >= order[None, :]) & (ids[:, None] == ids[None, :])
    bias = jnp.where(pair, 0.0, -1e30).astype(jnp.float32)
    bias_turned = jnp.where(
        (order[:, None] <= order[None, :]) & (ids[:, None] == ids[None, :]), 0.0, -1e30
    ).astype(jnp.float32)
    inbound = (ids == prior_id[0]).astype(jnp.float32)[:, None]
    outbound = (ids == ids[-1]).astype(jnp.float32)[:, None]
    rate = -jnp.exp(a_log)
    ladder = (order[:, None] >= order[None, :]).astype(jnp.float32)
    decay = jnp.dot(ladder, step * rate, precision=lax.Precision.HIGHEST)
    entry = jnp.exp(decay) * inbound
    tail = jnp.exp(decay[-1:] - decay) * outbound
    carry = jnp.exp(decay[-1]) * inbound[-1, 0]
    cols = jnp.stack([decay, step, entry, tail], axis=1)
    cols = cols.reshape(rows, 4, SSM_PAIRS, 2).transpose(2, 0, 1, 3).reshape(SSM_PAIRS, rows, 8)
    turned = decay.T.reshape(SSM_PAIRS, 2, rows)
    skip_row = jnp.repeat(d_skip, SSM_HEAD)[None, :]
    carry_rows = jnp.repeat(carry, SSM_HEAD).reshape(SSM_PAIRS, LANES, 1)
    state_local = ssm_state(act, cols)
    outgoing = state_local
    for hop in range(hops):
        incoming = passed_along(outgoing.astype(jnp.bfloat16), "seq", 1)
        outgoing = carry_rows * incoming.astype(jnp.float32) + state_local
    local_part = ssm_local(act, cols, turned, bias)
    ssm_out, gated = ssm_carried(local_part, act, cols, incoming, skip_row, projected)
    silu_z = jax.nn.silu(gate_z)
    mixed_norm, factor_m = rms_forward(gated, inner_norm)
    mixed_b = mixed_norm.astype(jnp.bfloat16)
    query = projected[:, at_q:at_u].reshape(sequences, rows, Q_HEADS, HEAD)
    keyval = projected[:, at_kv:at_dt].reshape(sequences, rows, 2 * KV_HEADS, HEAD)
    query_b = rotate(query, cos_b, sin_b).astype(jnp.bfloat16)
    keys_local = rotate(keyval[:, :, :KV_HEADS], cos_b, sin_b)
    kv_local = jnp.concatenate([keys_local, keyval[:, :, KV_HEADS:]], axis=2).astype(jnp.bfloat16)
    kv_flat = kv_local.reshape(sequences, rows, kv_width)
    kv_all = jnp.concatenate(
        [passed_along(kv_flat, "seq", far) for far in range(hops, 0, -1)] + [kv_flat], axis=1
    )
    window = kv_all.shape[1]
    kv_all = kv_all.reshape(sequences, window, 2 * KV_HEADS, HEAD)
    keys = kv_all[:, :, :KV_HEADS]
    values = kv_all[:, :, KV_HEADS:]
    query_g = query_b.reshape(sequences, rows, KV_HEADS, group, HEAD)

    def attention_scores():
        raw = (
            jnp.einsum("stkgd,slkd->skgtl", query_g, keys, preferred_element_type=jnp.float32)
            * inv_root
        )
        return jnp.where(allowed[:, None, None], raw, -1e30)

    scores = attention_scores()
    top = jnp.max(scores, axis=-1, keepdims=True)
    lse = top + jnp.log(jnp.sum(jnp.exp(scores - top), axis=-1, keepdims=True))
    probs_b = jnp.exp(scores - lse).astype(jnp.bfloat16)
    attended = jnp.einsum("skgtl,slkd->stkgd", probs_b, values, preferred_element_type=jnp.float32)
    attended_b = attended.reshape(total_rows, Q_HEADS * HEAD).astype(jnp.bfloat16)
    mixers_b = jnp.concatenate([mixed_b, attended_b], axis=1)
    mid = x_in + matmul_nt(mixers_b, full_mixer)
    fnormed, factor_two = rms_forward(mid, gain_two)
    fnormed_b = fnormed.astype(jnp.bfloat16)
    gateup_h = matmul(fnormed_b, full_gateup)
    gate_h = gateup_h[:, :hidden_width]
    up_h = gateup_h[:, hidden_width:]
    hidden_b = (jax.nn.silu(gate_h) * up_h).astype(jnp.bfloat16)
    block_out = (
        (mid + matmul_nt(hidden_b, full_down)).astype(jnp.bfloat16).reshape(sequences, rows, width)
    )
    grad_flat = grad_out.reshape(total_rows, width)
    d_hidden = matmul(grad_flat, full_down)
    d_gate_b = (d_hidden * up_h * silu_grad(gate_h)).astype(jnp.bfloat16)
    d_up_b = (d_hidden * jax.nn.silu(gate_h)).astype(jnp.bfloat16)
    d_gateup_b = jnp.concatenate([d_gate_b, d_up_b], axis=1)
    part_ffn = scattered_dp(outer_pair(fnormed_b, d_gateup_b, grad_flat, hidden_b)[0])
    d_fnorm = matmul_nt(d_gateup_b, full_gateup)
    d_mid_norm, g_fnorm = rms_backward(mid, factor_two, gain_two, d_fnorm)
    d_mid = grad_flat.astype(jnp.float32) + d_mid_norm
    d_mid_b = d_mid.astype(jnp.bfloat16)
    d_mixers = matmul(d_mid_b, full_mixer)
    d_mnorm = d_mixers[:, :inner_width]
    d_gated, g_inner = rms_backward(gated, factor_m, inner_norm, d_mnorm)
    d_ssm = d_gated * silu_z
    d_z = d_gated * ssm_out * silu_grad(gate_z)
    direct = ssm_direct(d_ssm, act, cols)
    backlog = direct
    for hop in range(hops):
        later_grad = passed_along(backlog.astype(jnp.bfloat16), "seq", -1)
        backlog = direct + carry_rows * later_grad.astype(jnp.float32)
    d_carry = jnp.sum(
        (later_grad.astype(jnp.float32) * incoming.astype(jnp.float32)).reshape(
            SSM_HEADS, SSM_HEAD, STATE
        ),
        axis=(1, 2),
    )
    d_att_b = d_mixers[:, inner_width:].astype(jnp.bfloat16)
    d_att_g = d_att_b.reshape(sequences, rows, KV_HEADS, group, HEAD)
    probs = jnp.exp(attention_scores() - lse)
    d_probs = jnp.einsum("stkgd,slkd->skgtl", d_att_g, values, preferred_element_type=jnp.float32)
    d_scores_b = (probs * (d_probs - jnp.sum(probs * d_probs, axis=-1, keepdims=True))).astype(
        jnp.bfloat16
    )
    d_query = (
        jnp.einsum("skgtl,slkd->stkgd", d_scores_b, keys, preferred_element_type=jnp.float32)
        * inv_root
    )
    d_keys = (
        jnp.einsum("skgtl,stkgd->slkd", d_scores_b, query_g, preferred_element_type=jnp.float32)
        * inv_root
    )
    d_values = jnp.einsum("skgtl,stkgd->slkd", probs_b, d_att_g, preferred_element_type=jnp.float32)
    d_kv_all = jnp.concatenate([d_keys, d_values], axis=2).reshape(sequences, window, kv_width)
    d_kv_local = d_kv_all[:, window - rows :]
    for far in range(1, hops + 1):
        start = window - (far + 1) * rows
        term = d_kv_all[:, start : start + rows].astype(jnp.bfloat16)
        d_kv_local = d_kv_local + passed_along(term, "seq", -far).astype(jnp.float32)
    d_kv_local = d_kv_local.reshape(sequences, rows, 2 * KV_HEADS, HEAD)
    d_key_local = rotate_back(d_kv_local[:, :, :KV_HEADS], cos_b, sin_b)
    d_kv_b = (
        jnp.concatenate([d_key_local, d_kv_local[:, :, KV_HEADS:]], axis=2)
        .reshape(total_rows, 2 * KV_HEADS * HEAD)
        .astype(jnp.bfloat16)
    )
    d_q_b = (
        rotate_back(d_query.reshape(sequences, rows, Q_HEADS, HEAD), cos_b, sin_b)
        .reshape(total_rows, Q_HEADS * HEAD)
        .astype(jnp.bfloat16)
    )
    d_early = jnp.concatenate([d_z.astype(jnp.bfloat16), d_q_b], axis=1)
    normed_own, normed_other = split_by_core(normed_b)
    d_mid_own, d_mid_other = split_by_core(d_mid_b)
    early_own, early_other = outer_pair(
        jnp.concatenate([normed_own, normed_other], axis=1),
        d_early,
        jnp.concatenate([d_mid_own, d_mid_other], axis=1),
        mixers_b,
        2,
    )
    later_grad, early_own, early_other = lax.optimization_barrier(
        (later_grad, early_own, early_other)
    )
    part_early = scattered_own(paired_cores(early_own, early_other))
    d_xs, d_bmat, d_cmat, d_cols, d_rows = ssm_backward(
        d_ssm, act, ssm_out, cols, turned, bias_turned, incoming, later_grad, skip_row
    )
    d_pairs = d_cols[:, :, :6].reshape(SSM_PAIRS, rows, 3, 2).transpose(2, 1, 0, 3)
    d_pairs = d_pairs.reshape(3, rows, SSM_HEADS)
    d_sums = jnp.sum(d_rows.reshape(SSM_PAIRS, 2, 2, SSM_HEAD), axis=3).transpose(1, 0, 2)
    d_sums = d_sums.reshape(2, SSM_HEADS)
    g_skip = d_sums[1]
    d_decay = d_pairs[0] - d_pairs[2]
    d_rise = jnp.dot(ladder.T, d_decay, precision=lax.Precision.HIGHEST)
    d_rise = d_rise + (d_sums[0] + d_carry * carry)
    d_step = d_pairs[1] + d_rise * rate
    g_alog = jnp.sum(d_rise * step, axis=0) * rate
    d_act = jnp.concatenate([d_xs, d_bmat, d_cmat], axis=1).reshape(sequences, rows, channels)
    d_act, part_ffn = lax.optimization_barrier((d_act, part_ffn))
    owned_ffn, _ = hopped_seq(part_ffn, None)
    d_pre = d_act * silu_grad(conv_pre)
    g_cbias = jnp.sum(d_pre, axis=(0, 1))
    g_cweight = jnp.stack(
        [
            jnp.sum(d_pre * extended[:, tap : tap + rows] * tap_masks[tap], axis=(0, 1))
            for tap in range(taps)
        ]
    )
    d_padded = jnp.zeros_like(extended)
    for tap in range(taps):
        d_padded = d_padded + jnp.pad(
            d_pre * tap_masks[tap] * conv_weight[tap], ((0, 0), (tap, taps - 1 - tap), (0, 0))
        )
    edge_grad = passed_along(d_padded[:, : taps - 1], "seq", -1)
    d_inner = d_padded[:, taps - 1 :] + jnp.pad(edge_grad, ((0, 0), (rows - taps + 1, 0), (0, 0)))
    d_inner = d_inner.reshape(total_rows, channels)
    d_step_raw = d_step.reshape(total_rows, SSM_HEADS) * jax.nn.sigmoid(step_raw + dt_bias)
    g_dtb = jnp.sum(d_step_raw, axis=0)
    d_x_b = d_inner[:, :inner_width].astype(jnp.bfloat16)
    d_bc_b = d_inner[:, inner_width:].astype(jnp.bfloat16)
    d_st_b = d_step_raw.astype(jnp.bfloat16)
    d_late = jnp.concatenate(
        [
            d_x_b,
            d_bc_b,
            d_kv_b,
            d_st_b,
            jnp.zeros((total_rows, spare + 2), jnp.bfloat16),
        ],
        axis=1,
    )
    late_pair = paired_cores(
        matmul_tn(normed_own, d_late).astype(jnp.bfloat16),
        matmul_tn(normed_other, d_late).astype(jnp.bfloat16),
    )
    d_norm = matmul_nt(d_early, full_in[:, :at_u]) + matmul_nt(d_late, full_in[:, at_u:])
    d_in_norm, g_mnorm = rms_backward(x_in, factor_one, gain_one, d_norm)
    grad_in = (d_mid + d_in_norm).astype(jnp.bfloat16).reshape(sequences, rows, width)
    smalls = jnp.concatenate([g_dtb, g_alog, g_skip])
    strips = [g_inner, g_mnorm, g_fnorm, smalls]
    packed = jnp.concatenate(
        [g_cweight, g_cbias[None]]
        + [jnp.pad(strip, (0, channels - strip.shape[0]))[None] for strip in strips],
        axis=0,
    )
    packed, late_pair = lax.optimization_barrier((packed, late_pair))
    part_late = scattered_own(late_pair)
    summed = summed_everywhere(packed)
    gain_rows = mixer_norm.shape[0]
    part_early, summed, grad_in = lax.optimization_barrier((part_early, summed, grad_in))
    owned_early, part_late = hopped_seq(part_early, part_late)
    owned_late = scattered_seq(part_late)
    owner = lax.axis_index("dpo") * 2 + lax.axis_index("core")
    first_row = (owner * lax.axis_size("seq") + lax.axis_index("seq")) * gain_rows
    g_mnorm_own = lax.dynamic_slice_in_dim(summed[taps + 2], first_row, gain_rows, 0)
    g_fnorm_own = lax.dynamic_slice_in_dim(summed[taps + 3], first_row, gain_rows, 0)
    at_mixers = at_u
    late_kv = at_kv - at_u
    late_dt = at_dt - at_u
    return (
        block_out,
        grad_in,
        owned_early[:, :at_q],
        owned_late[:, :inner_width],
        owned_late[:, inner_width:late_kv],
        owned_late[:, late_dt : late_dt + SSM_HEADS],
        owned_early[:, at_mixers : at_mixers + inner_width],
        owned_early[:, at_q:at_u],
        owned_late[:, late_kv:late_dt],
        owned_early[:, at_mixers + inner_width :],
        owned_ffn[:, :hidden_width],
        owned_ffn[:, hidden_width : 2 * hidden_width],
        owned_ffn[:, 2 * hidden_width :],
        g_mnorm_own,
        g_fnorm_own,
        summed[:taps],
        summed[taps],
        summed[taps + 4, :SSM_HEADS],
        summed[taps + 4, SSM_HEADS : 2 * SSM_HEADS],
        summed[taps + 4, 2 * SSM_HEADS : 3 * SSM_HEADS],
        summed[taps + 1, :inner_width],
    )


def solution(mesh):
    grid = mesh.devices
    mesh = Mesh(grid.reshape(grid.shape[0] // 2, 2, grid.shape[1]), DP + ("seq",))
    in_specs = (
        P(DP, "seq", None),
        P(DP, None),
        P(DP + ("seq",), None),
        P(DP + ("seq",), None),
        P(DP + ("seq",), None),
        P(DP + ("seq",), None),
        P(DP + ("seq",), None),
        P(DP + ("seq",), None),
        P(DP + ("seq",), None),
        P(DP + ("seq",), None),
        P(DP + ("seq",), None),
        P(DP + ("seq",), None),
        P(DP + ("seq",), None),
        P(DP + ("seq",)),
        P(DP + ("seq",)),
        P(),
        P(),
        P(),
        P(),
        P(),
        P(),
        P(DP, "seq", None),
    )
    out_specs = (
        P(DP, "seq", None),
        P(DP, "seq", None),
        P(DP + ("seq",), None),
        P(DP + ("seq",), None),
        P(DP + ("seq",), None),
        P(DP + ("seq",), None),
        P(DP + ("seq",), None),
        P(DP + ("seq",), None),
        P(DP + ("seq",), None),
        P(DP + ("seq",), None),
        P(DP + ("seq",), None),
        P(DP + ("seq",), None),
        P(DP + ("seq",), None),
        P(DP + ("seq",)),
        P(DP + ("seq",)),
        P(),
        P(),
        P(),
        P(),
        P(),
        P(),
    )
    return jax.shard_map(local, mesh=mesh, in_specs=in_specs, out_specs=out_specs, check_vma=False)
```

```python
import functools
import math

import jax
import jax.numpy as jnp
from jax import lax
from jax.experimental import pallas as pl
from jax.experimental.pallas import tpu as pltpu
from jax.sharding import Mesh
from jax.sharding import PartitionSpec as P

SSM_HEADS = 24
SSM_HEAD = 64
STATE = 128
Q_HEADS = 8
KV_HEADS = 2
HEAD = 64


EPSILON = 1e-05
ROPE_BASE = 100000000000.0
MAX_DOC = 512
LANES = 128
SSM_PAIRS = SSM_HEADS * SSM_HEAD // LANES
PAIR_GROUP = 4
DP = ("dpo", "core")


def passed_along(block, axis, distance):
    devices = range(lax.axis_size(axis))
    route = [(i - distance, i) for i in devices if i - distance in devices]
    return lax.ppermute(block, axis, route)


def scattered_dp(grad):
    return lax.psum_scatter(grad, ("dpo", "core"), scatter_dimension=0, tiled=True)


def swapped(block):
    return lax.ppermute(block, "core", [(0, 1), (1, 0)])


def paired_cores(own, other):
    return (own.astype(jnp.float32) + swapped(other).astype(jnp.float32)).astype(jnp.bfloat16)


def scattered_own(paired):
    return lax.psum_scatter(paired, "dpo", scatter_dimension=0, tiled=True)


def summed_everywhere(block):
    for axis in ("core", "dpo", "seq"):
        count = lax.axis_size(axis)
        bit = 1
        while bit < count:
            block = block + lax.ppermute(block, axis, [(i, i ^ bit) for i in range(count)])
            bit *= 2
    return block


def scattered_seq(part):
    return lax.psum_scatter(part, "seq", scatter_dimension=0, tiled=True).astype(jnp.float32)


def gathered_seq(shard):
    index = lax.axis_index("seq")
    count = lax.axis_size("seq")
    held = shard
    bit = 1
    while bit < count:
        got = lax.ppermute(held, "seq", [(i, i ^ bit) for i in range(count)])
        odd = (index // bit) % 2 == 1
        held = jnp.concatenate([jnp.where(odd, got, held), jnp.where(odd, held, got)], axis=0)
        bit *= 2
    return held


def chained_seq(shard):
    count = lax.axis_size("seq")
    before = [shard]
    after = [shard]
    for hop in range(count - 1):
        before.append(passed_along(before[-1], "seq", 1))
        after.append(passed_along(after[-1], "seq", -1))
    line = jnp.concatenate(before[:0:-1] + after, axis=0)
    rows = shard.shape[0]
    start = (count - 1 - lax.axis_index("seq")) * rows
    return lax.dynamic_slice_in_dim(line, start, count * rows, 0)


def hopped_seq(part, rider):
    index = lax.axis_index("seq")
    count = lax.axis_size("seq")
    held = part.reshape(count, part.shape[0] // count, part.shape[1])
    bit = 1
    while bit < count:
        halves = held.reshape(held.shape[0] // 2, 2, *held.shape[1:])
        odd = (index // bit) % 2 == 1
        mine = jnp.where(odd, halves[:, 1], halves[:, 0])
        other = jnp.where(odd, halves[:, 0], halves[:, 1])
        got = lax.ppermute(other, "seq", [(i, i ^ bit) for i in range(count)])
        held = mine.astype(jnp.float32) + got.astype(jnp.float32)
        bit *= 2
        if bit < count:
            held = held.astype(jnp.bfloat16)
        if bit == 2 and rider is not None:
            held, rider = lax.optimization_barrier((held, rider))
    return held[0].astype(jnp.float32), rider


def silu_grad(value):
    sigma = jax.nn.sigmoid(value)
    return sigma * (1.0 + value * (1.0 - sigma))


def rms_forward(value, gain):
    factor = lax.rsqrt(jnp.mean(value * value, axis=-1, keepdims=True) + EPSILON)
    return (value * factor * gain, factor)


def rms_backward(value, factor, gain, upstream):
    weighted = upstream * gain
    gain_grad = jnp.sum(upstream * value * factor, axis=0)
    inward = factor * weighted - value * factor * factor * factor * jnp.mean(
        weighted * value, axis=-1, keepdims=True
    )
    return (inward, gain_grad)


def matmul(left, right):
    return jnp.dot(left, right, preferred_element_type=jnp.float32)


def matmul_nt(left, right):
    return lax.dot_general(
        left, right, (((1,), (1,)), ((), ())), preferred_element_type=jnp.float32
    )


def matmul_tn(left, right):
    return lax.dot_general(
        left, right, (((0,), (0,)), ((), ())), preferred_element_type=jnp.float32
    )


def rope_tables(positions, head_size):
    half = head_size // 2
    freq_scale = ROPE_BASE ** (-jnp.arange(half, dtype=jnp.float32) / half)
    angles = positions.astype(jnp.float32)[:, None] * freq_scale[None, :]
    return (jnp.cos(angles), jnp.sin(angles))


def rotate(value, cosine, sine):
    half = value.shape[-1] // 2
    first = value[..., :half]
    second = value[..., half:]
    return jnp.concatenate(
        [first * cosine - second * sine, second * cosine + first * sine], axis=-1
    )


def rotate_back(grad, cosine, sine):
    half = grad.shape[-1] // 2
    first = grad[..., :half]
    second = grad[..., half:]
    return jnp.concatenate(
        [first * cosine + second * sine, second * cosine - first * sine], axis=-1
    )


def half_lanes(cols, first, shape):
    lane = lax.broadcasted_iota(jnp.int32, shape, 1)
    return jnp.where(lane < SSM_HEAD, cols[:, first : first + 1], cols[:, first + 1 : first + 2])


def dot_nn(left, right):
    return lax.dot_general(
        left, right, (((1,), (0,)), ((), ())), preferred_element_type=jnp.float32
    )


def each_pair(body):
    def turn(k, carry):
        body(k, pl.ds(pl.multiple_of(k * LANES, LANES), LANES))
        return carry

    lax.fori_loop(0, PAIR_GROUP, turn, 0)


def ssm_state_kernel(xs_ref, b_ref, cols_ref, state_ref):
    b_low = b_ref[...].astype(jnp.bfloat16)

    def one(k, lanes):
        xs = xs_ref[:, lanes]
        cols = cols_ref[k]
        scaled = xs * half_lanes(cols, 2, xs.shape)
        tailed = (scaled * half_lanes(cols, 6, xs.shape)).astype(jnp.bfloat16)
        state_ref[k] = lax.dot_general(
            tailed, b_low, (((0,), (0,)), ((), ())), preferred_element_type=jnp.float32
        )

    each_pair(one)


def ssm_local_kernel(xs_ref, b_ref, c_ref, cols_ref, rows_ref, bias_ref, out_ref, cb_ref):
    bmat = b_ref[...]

    @pl.when(pl.program_id(0) == 0)
    def _():
        cb_ref[...] = lax.dot_general(
            c_ref[...],
            bmat,
            (((1,), (1,)), ((), ())),
            precision=lax.Precision.HIGHEST,
            preferred_element_type=jnp.float32,
        )

    def one(k, lanes):
        xs = xs_ref[:, lanes]
        cols = cols_ref[k]
        rows = rows_ref[k]
        scaled_b = (xs * half_lanes(cols, 2, xs.shape)).astype(jnp.bfloat16)
        parts = []
        for h in range(2):
            kernel = jnp.exp(cols[:, h : h + 1] - rows[h : h + 1, :] + bias_ref[...])
            parts.append(dot_nn((kernel * cb_ref[...]).astype(jnp.bfloat16), scaled_b))
        lane = lax.broadcasted_iota(jnp.int32, xs.shape, 1)
        out_ref[:, lanes] = jnp.where(lane < SSM_HEAD, parts[0], parts[1])

    each_pair(one)


def ssm_carry_kernel(local_ref, xs_ref, c_ref, cols_ref, state_ref, skip_ref, z_ref, out_ref, gated_ref):
    c_low = c_ref[...].astype(jnp.bfloat16)

    def one(k, lanes):
        xs = xs_ref[:, lanes]
        carried = lax.dot_general(
            c_low, state_ref[k], (((1,), (1,)), ((), ())), preferred_element_type=jnp.float32
        )
        entry = half_lanes(cols_ref[k], 4, xs.shape)
        out = local_ref[:, lanes] + entry * carried + skip_ref[:, lanes] * xs
        out_ref[:, lanes] = out
        gate = z_ref[:, lanes]
        gated_ref[:, lanes] = out * (gate * jax.nn.sigmoid(gate))

    each_pair(one)


def ssm_direct_kernel(g_ref, c_ref, cols_ref, direct_ref):
    c_low = c_ref[...].astype(jnp.bfloat16)

    def one(k, lanes):
        g = g_ref[:, lanes]
        entered = (g * half_lanes(cols_ref[k], 4, g.shape)).astype(jnp.bfloat16)
        direct_ref[k] = lax.dot_general(
            entered, c_low, (((0,), (0,)), ((), ())), preferred_element_type=jnp.float32
        )

    each_pair(one)


def ssm_backward_kernel(
    g_ref,
    xs_ref,
    out_ref,
    b_ref,
    c_ref,
    cols_ref,
    rows_ref,
    bias_ref,
    state_ref,
    later_ref,
    skip_ref,
    dxs_ref,
    db_ref,
    dc_ref,
    dcols_ref,
    drows_ref,
    cb_ref,
    dcb_ref,
):
    pair = pl.program_id(0)
    bmat = b_ref[...]
    cmat = c_ref[...]
    b_low = bmat.astype(jnp.bfloat16)
    c_low = cmat.astype(jnp.bfloat16)

    @pl.when(pair == 0)
    def _():
        cb_ref[...] = lax.dot_general(
            bmat,
            cmat,
            (((1,), (1,)), ((), ())),
            precision=lax.Precision.HIGHEST,
            preferred_element_type=jnp.float32,
        )
        dcb_ref[...] = jnp.zeros_like(dcb_ref)
        db_ref[...] = jnp.zeros_like(db_ref)
        dc_ref[...] = jnp.zeros_like(dc_ref)

    def one(at, lanes):
        g = g_ref[:, lanes]
        xs = xs_ref[:, lanes]
        skip = skip_ref[:, lanes]
        cols = cols_ref[at]
        rows = rows_ref[at]
        step = half_lanes(cols, 2, xs.shape)
        tail = half_lanes(cols, 6, xs.shape)
        lane = lax.broadcasted_iota(jnp.int32, xs.shape, 1)
        first = lane < SSM_HEAD
        g_low = g.astype(jnp.bfloat16)
        scaled = xs * step
        parts = []
        total = dcb_ref[...]
        for k in range(2):
            mine = first if k == 0 else jnp.logical_not(first)
            kernel = jnp.exp(rows[k : k + 1, :] - cols[:, k : k + 1] + bias_ref[...])
            parts.append(dot_nn((kernel * cb_ref[...]).astype(jnp.bfloat16), g_low))
            crossed = lax.dot_general(
                jnp.where(mine, scaled, 0.0).astype(jnp.bfloat16),
                g_low,
                (((1,), (1,)), ((), ())),
                preferred_element_type=jnp.float32,
            )
            total = total + crossed * kernel
        dcb_ref[...] = total
        later = later_ref[at]
        swept = tail * lax.dot_general(
            b_low, later, (((1,), (1,)), ((), ())), preferred_element_type=jnp.float32
        )
        inner = jnp.where(first, parts[0], parts[1]) + swept
        dxs_ref[:, lanes] = step * inner + skip * g
        db_ref[...] += dot_nn((scaled * tail).astype(jnp.bfloat16), later)
        entered = (g * half_lanes(cols, 4, g.shape)).astype(jnp.bfloat16)
        dc_ref[...] += dot_nn(entered, state_ref[at])
        rose = g_low.astype(jnp.float32) * (out_ref[:, lanes] - skip * xs)
        stepped = xs * inner
        kept = scaled.astype(jnp.bfloat16).astype(jnp.float32)
        fell = kept * (inner - swept) + scaled * swept
        columns = [
            jnp.sum(jnp.where(first, value, 0.0), axis=1, keepdims=True)
            if k == 0
            else jnp.sum(jnp.where(first, 0.0, value), axis=1, keepdims=True)
            for value in (rose, stepped, fell)
            for k in range(2)
        ]
        spot = lax.broadcasted_iota(jnp.int32, cols.shape, 1)
        packed = jnp.zeros_like(cols)
        for index, column in enumerate(columns):
            packed = jnp.where(spot == index, column, packed)
        dcols_ref[at] = packed
        drows_ref[at, 0:1, :] = jnp.sum(scaled * swept, axis=0, keepdims=True)
        drows_ref[at, 1:2, :] = jnp.sum(g * xs, axis=0, keepdims=True)

    each_pair(one)

    @pl.when(pair == pl.num_programs(0) - 1)
    def _():
        low = dcb_ref[...].astype(jnp.bfloat16)
        db_ref[...] += dot_nn(low, c_low)
        dc_ref[...] += lax.dot_general(
            low, b_low, (((0,), (0,)), ((), ())), preferred_element_type=jnp.float32
        )


def ssm_specs(rows):
    wide = PAIR_GROUP * LANES
    block = pl.BlockSpec((rows, wide), lambda p: (0, p))
    bmat = pl.BlockSpec((rows, LANES), lambda p: (0, SSM_PAIRS))
    cmat = pl.BlockSpec((rows, LANES), lambda p: (0, SSM_PAIRS + 1))
    cols = pl.BlockSpec((PAIR_GROUP, rows, 8), lambda p: (p, 0, 0))
    turned = pl.BlockSpec((PAIR_GROUP, 2, rows), lambda p: (p, 0, 0))
    bias = pl.BlockSpec((rows, rows), lambda p: (0, 0))
    state = pl.BlockSpec((PAIR_GROUP, LANES, STATE), lambda p: (p, 0, 0))
    skip = pl.BlockSpec((1, wide), lambda p: (0, p))
    whole = pl.BlockSpec((rows, LANES), lambda p: (0, 0))
    return block, bmat, cmat, cols, turned, bias, state, skip, whole


def ssm_state(act, cols):
    rows = act.shape[0]
    block, bmat, cmat, col, turn, square, state, skip, whole = ssm_specs(rows)
    return pl.pallas_call(
        ssm_state_kernel,
        grid=(SSM_PAIRS // PAIR_GROUP,),
        in_specs=[block, bmat, col],
        out_specs=state,
        out_shape=jax.ShapeDtypeStruct((SSM_PAIRS, LANES, STATE), jnp.float32),
        name="ssm_state",
        cost_estimate=pl.CostEstimate(flops=10**8, transcendentals=0, bytes_accessed=4 * 10**6),
    )(act, act, cols)


def ssm_local(act, cols, turned, bias):
    rows = act.shape[0]
    block, bmat, cmat, col, turn, square, state, skip, whole = ssm_specs(rows)
    return pl.pallas_call(
        ssm_local_kernel,
        grid=(SSM_PAIRS // PAIR_GROUP,),
        in_specs=[block, bmat, cmat, col, turn, square],
        out_specs=block,
        out_shape=jax.ShapeDtypeStruct((rows, SSM_PAIRS * LANES), jnp.float32),
        scratch_shapes=[pltpu.VMEM((rows, rows), jnp.float32)],
        name="ssm_local",
        cost_estimate=pl.CostEstimate(flops=10**9, transcendentals=24 * rows * rows, bytes_accessed=6 * 10**6),
    )(act, act, act, cols, turned, bias)


def ssm_carried(local_part, act, cols, state, skip_row, projected):
    rows = act.shape[0]
    block, bmat, cmat, col, turn, square, states, skip, whole = ssm_specs(rows)
    shape = jax.ShapeDtypeStruct((rows, SSM_PAIRS * LANES), jnp.float32)
    return pl.pallas_call(
        ssm_carry_kernel,
        grid=(SSM_PAIRS // PAIR_GROUP,),
        in_specs=[block, block, cmat, col, states, skip, block],
        out_specs=[block, block],
        out_shape=[shape, shape],
        name="ssm_carried",
        cost_estimate=pl.CostEstimate(flops=10**8, transcendentals=rows * 1536, bytes_accessed=9 * 10**6),
    )(local_part, act, act, cols, state, skip_row, projected)


def ssm_direct(g, act, cols):
    rows = act.shape[0]
    block, bmat, cmat, col, turn, square, states, skip, whole = ssm_specs(rows)
    return pl.pallas_call(
        ssm_direct_kernel,
        grid=(SSM_PAIRS // PAIR_GROUP,),
        in_specs=[block, cmat, col],
        out_specs=states,
        out_shape=jax.ShapeDtypeStruct((SSM_PAIRS, LANES, STATE), jnp.float32),
        name="ssm_direct",
        cost_estimate=pl.CostEstimate(flops=10**8, transcendentals=0, bytes_accessed=4 * 10**6),
    )(g, act, cols)


def ssm_backward(g, act, out, cols, turned, bias_turned, state, later, skip_row):
    rows = act.shape[0]
    block, bmat, cmat, col, turn, square, states, skip, whole = ssm_specs(rows)
    return pl.pallas_call(
        ssm_backward_kernel,
        grid=(SSM_PAIRS // PAIR_GROUP,),
        in_specs=[block, block, block, bmat, cmat, col, turn, square, states, states, skip],
        out_specs=[block, whole, whole, col, pl.BlockSpec((PAIR_GROUP, 2, LANES), lambda p: (p, 0, 0))],
        out_shape=[
            jax.ShapeDtypeStruct((rows, SSM_PAIRS * LANES), jnp.float32),
            jax.ShapeDtypeStruct((rows, STATE), jnp.float32),
            jax.ShapeDtypeStruct((rows, STATE), jnp.float32),
            jax.ShapeDtypeStruct((SSM_PAIRS, rows, 8), jnp.float32),
            jax.ShapeDtypeStruct((SSM_PAIRS, 2, LANES), jnp.float32),
        ],
        scratch_shapes=[pltpu.VMEM((rows, rows), jnp.float32)] * 2,
        name="ssm_backward",
        cost_estimate=pl.CostEstimate(flops=2 * 10**9, transcendentals=24 * rows * rows, bytes_accessed=12 * 10**6),
    )(g, act, out, act, act, cols, turned, bias_turned, state, later, skip_row)


def outer_kernel(split, blocks, core_ref, left_a_ref, right_a_ref, left_b_ref, right_b_ref, *rest):
    outs, turned_ref = rest[:-1], rest[-1]
    step = pl.program_id(0)

    def turn(left_ref):
        turned = left_ref[...].T
        if len(outs) == 1:
            turned_ref[...] = turned
            return
        tall = turned.shape[0] // (2 * blocks)
        second = core_ref[0] == 1
        for block in range(blocks):
            low = turned[2 * block * tall : (2 * block + 1) * tall]
            high = turned[(2 * block + 1) * tall : (2 * block + 2) * tall]
            turned_ref[pl.ds(block * tall, tall), :] = jnp.where(second, high, low)
            turned_ref[pl.ds((blocks + block) * tall, tall), :] = jnp.where(second, low, high)

    @pl.when(step == 0)
    def _():
        turn(left_a_ref)

    @pl.when(step == split)
    def _():
        turn(left_b_ref)

    def filled(right_ref):
        wide = right_ref.shape[1]
        piece = math.gcd(wide, 256)
        for at in range(0, wide, piece):
            lanes = pl.ds(at, piece)
            product = dot_nn(turned_ref[...], right_ref[:, lanes]).astype(jnp.bfloat16)
            for place, out_ref in enumerate(outs):
                tall = out_ref.shape[0]
                out_ref[:, lanes] = product[place * tall : (place + 1) * tall]

    @pl.when(step < split)
    def _():
        filled(right_a_ref)

    @pl.when(step >= split)
    def _():
        filled(right_b_ref)


def outer_pair(left_a, right_a, left_b, right_b, outputs=1):
    rows, width = left_a.shape
    wide_a = right_a.shape[1]
    wide_b = 0 if right_b is None else right_b.shape[1]
    wide = math.gcd(math.gcd(wide_a, wide_b), 1024) if wide_b else wide_a
    split = wide_a // wide
    total = split + wide_b // wide
    held = pl.BlockSpec((rows, width), lambda j, core: (0, 0))
    core = lax.axis_index("core").astype(jnp.int32).reshape(1)
    if right_b is None:
        left_b, right_b = left_a, right_a
    last = right_b.shape[1] // wide - 1
    return pl.pallas_call(
        functools.partial(outer_kernel, split, lax.axis_size("dpo")),
        grid_spec=pltpu.PrefetchScalarGridSpec(
            num_scalar_prefetch=1,
            grid=(total,),
            in_specs=[
                held,
                pl.BlockSpec((rows, wide), lambda j, core: (0, jnp.minimum(j, split - 1))),
                held,
                pl.BlockSpec((rows, wide), lambda j, core: (0, jnp.clip(j - split, 0, last))),
            ],
            out_specs=[pl.BlockSpec((width // outputs, wide), lambda j, core: (0, j))] * outputs,
            scratch_shapes=[pltpu.VMEM((width, rows), jnp.bfloat16)],
        ),
        out_shape=[jax.ShapeDtypeStruct((width // outputs, wide * total), jnp.bfloat16)]
        * outputs,
        name="outer_pair",
        cost_estimate=pl.CostEstimate(
            flops=2 * rows * width * wide * total,
            transcendentals=0,
            bytes_accessed=2 * width * wide * total,
        ),
    )(core, left_a, right_a, left_b, right_b)


def local(
    block_in,
    segment_ids,
    mamba_z,
    mamba_x,
    mamba_bc,
    mamba_dt,
    mamba_out,
    attn_q,
    attn_kv,
    attn_out,
    ffn_gate,
    ffn_up,
    ffn_down,
    mixer_norm,
    ffn_norm,
    conv_weight,
    conv_bias,
    dt_bias,
    a_log,
    d_skip,
    inner_norm,
    grad_out,
):
    sequences, rows, width = block_in.shape
    length = segment_ids.shape[1]
    taps = conv_weight.shape[0]
    group = Q_HEADS // KV_HEADS
    inner_width = SSM_HEADS * SSM_HEAD
    total_rows = sequences * rows
    inv_root = HEAD ** (-0.5)
    offset = lax.axis_index("seq") * rows
    positions = offset + jnp.arange(rows, dtype=jnp.int32)
    local_ids = lax.dynamic_slice_in_dim(segment_ids, offset, rows, 1)
    padded_ids = jnp.concatenate(
        [jnp.full((sequences, taps - 1), -1, jnp.int32), segment_ids], axis=1
    )
    window_ids = lax.dynamic_slice_in_dim(padded_ids, offset, rows + taps - 1, 1)
    prior_id = window_ids[:, taps - 2]
    tap_masks = [
        (window_ids[:, tap : tap + rows] == local_ids).astype(jnp.float32)[:, :, None]
        for tap in range(taps)
    ]
    cosine, sine = rope_tables(positions, HEAD)
    cos_b = cosine[:, None, :]
    sin_b = sine[:, None, :]
    behind = min(lax.axis_size("seq") - 1, (MAX_DOC - 2) // rows + 1) * rows
    key_ids = lax.dynamic_slice_in_dim(
        jnp.concatenate([jnp.full((sequences, behind), -1, jnp.int32), segment_ids], axis=1),
        offset,
        behind + rows,
        1,
    )
    key_order = jnp.arange(behind + rows, dtype=jnp.int32) - behind
    allowed = (key_order[None, None, :] <= jnp.arange(rows, dtype=jnp.int32)[None, :, None]) & (
        key_ids[:, None, :] == local_ids[:, :, None]
    )
    hops = min(lax.axis_size("seq") - 1, (MAX_DOC - 2) // rows + 1)
    spare = -(mamba_dt.shape[1] + 2) % LANES
    shard_in = jnp.concatenate(
        [
            mamba_z,
            attn_q,
            mamba_x,
            mamba_bc,
            attn_kv,
            mamba_dt,
            mixer_norm[:, None],
            ffn_norm[:, None],
            jnp.zeros((mixer_norm.shape[0], spare), jnp.bfloat16),
        ],
        axis=1,
    )
    shard_out = jnp.concatenate([mamba_out, attn_out, ffn_gate, ffn_up, ffn_down], axis=1)
    held_in, shard_out = lax.optimization_barrier((gathered_seq(shard_in), shard_out))
    full_in = lax.all_gather(held_in, ("dpo", "core"), axis=0, tiled=True)
    full_out = lax.all_gather(chained_seq(shard_out), ("dpo", "core"), axis=0, tiled=True)
    bc_width = mamba_bc.shape[1]
    q_width = attn_q.shape[1]
    kv_width = attn_kv.shape[1]
    hidden_width = ffn_gate.shape[1]
    at_q = inner_width
    at_u = at_q + q_width
    at_kv = at_u + inner_width + bc_width
    at_dt = at_kv + kv_width
    at_gain = at_dt + SSM_HEADS
    mixer_width = inner_width + q_width
    full_mixer = full_out[:, :mixer_width]
    full_gateup = full_out[:, mixer_width : mixer_width + 2 * hidden_width]
    full_down = full_out[:, mixer_width + 2 * hidden_width :]
    gain_one = full_in[:, at_gain].astype(jnp.float32)
    gain_two = full_in[:, at_gain + 1].astype(jnp.float32)
    x_in = block_in.reshape(total_rows, width).astype(jnp.float32)
    normed, factor_one = rms_forward(x_in, gain_one)
    normed_b = normed.astype(jnp.bfloat16)
    projected = matmul(normed_b, full_in)
    gate_z = projected[:, :at_q]
    inner_u = projected[:, at_u:at_kv]
    step_raw = projected[:, at_dt:at_gain]
    channels = inner_u.shape[1]
    conv_in = inner_u.reshape(sequences, rows, channels)
    edge_in = passed_along(conv_in[:, rows - taps + 1 :, :], "seq", 1)
    extended = jnp.concatenate([edge_in, conv_in], axis=1)
    conv_pre = jnp.zeros_like(conv_in) + conv_bias
    for tap in range(taps):
        conv_pre = conv_pre + conv_weight[tap] * extended[:, tap : tap + rows] * tap_masks[tap]
    activated = jax.nn.silu(conv_pre)
    act = activated.reshape(total_rows, channels)
    step = jax.nn.softplus(step_raw + dt_bias)
    ids = local_ids.reshape(total_rows)
    order = jnp.arange(rows)
    pair = (order[:, None] >= order[None, :]) & (ids[:, None] == ids[None, :])
    bias = jnp.where(pair, 0.0, -1e30).astype(jnp.float32)
    bias_turned = jnp.where(
        (order[:, None] <= order[None, :]) & (ids[:, None] == ids[None, :]), 0.0, -1e30
    ).astype(jnp.float32)
    inbound = (ids == prior_id[0]).astype(jnp.float32)[:, None]
    outbound = (ids == ids[-1]).astype(jnp.float32)[:, None]
    rate = -jnp.exp(a_log)
    ladder = (order[:, None] >= order[None, :]).astype(jnp.float32)
    decay = jnp.dot(ladder, step * rate, precision=lax.Precision.HIGHEST)
    entry = jnp.exp(decay) * inbound
    tail = jnp.exp(decay[-1:] - decay) * outbound
    carry = jnp.exp(decay[-1]) * inbound[-1, 0]
    cols = jnp.stack([decay, step, entry, tail], axis=1)
    cols = cols.reshape(rows, 4, SSM_PAIRS, 2).transpose(2, 0, 1, 3).reshape(SSM_PAIRS, rows, 8)
    turned = decay.T.reshape(SSM_PAIRS, 2, rows)
    skip_row = jnp.repeat(d_skip, SSM_HEAD)[None, :]
    carry_rows = jnp.repeat(carry, SSM_HEAD).reshape(SSM_PAIRS, LANES, 1)
    state_local = ssm_state(act, cols)
    outgoing = state_local
    for hop in range(hops):
        incoming = passed_along(outgoing.astype(jnp.bfloat16), "seq", 1)
        outgoing = carry_rows * incoming.astype(jnp.float32) + state_local
    local_part = ssm_local(act, cols, turned, bias)
    ssm_out, gated = ssm_carried(local_part, act, cols, incoming, skip_row, projected)
    silu_z = jax.nn.silu(gate_z)
    mixed_norm, factor_m = rms_forward(gated, inner_norm)
    mixed_b = mixed_norm.astype(jnp.bfloat16)
    query = projected[:, at_q:at_u].reshape(sequences, rows, Q_HEADS, HEAD)
    keyval = projected[:, at_kv:at_dt].reshape(sequences, rows, 2 * KV_HEADS, HEAD)
    query_b = rotate(query, cos_b, sin_b).astype(jnp.bfloat16)
    keys_local = rotate(keyval[:, :, :KV_HEADS], cos_b, sin_b)
    kv_local = jnp.concatenate([keys_local, keyval[:, :, KV_HEADS:]], axis=2).astype(jnp.bfloat16)
    kv_flat = kv_local.reshape(sequences, rows, kv_width)
    kv_all = jnp.concatenate(
        [passed_along(kv_flat, "seq", far) for far in range(hops, 0, -1)] + [kv_flat], axis=1
    )
    window = kv_all.shape[1]
    kv_all = kv_all.reshape(sequences, window, 2 * KV_HEADS, HEAD)
    keys = kv_all[:, :, :KV_HEADS]
    values = kv_all[:, :, KV_HEADS:]
    query_g = query_b.reshape(sequences, rows, KV_HEADS, group, HEAD)

    def attention_scores():
        raw = (
            jnp.einsum("stkgd,slkd->skgtl", query_g, keys, preferred_element_type=jnp.float32)
            * inv_root
        )
        return jnp.where(allowed[:, None, None], raw, -1e30)

    scores = attention_scores()
    top = jnp.max(scores, axis=-1, keepdims=True)
    lse = top + jnp.log(jnp.sum(jnp.exp(scores - top), axis=-1, keepdims=True))
    probs_b = jnp.exp(scores - lse).astype(jnp.bfloat16)
    attended = jnp.einsum("skgtl,slkd->stkgd", probs_b, values, preferred_element_type=jnp.float32)
    attended_b = attended.reshape(total_rows, Q_HEADS * HEAD).astype(jnp.bfloat16)
    mixers_b = jnp.concatenate([mixed_b, attended_b], axis=1)
    mid = x_in + matmul_nt(mixers_b, full_mixer)
    fnormed, factor_two = rms_forward(mid, gain_two)
    fnormed_b = fnormed.astype(jnp.bfloat16)
    gateup_h = matmul(fnormed_b, full_gateup)
    gate_h = gateup_h[:, :hidden_width]
    up_h = gateup_h[:, hidden_width:]
    hidden_b = (jax.nn.silu(gate_h) * up_h).astype(jnp.bfloat16)
    block_out = (
        (mid + matmul_nt(hidden_b, full_down)).astype(jnp.bfloat16).reshape(sequences, rows, width)
    )
    grad_flat = grad_out.reshape(total_rows, width)
    d_hidden = matmul(grad_flat, full_down)
    d_gate_b = (d_hidden * up_h * silu_grad(gate_h)).astype(jnp.bfloat16)
    d_up_b = (d_hidden * jax.nn.silu(gate_h)).astype(jnp.bfloat16)
    d_gateup_b = jnp.concatenate([d_gate_b, d_up_b], axis=1)
    part_ffn = scattered_dp(outer_pair(fnormed_b, d_gateup_b, grad_flat, hidden_b)[0])
    d_fnorm = matmul_nt(d_gateup_b, full_gateup)
    d_mid_norm, g_fnorm = rms_backward(mid, factor_two, gain_two, d_fnorm)
    d_mid = grad_flat.astype(jnp.float32) + d_mid_norm
    d_mid_b = d_mid.astype(jnp.bfloat16)
    d_mixers = matmul(d_mid_b, full_mixer)
    d_mnorm = d_mixers[:, :inner_width]
    d_gated, g_inner = rms_backward(gated, factor_m, inner_norm, d_mnorm)
    d_ssm = d_gated * silu_z
    d_z = d_gated * ssm_out * silu_grad(gate_z)
    direct = ssm_direct(d_ssm, act, cols)
    backlog = direct
    for hop in range(hops):
        later_grad = passed_along(backlog.astype(jnp.bfloat16), "seq", -1)
        backlog = direct + carry_rows * later_grad.astype(jnp.float32)
    d_carry = jnp.sum(
        (later_grad.astype(jnp.float32) * incoming.astype(jnp.float32)).reshape(
            SSM_HEADS, SSM_HEAD, STATE
        ),
        axis=(1, 2),
    )
    d_att_b = d_mixers[:, inner_width:].astype(jnp.bfloat16)
    d_att_g = d_att_b.reshape(sequences, rows, KV_HEADS, group, HEAD)
    probs = jnp.exp(attention_scores() - lse)
    d_probs = jnp.einsum("stkgd,slkd->skgtl", d_att_g, values, preferred_element_type=jnp.float32)
    d_scores_b = (probs * (d_probs - jnp.sum(probs * d_probs, axis=-1, keepdims=True))).astype(
        jnp.bfloat16
    )
    d_query = (
        jnp.einsum("skgtl,slkd->stkgd", d_scores_b, keys, preferred_element_type=jnp.float32)
        * inv_root
    )
    d_keys = (
        jnp.einsum("skgtl,stkgd->slkd", d_scores_b, query_g, preferred_element_type=jnp.float32)
        * inv_root
    )
    d_values = jnp.einsum("skgtl,stkgd->slkd", probs_b, d_att_g, preferred_element_type=jnp.float32)
    d_kv_all = jnp.concatenate([d_keys, d_values], axis=2).reshape(sequences, window, kv_width)
    d_kv_local = d_kv_all[:, window - rows :]
    for far in range(1, hops + 1):
        start = window - (far + 1) * rows
        term = d_kv_all[:, start : start + rows].astype(jnp.bfloat16)
        d_kv_local = d_kv_local + passed_along(term, "seq", -far).astype(jnp.float32)
    d_kv_local = d_kv_local.reshape(sequences, rows, 2 * KV_HEADS, HEAD)
    d_key_local = rotate_back(d_kv_local[:, :, :KV_HEADS], cos_b, sin_b)
    d_kv_b = (
        jnp.concatenate([d_key_local, d_kv_local[:, :, KV_HEADS:]], axis=2)
        .reshape(total_rows, 2 * KV_HEADS * HEAD)
        .astype(jnp.bfloat16)
    )
    d_q_b = (
        rotate_back(d_query.reshape(sequences, rows, Q_HEADS, HEAD), cos_b, sin_b)
        .reshape(total_rows, Q_HEADS * HEAD)
        .astype(jnp.bfloat16)
    )
    d_early = jnp.concatenate([d_z.astype(jnp.bfloat16), d_q_b], axis=1)
    early_own, early_other = outer_pair(normed_b, d_early, d_mid_b, mixers_b, 2)
    early_pair = paired_cores(early_own, early_other)
    later_grad, early_pair = lax.optimization_barrier((later_grad, early_pair))
    part_early = scattered_own(early_pair)
    d_xs, d_bmat, d_cmat, d_cols, d_rows = ssm_backward(
        d_ssm, act, ssm_out, cols, turned, bias_turned, incoming, later_grad, skip_row
    )
    d_pairs = d_cols[:, :, :6].reshape(SSM_PAIRS, rows, 3, 2).transpose(2, 1, 0, 3)
    d_pairs = d_pairs.reshape(3, rows, SSM_HEADS)
    d_sums = jnp.sum(d_rows.reshape(SSM_PAIRS, 2, 2, SSM_HEAD), axis=3).transpose(1, 0, 2)
    d_sums = d_sums.reshape(2, SSM_HEADS)
    g_skip = d_sums[1]
    d_decay = d_pairs[0] - d_pairs[2]
    d_rise = jnp.dot(ladder.T, d_decay, precision=lax.Precision.HIGHEST)
    d_rise = d_rise + (d_sums[0] + d_carry * carry)
    d_step = d_pairs[1] + d_rise * rate
    g_alog = jnp.sum(d_rise * step, axis=0) * rate
    d_act = jnp.concatenate([d_xs, d_bmat, d_cmat], axis=1).reshape(sequences, rows, channels)
    d_act, part_ffn = lax.optimization_barrier((d_act, part_ffn))
    owned_ffn, _ = hopped_seq(part_ffn, None)
    d_pre = d_act * silu_grad(conv_pre)
    g_cbias = jnp.sum(d_pre, axis=(0, 1))
    g_cweight = jnp.stack(
        [
            jnp.sum(d_pre * extended[:, tap : tap + rows] * tap_masks[tap], axis=(0, 1))
            for tap in range(taps)
        ]
    )
    d_padded = jnp.zeros_like(extended)
    for tap in range(taps):
        d_padded = d_padded + jnp.pad(
            d_pre * tap_masks[tap] * conv_weight[tap], ((0, 0), (tap, taps - 1 - tap), (0, 0))
        )
    edge_grad = passed_along(d_padded[:, : taps - 1], "seq", -1)
    d_inner = d_padded[:, taps - 1 :] + jnp.pad(edge_grad, ((0, 0), (rows - taps + 1, 0), (0, 0)))
    d_inner = d_inner.reshape(total_rows, channels)
    d_step_raw = d_step.reshape(total_rows, SSM_HEADS) * jax.nn.sigmoid(step_raw + dt_bias)
    g_dtb = jnp.sum(d_step_raw, axis=0)
    d_x_b = d_inner[:, :inner_width].astype(jnp.bfloat16)
    d_bc_b = d_inner[:, inner_width:].astype(jnp.bfloat16)
    d_st_b = d_step_raw.astype(jnp.bfloat16)
    d_late = jnp.concatenate(
        [
            d_x_b,
            d_bc_b,
            d_kv_b,
            d_st_b,
            jnp.zeros((total_rows, spare + 2), jnp.bfloat16),
        ],
        axis=1,
    )
    late_own, late_other = outer_pair(normed_b, d_late, None, None, 2)
    late_pair = paired_cores(late_own, late_other)
    d_norm = matmul_nt(d_early, full_in[:, :at_u]) + matmul_nt(d_late, full_in[:, at_u:])
    d_in_norm, g_mnorm = rms_backward(x_in, factor_one, gain_one, d_norm)
    grad_in = (d_mid + d_in_norm).astype(jnp.bfloat16).reshape(sequences, rows, width)
    smalls = jnp.concatenate([g_dtb, g_alog, g_skip])
    strips = [g_inner, g_mnorm, g_fnorm, smalls]
    packed = jnp.concatenate(
        [g_cweight, g_cbias[None]]
        + [jnp.pad(strip, (0, channels - strip.shape[0]))[None] for strip in strips],
        axis=0,
    )
    packed, late_pair = lax.optimization_barrier((packed, late_pair))
    part_late = scattered_own(late_pair)
    summed = summed_everywhere(packed)
    gain_rows = mixer_norm.shape[0]
    part_early, summed, grad_in = lax.optimization_barrier((part_early, summed, grad_in))
    owned_early, part_late = hopped_seq(part_early, part_late)
    owned_late = scattered_seq(part_late)
    owner = lax.axis_index("dpo") * 2 + lax.axis_index("core")
    first_row = (owner * lax.axis_size("seq") + lax.axis_index("seq")) * gain_rows
    g_mnorm_own = lax.dynamic_slice_in_dim(summed[taps + 2], first_row, gain_rows, 0)
    g_fnorm_own = lax.dynamic_slice_in_dim(summed[taps + 3], first_row, gain_rows, 0)
    at_mixers = at_u
    late_kv = at_kv - at_u
    late_dt = at_dt - at_u
    return (
        block_out,
        grad_in,
        owned_early[:, :at_q],
        owned_late[:, :inner_width],
        owned_late[:, inner_width:late_kv],
        owned_late[:, late_dt : late_dt + SSM_HEADS],
        owned_early[:, at_mixers : at_mixers + inner_width],
        owned_early[:, at_q:at_u],
        owned_late[:, late_kv:late_dt],
        owned_early[:, at_mixers + inner_width :],
        owned_ffn[:, :hidden_width],
        owned_ffn[:, hidden_width : 2 * hidden_width],
        owned_ffn[:, 2 * hidden_width :],
        g_mnorm_own,
        g_fnorm_own,
        summed[:taps],
        summed[taps],
        summed[taps + 4, :SSM_HEADS],
        summed[taps + 4, SSM_HEADS : 2 * SSM_HEADS],
        summed[taps + 4, 2 * SSM_HEADS : 3 * SSM_HEADS],
        summed[taps + 1, :inner_width],
    )


def solution(mesh):
    grid = mesh.devices
    mesh = Mesh(grid.reshape(grid.shape[0] // 2, 2, grid.shape[1]), DP + ("seq",))
    in_specs = (
        P(DP, "seq", None),
        P(DP, None),
        P(DP + ("seq",), None),
        P(DP + ("seq",), None),
        P(DP + ("seq",), None),
        P(DP + ("seq",), None),
        P(DP + ("seq",), None),
        P(DP + ("seq",), None),
        P(DP + ("seq",), None),
        P(DP + ("seq",), None),
        P(DP + ("seq",), None),
        P(DP + ("seq",), None),
        P(DP + ("seq",), None),
        P(DP + ("seq",)),
        P(DP + ("seq",)),
        P(),
        P(),
        P(),
        P(),
        P(),
        P(),
        P(DP, "seq", None),
    )
    out_specs = (
        P(DP, "seq", None),
        P(DP, "seq", None),
        P(DP + ("seq",), None),
        P(DP + ("seq",), None),
        P(DP + ("seq",), None),
        P(DP + ("seq",), None),
        P(DP + ("seq",), None),
        P(DP + ("seq",), None),
        P(DP + ("seq",), None),
        P(DP + ("seq",), None),
        P(DP + ("seq",), None),
        P(DP + ("seq",), None),
        P(DP + ("seq",), None),
        P(DP + ("seq",)),
        P(DP + ("seq",)),
        P(),
        P(),
        P(),
        P(),
        P(),
        P(),
    )
    return jax.shard_map(local, mesh=mesh, in_specs=in_specs, out_specs=out_specs, check_vma=False)
```

```python
import functools
import math

import jax
import jax.numpy as jnp
from jax import lax
from jax.experimental import pallas as pl
from jax.experimental.pallas import tpu as pltpu
from jax.sharding import Mesh
from jax.sharding import PartitionSpec as P

SSM_HEADS = 24
SSM_HEAD = 64
STATE = 128
Q_HEADS = 8
KV_HEADS = 2
HEAD = 64


EPSILON = 1e-05
ROPE_BASE = 100000000000.0
MAX_DOC = 512
LANES = 128
SSM_PAIRS = SSM_HEADS * SSM_HEAD // LANES
PAIR_GROUP = 4
DP = ("dpo", "core")


def passed_along(block, axis, distance):
    devices = range(lax.axis_size(axis))
    route = [(i - distance, i) for i in devices if i - distance in devices]
    return lax.ppermute(block, axis, route)


def scattered_dp(grad):
    return lax.psum_scatter(grad, ("dpo", "core"), scatter_dimension=0, tiled=True)


def swapped(block):
    return lax.ppermute(block, "core", [(0, 1), (1, 0)])


def paired_cores(own, other):
    return (own.astype(jnp.float32) + swapped(other).astype(jnp.float32)).astype(jnp.bfloat16)


def scattered_own(paired):
    return lax.psum_scatter(paired, "dpo", scatter_dimension=0, tiled=True)


def summed_everywhere(block):
    for axis in ("core", "dpo", "seq"):
        count = lax.axis_size(axis)
        bit = 1
        while bit < count:
            block = block + lax.ppermute(block, axis, [(i, i ^ bit) for i in range(count)])
            bit *= 2
    return block


def scattered_seq(part):
    return lax.psum_scatter(part, "seq", scatter_dimension=0, tiled=True).astype(jnp.float32)


def chained_seq(shard):
    count = lax.axis_size("seq")
    before = [shard]
    after = [shard]
    for hop in range(count - 1):
        before.append(passed_along(before[-1], "seq", 1))
        after.append(passed_along(after[-1], "seq", -1))
    line = jnp.concatenate(before[:0:-1] + after, axis=0)
    rows = shard.shape[0]
    start = (count - 1 - lax.axis_index("seq")) * rows
    return lax.dynamic_slice_in_dim(line, start, count * rows, 0)


def hopped_seq(part, rider):
    index = lax.axis_index("seq")
    count = lax.axis_size("seq")
    held = part.reshape(count, part.shape[0] // count, part.shape[1])
    bit = 1
    while bit < count:
        halves = held.reshape(held.shape[0] // 2, 2, *held.shape[1:])
        odd = (index // bit) % 2 == 1
        mine = jnp.where(odd, halves[:, 1], halves[:, 0])
        other = jnp.where(odd, halves[:, 0], halves[:, 1])
        got = lax.ppermute(other, "seq", [(i, i ^ bit) for i in range(count)])
        held = mine.astype(jnp.float32) + got.astype(jnp.float32)
        bit *= 2
        if bit < count:
            held = held.astype(jnp.bfloat16)
        if bit == 2 and rider is not None:
            held, rider = lax.optimization_barrier((held, rider))
    return held[0].astype(jnp.float32), rider


def silu_grad(value):
    sigma = jax.nn.sigmoid(value)
    return sigma * (1.0 + value * (1.0 - sigma))


def rms_forward(value, gain):
    factor = lax.rsqrt(jnp.mean(value * value, axis=-1, keepdims=True) + EPSILON)
    return (value * factor * gain, factor)


def rms_backward(value, factor, gain, upstream):
    weighted = upstream * gain
    gain_grad = jnp.sum(upstream * value * factor, axis=0)
    inward = factor * weighted - value * factor * factor * factor * jnp.mean(
        weighted * value, axis=-1, keepdims=True
    )
    return (inward, gain_grad)


def matmul(left, right):
    return jnp.dot(left, right, preferred_element_type=jnp.float32)


def matmul_nt(left, right):
    return lax.dot_general(
        left, right, (((1,), (1,)), ((), ())), preferred_element_type=jnp.float32
    )


def matmul_tn(left, right):
    return lax.dot_general(
        left, right, (((0,), (0,)), ((), ())), preferred_element_type=jnp.float32
    )


def rope_tables(positions, head_size):
    half = head_size // 2
    freq_scale = ROPE_BASE ** (-jnp.arange(half, dtype=jnp.float32) / half)
    angles = positions.astype(jnp.float32)[:, None] * freq_scale[None, :]
    return (jnp.cos(angles), jnp.sin(angles))


def rotate(value, cosine, sine):
    half = value.shape[-1] // 2
    first = value[..., :half]
    second = value[..., half:]
    return jnp.concatenate(
        [first * cosine - second * sine, second * cosine + first * sine], axis=-1
    )


def rotate_back(grad, cosine, sine):
    half = grad.shape[-1] // 2
    first = grad[..., :half]
    second = grad[..., half:]
    return jnp.concatenate(
        [first * cosine + second * sine, second * cosine - first * sine], axis=-1
    )


def half_lanes(cols, first, shape):
    lane = lax.broadcasted_iota(jnp.int32, shape, 1)
    return jnp.where(lane < SSM_HEAD, cols[:, first : first + 1], cols[:, first + 1 : first + 2])


def dot_nn(left, right):
    return lax.dot_general(
        left, right, (((1,), (0,)), ((), ())), preferred_element_type=jnp.float32
    )


def each_pair(body):
    for k in range(PAIR_GROUP):
        body(k, pl.ds(k * LANES, LANES))


def ssm_state_kernel(xs_ref, b_ref, cols_ref, state_ref):
    b_low = b_ref[...].astype(jnp.bfloat16)

    def one(k, lanes):
        xs = xs_ref[:, lanes]
        cols = cols_ref[k]
        scaled = xs * half_lanes(cols, 2, xs.shape)
        tailed = (scaled * half_lanes(cols, 6, xs.shape)).astype(jnp.bfloat16)
        state_ref[k] = lax.dot_general(
            tailed, b_low, (((0,), (0,)), ((), ())), preferred_element_type=jnp.float32
        )

    each_pair(one)


def ssm_local_kernel(xs_ref, b_ref, c_ref, cols_ref, rows_ref, bias_ref, out_ref, cb_ref):
    bmat = b_ref[...]

    @pl.when(pl.program_id(0) == 0)
    def _():
        cb_ref[...] = lax.dot_general(
            c_ref[...],
            bmat,
            (((1,), (1,)), ((), ())),
            precision=lax.Precision.HIGHEST,
            preferred_element_type=jnp.float32,
        )

    def one(k, lanes):
        xs = xs_ref[:, lanes]
        cols = cols_ref[k]
        rows = rows_ref[k]
        scaled_b = (xs * half_lanes(cols, 2, xs.shape)).astype(jnp.bfloat16)
        parts = []
        for h in range(2):
            kernel = jnp.exp(cols[:, h : h + 1] - rows[h : h + 1, :] + bias_ref[...])
            parts.append(dot_nn((kernel * cb_ref[...]).astype(jnp.bfloat16), scaled_b))
        lane = lax.broadcasted_iota(jnp.int32, xs.shape, 1)
        out_ref[:, lanes] = jnp.where(lane < SSM_HEAD, parts[0], parts[1])

    each_pair(one)


def ssm_carry_kernel(local_ref, xs_ref, c_ref, cols_ref, state_ref, skip_ref, z_ref, out_ref, gated_ref):
    c_low = c_ref[...].astype(jnp.bfloat16)

    def one(k, lanes):
        xs = xs_ref[:, lanes]
        carried = lax.dot_general(
            c_low, state_ref[k], (((1,), (1,)), ((), ())), preferred_element_type=jnp.float32
        )
        entry = half_lanes(cols_ref[k], 4, xs.shape)
        out = local_ref[:, lanes] + entry * carried + skip_ref[:, lanes] * xs
        out_ref[:, lanes] = out
        gate = z_ref[:, lanes]
        gated_ref[:, lanes] = out * (gate * jax.nn.sigmoid(gate))

    each_pair(one)


def ssm_direct_kernel(g_ref, c_ref, cols_ref, direct_ref):
    c_low = c_ref[...].astype(jnp.bfloat16)

    def one(k, lanes):
        g = g_ref[:, lanes]
        entered = (g * half_lanes(cols_ref[k], 4, g.shape)).astype(jnp.bfloat16)
        direct_ref[k] = lax.dot_general(
            entered, c_low, (((0,), (0,)), ((), ())), preferred_element_type=jnp.float32
        )

    each_pair(one)


def ssm_backward_kernel(
    g_ref,
    xs_ref,
    out_ref,
    b_ref,
    c_ref,
    cols_ref,
    rows_ref,
    bias_ref,
    state_ref,
    later_ref,
    skip_ref,
    dxs_ref,
    db_ref,
    dc_ref,
    dcols_ref,
    drows_ref,
    cb_ref,
    dcb_ref,
):
    pair = pl.program_id(0)
    bmat = b_ref[...]
    cmat = c_ref[...]
    b_low = bmat.astype(jnp.bfloat16)
    c_low = cmat.astype(jnp.bfloat16)

    @pl.when(pair == 0)
    def _():
        cb_ref[...] = lax.dot_general(
            bmat,
            cmat,
            (((1,), (1,)), ((), ())),
            precision=lax.Precision.HIGHEST,
            preferred_element_type=jnp.float32,
        )
        dcb_ref[...] = jnp.zeros_like(dcb_ref)
        db_ref[...] = jnp.zeros_like(db_ref)
        dc_ref[...] = jnp.zeros_like(dc_ref)

    def one(at, lanes):
        g = g_ref[:, lanes]
        xs = xs_ref[:, lanes]
        skip = skip_ref[:, lanes]
        cols = cols_ref[at]
        rows = rows_ref[at]
        step = half_lanes(cols, 2, xs.shape)
        tail = half_lanes(cols, 6, xs.shape)
        lane = lax.broadcasted_iota(jnp.int32, xs.shape, 1)
        first = lane < SSM_HEAD
        g_low = g.astype(jnp.bfloat16)
        scaled = xs * step
        parts = []
        total = dcb_ref[...]
        for k in range(2):
            mine = first if k == 0 else jnp.logical_not(first)
            kernel = jnp.exp(rows[k : k + 1, :] - cols[:, k : k + 1] + bias_ref[...])
            parts.append(dot_nn((kernel * cb_ref[...]).astype(jnp.bfloat16), g_low))
            crossed = lax.dot_general(
                jnp.where(mine, scaled, 0.0).astype(jnp.bfloat16),
                g_low,
                (((1,), (1,)), ((), ())),
                preferred_element_type=jnp.float32,
            )
            total = total + crossed * kernel
        dcb_ref[...] = total
        later = later_ref[at]
        swept = tail * lax.dot_general(
            b_low, later, (((1,), (1,)), ((), ())), preferred_element_type=jnp.float32
        )
        inner = jnp.where(first, parts[0], parts[1]) + swept
        dxs_ref[:, lanes] = step * inner + skip * g
        db_ref[...] += dot_nn((scaled * tail).astype(jnp.bfloat16), later)
        entered = (g * half_lanes(cols, 4, g.shape)).astype(jnp.bfloat16)
        dc_ref[...] += dot_nn(entered, state_ref[at])
        rose = g_low.astype(jnp.float32) * (out_ref[:, lanes] - skip * xs)
        stepped = xs * inner
        kept = scaled.astype(jnp.bfloat16).astype(jnp.float32)
        fell = kept * (inner - swept) + scaled * swept
        columns = [
            jnp.sum(jnp.where(first, value, 0.0), axis=1, keepdims=True)
            if k == 0
            else jnp.sum(jnp.where(first, 0.0, value), axis=1, keepdims=True)
            for value in (rose, stepped, fell)
            for k in range(2)
        ]
        spot = lax.broadcasted_iota(jnp.int32, cols.shape, 1)
        packed = jnp.zeros_like(cols)
        for index, column in enumerate(columns):
            packed = jnp.where(spot == index, column, packed)
        dcols_ref[at] = packed
        drows_ref[at, 0:1, :] = jnp.sum(scaled * swept, axis=0, keepdims=True)
        drows_ref[at, 1:2, :] = jnp.sum(g * xs, axis=0, keepdims=True)

    each_pair(one)

    @pl.when(pair == pl.num_programs(0) - 1)
    def _():
        low = dcb_ref[...].astype(jnp.bfloat16)
        db_ref[...] += dot_nn(low, c_low)
        dc_ref[...] += lax.dot_general(
            low, b_low, (((0,), (0,)), ((), ())), preferred_element_type=jnp.float32
        )


def ssm_specs(rows):
    wide = PAIR_GROUP * LANES
    block = pl.BlockSpec((rows, wide), lambda p: (0, p))
    bmat = pl.BlockSpec((rows, LANES), lambda p: (0, SSM_PAIRS))
    cmat = pl.BlockSpec((rows, LANES), lambda p: (0, SSM_PAIRS + 1))
    cols = pl.BlockSpec((PAIR_GROUP, rows, 8), lambda p: (p, 0, 0))
    turned = pl.BlockSpec((PAIR_GROUP, 2, rows), lambda p: (p, 0, 0))
    bias = pl.BlockSpec((rows, rows), lambda p: (0, 0))
    state = pl.BlockSpec((PAIR_GROUP, LANES, STATE), lambda p: (p, 0, 0))
    skip = pl.BlockSpec((1, wide), lambda p: (0, p))
    whole = pl.BlockSpec((rows, LANES), lambda p: (0, 0))
    return block, bmat, cmat, cols, turned, bias, state, skip, whole


def ssm_state(act, cols):
    rows = act.shape[0]
    block, bmat, cmat, col, turn, square, state, skip, whole = ssm_specs(rows)
    return pl.pallas_call(
        ssm_state_kernel,
        grid=(SSM_PAIRS // PAIR_GROUP,),
        in_specs=[block, bmat, col],
        out_specs=state,
        out_shape=jax.ShapeDtypeStruct((SSM_PAIRS, LANES, STATE), jnp.float32),
        name="ssm_state",
        cost_estimate=pl.CostEstimate(flops=10**8, transcendentals=0, bytes_accessed=4 * 10**6),
    )(act, act, cols)


def ssm_local(act, cols, turned, bias):
    rows = act.shape[0]
    block, bmat, cmat, col, turn, square, state, skip, whole = ssm_specs(rows)
    return pl.pallas_call(
        ssm_local_kernel,
        grid=(SSM_PAIRS // PAIR_GROUP,),
        in_specs=[block, bmat, cmat, col, turn, square],
        out_specs=block,
        out_shape=jax.ShapeDtypeStruct((rows, SSM_PAIRS * LANES), jnp.float32),
        scratch_shapes=[pltpu.VMEM((rows, rows), jnp.float32)],
        name="ssm_local",
        cost_estimate=pl.CostEstimate(flops=10**9, transcendentals=24 * rows * rows, bytes_accessed=6 * 10**6),
    )(act, act, act, cols, turned, bias)


def ssm_carried(local_part, act, cols, state, skip_row, projected):
    rows = act.shape[0]
    block, bmat, cmat, col, turn, square, states, skip, whole = ssm_specs(rows)
    shape = jax.ShapeDtypeStruct((rows, SSM_PAIRS * LANES), jnp.float32)
    return pl.pallas_call(
        ssm_carry_kernel,
        grid=(SSM_PAIRS // PAIR_GROUP,),
        in_specs=[block, block, cmat, col, states, skip, block],
        out_specs=[block, block],
        out_shape=[shape, shape],
        name="ssm_carried",
        cost_estimate=pl.CostEstimate(flops=10**8, transcendentals=rows * 1536, bytes_accessed=9 * 10**6),
    )(local_part, act, act, cols, state, skip_row, projected)


def ssm_direct(g, act, cols):
    rows = act.shape[0]
    block, bmat, cmat, col, turn, square, states, skip, whole = ssm_specs(rows)
    return pl.pallas_call(
        ssm_direct_kernel,
        grid=(SSM_PAIRS // PAIR_GROUP,),
        in_specs=[block, cmat, col],
        out_specs=states,
        out_shape=jax.ShapeDtypeStruct((SSM_PAIRS, LANES, STATE), jnp.float32),
        name="ssm_direct",
        cost_estimate=pl.CostEstimate(flops=10**8, transcendentals=0, bytes_accessed=4 * 10**6),
    )(g, act, cols)


def ssm_backward(g, act, out, cols, turned, bias_turned, state, later, skip_row):
    rows = act.shape[0]
    block, bmat, cmat, col, turn, square, states, skip, whole = ssm_specs(rows)
    return pl.pallas_call(
        ssm_backward_kernel,
        grid=(SSM_PAIRS // PAIR_GROUP,),
        in_specs=[block, block, block, bmat, cmat, col, turn, square, states, states, skip],
        out_specs=[block, whole, whole, col, pl.BlockSpec((PAIR_GROUP, 2, LANES), lambda p: (p, 0, 0))],
        out_shape=[
            jax.ShapeDtypeStruct((rows, SSM_PAIRS * LANES), jnp.float32),
            jax.ShapeDtypeStruct((rows, STATE), jnp.float32),
            jax.ShapeDtypeStruct((rows, STATE), jnp.float32),
            jax.ShapeDtypeStruct((SSM_PAIRS, rows, 8), jnp.float32),
            jax.ShapeDtypeStruct((SSM_PAIRS, 2, LANES), jnp.float32),
        ],
        scratch_shapes=[pltpu.VMEM((rows, rows), jnp.float32)] * 2,
        name="ssm_backward",
        cost_estimate=pl.CostEstimate(flops=2 * 10**9, transcendentals=24 * rows * rows, bytes_accessed=12 * 10**6),
    )(g, act, out, act, act, cols, turned, bias_turned, state, later, skip_row)


def outer_kernel(split, blocks, core_ref, left_a_ref, right_a_ref, left_b_ref, right_b_ref, *rest):
    outs, turned_ref = rest[:-1], rest[-1]
    step = pl.program_id(0)

    def turn(left_ref):
        turned = left_ref[...].T
        if len(outs) == 1:
            turned_ref[...] = turned
            return
        tall = turned.shape[0] // (2 * blocks)
        second = core_ref[0] == 1
        for block in range(blocks):
            low = turned[2 * block * tall : (2 * block + 1) * tall]
            high = turned[(2 * block + 1) * tall : (2 * block + 2) * tall]
            turned_ref[pl.ds(block * tall, tall), :] = jnp.where(second, high, low)
            turned_ref[pl.ds((blocks + block) * tall, tall), :] = jnp.where(second, low, high)

    @pl.when(step == 0)
    def _():
        turn(left_a_ref)

    @pl.when(step == split)
    def _():
        turn(left_b_ref)

    def filled(right_ref):
        wide = right_ref.shape[1]
        piece = math.gcd(wide, 256)
        for at in range(0, wide, piece):
            lanes = pl.ds(at, piece)
            product = dot_nn(turned_ref[...], right_ref[:, lanes]).astype(jnp.bfloat16)
            for place, out_ref in enumerate(outs):
                tall = out_ref.shape[0]
                out_ref[:, lanes] = product[place * tall : (place + 1) * tall]

    @pl.when(step < split)
    def _():
        filled(right_a_ref)

    @pl.when(step >= split)
    def _():
        filled(right_b_ref)


def outer_pair(left_a, right_a, left_b, right_b, outputs=1):
    rows, width = left_a.shape
    wide_a = right_a.shape[1]
    wide_b = 0 if right_b is None else right_b.shape[1]
    wide = math.gcd(math.gcd(wide_a, wide_b), 1024) if wide_b else wide_a
    split = wide_a // wide
    total = split + wide_b // wide
    held = pl.BlockSpec((rows, width), lambda j, core: (0, 0))
    core = lax.axis_index("core").astype(jnp.int32).reshape(1)
    if right_b is None:
        left_b, right_b = left_a, right_a
    last = right_b.shape[1] // wide - 1
    return pl.pallas_call(
        functools.partial(outer_kernel, split, lax.axis_size("dpo")),
        grid_spec=pltpu.PrefetchScalarGridSpec(
            num_scalar_prefetch=1,
            grid=(total,),
            in_specs=[
                held,
                pl.BlockSpec((rows, wide), lambda j, core: (0, jnp.minimum(j, split - 1))),
                held,
                pl.BlockSpec((rows, wide), lambda j, core: (0, jnp.clip(j - split, 0, last))),
            ],
            out_specs=[pl.BlockSpec((width // outputs, wide), lambda j, core: (0, j))] * outputs,
            scratch_shapes=[pltpu.VMEM((width, rows), jnp.bfloat16)],
        ),
        out_shape=[jax.ShapeDtypeStruct((width // outputs, wide * total), jnp.bfloat16)]
        * outputs,
        name="outer_pair",
        cost_estimate=pl.CostEstimate(
            flops=2 * rows * width * wide * total,
            transcendentals=0,
            bytes_accessed=2 * width * wide * total,
        ),
    )(core, left_a, right_a, left_b, right_b)


def local(
    block_in,
    segment_ids,
    mamba_z,
    mamba_x,
    mamba_bc,
    mamba_dt,
    mamba_out,
    attn_q,
    attn_kv,
    attn_out,
    ffn_gate,
    ffn_up,
    ffn_down,
    mixer_norm,
    ffn_norm,
    conv_weight,
    conv_bias,
    dt_bias,
    a_log,
    d_skip,
    inner_norm,
    grad_out,
):
    sequences, rows, width = block_in.shape
    length = segment_ids.shape[1]
    taps = conv_weight.shape[0]
    group = Q_HEADS // KV_HEADS
    inner_width = SSM_HEADS * SSM_HEAD
    total_rows = sequences * rows
    inv_root = HEAD ** (-0.5)
    offset = lax.axis_index("seq") * rows
    positions = offset + jnp.arange(rows, dtype=jnp.int32)
    local_ids = lax.dynamic_slice_in_dim(segment_ids, offset, rows, 1)
    padded_ids = jnp.concatenate(
        [jnp.full((sequences, taps - 1), -1, jnp.int32), segment_ids], axis=1
    )
    window_ids = lax.dynamic_slice_in_dim(padded_ids, offset, rows + taps - 1, 1)
    prior_id = window_ids[:, taps - 2]
    tap_masks = [
        (window_ids[:, tap : tap + rows] == local_ids).astype(jnp.float32)[:, :, None]
        for tap in range(taps)
    ]
    cosine, sine = rope_tables(positions, HEAD)
    cos_b = cosine[:, None, :]
    sin_b = sine[:, None, :]
    behind = min(lax.axis_size("seq") - 1, (MAX_DOC - 2) // rows + 1) * rows
    key_ids = lax.dynamic_slice_in_dim(
        jnp.concatenate([jnp.full((sequences, behind), -1, jnp.int32), segment_ids], axis=1),
        offset,
        behind + rows,
        1,
    )
    key_order = jnp.arange(behind + rows, dtype=jnp.int32) - behind
    allowed = (key_order[None, None, :] <= jnp.arange(rows, dtype=jnp.int32)[None, :, None]) & (
        key_ids[:, None, :] == local_ids[:, :, None]
    )
    hops = min(lax.axis_size("seq") - 1, (MAX_DOC - 2) // rows + 1)
    spare = -(mamba_dt.shape[1] + 2) % LANES
    shard_in = jnp.concatenate(
        [
            mamba_z,
            attn_q,
            mamba_x,
            mamba_bc,
            attn_kv,
            mamba_dt,
            mixer_norm[:, None],
            ffn_norm[:, None],
            jnp.zeros((mixer_norm.shape[0], spare), jnp.bfloat16),
        ],
        axis=1,
    )
    shard_out = jnp.concatenate([mamba_out, attn_out, ffn_gate, ffn_up, ffn_down], axis=1)
    held_in, shard_out = lax.optimization_barrier((chained_seq(shard_in), shard_out))
    full_in = lax.all_gather(held_in, ("dpo", "core"), axis=0, tiled=True)
    full_out = lax.all_gather(chained_seq(shard_out), ("dpo", "core"), axis=0, tiled=True)
    bc_width = mamba_bc.shape[1]
    q_width = attn_q.shape[1]
    kv_width = attn_kv.shape[1]
    hidden_width = ffn_gate.shape[1]
    at_q = inner_width
    at_u = at_q + q_width
    at_kv = at_u + inner_width + bc_width
    at_dt = at_kv + kv_width
    at_gain = at_dt + SSM_HEADS
    mixer_width = inner_width + q_width
    full_mixer = full_out[:, :mixer_width]
    full_gateup = full_out[:, mixer_width : mixer_width + 2 * hidden_width]
    full_down = full_out[:, mixer_width + 2 * hidden_width :]
    gain_one = full_in[:, at_gain].astype(jnp.float32)
    gain_two = full_in[:, at_gain + 1].astype(jnp.float32)
    x_in = block_in.reshape(total_rows, width).astype(jnp.float32)
    normed, factor_one = rms_forward(x_in, gain_one)
    normed_b = normed.astype(jnp.bfloat16)
    projected = matmul(normed_b, full_in)
    gate_z = projected[:, :at_q]
    inner_u = projected[:, at_u:at_kv]
    step_raw = projected[:, at_dt:at_gain]
    channels = inner_u.shape[1]
    conv_in = inner_u.reshape(sequences, rows, channels)
    edge_in = passed_along(conv_in[:, rows - taps + 1 :, :], "seq", 1)
    extended = jnp.concatenate([edge_in, conv_in], axis=1)
    conv_pre = jnp.zeros_like(conv_in) + conv_bias
    for tap in range(taps):
        conv_pre = conv_pre + conv_weight[tap] * extended[:, tap : tap + rows] * tap_masks[tap]
    activated = jax.nn.silu(conv_pre)
    act = activated.reshape(total_rows, channels)
    step = jax.nn.softplus(step_raw + dt_bias)
    ids = local_ids.reshape(total_rows)
    order = jnp.arange(rows)
    pair = (order[:, None] >= order[None, :]) & (ids[:, None] == ids[None, :])
    bias = jnp.where(pair, 0.0, -1e30).astype(jnp.float32)
    bias_turned = jnp.where(
        (order[:, None] <= order[None, :]) & (ids[:, None] == ids[None, :]), 0.0, -1e30
    ).astype(jnp.float32)
    inbound = (ids == prior_id[0]).astype(jnp.float32)[:, None]
    outbound = (ids == ids[-1]).astype(jnp.float32)[:, None]
    rate = -jnp.exp(a_log)
    ladder = (order[:, None] >= order[None, :]).astype(jnp.float32)
    decay = jnp.dot(ladder, step * rate, precision=lax.Precision.HIGHEST)
    entry = jnp.exp(decay) * inbound
    tail = jnp.exp(decay[-1:] - decay) * outbound
    carry = jnp.exp(decay[-1]) * inbound[-1, 0]
    cols = jnp.stack([decay, step, entry, tail], axis=1)
    cols = cols.reshape(rows, 4, SSM_PAIRS, 2).transpose(2, 0, 1, 3).reshape(SSM_PAIRS, rows, 8)
    turned = decay.T.reshape(SSM_PAIRS, 2, rows)
    skip_row = jnp.repeat(d_skip, SSM_HEAD)[None, :]
    carry_rows = jnp.repeat(carry, SSM_HEAD).reshape(SSM_PAIRS, LANES, 1)
    state_local = ssm_state(act, cols)
    outgoing = state_local
    for hop in range(hops):
        incoming = passed_along(outgoing.astype(jnp.bfloat16), "seq", 1)
        outgoing = carry_rows * incoming.astype(jnp.float32) + state_local
    local_part = ssm_local(act, cols, turned, bias)
    ssm_out, gated = ssm_carried(local_part, act, cols, incoming, skip_row, projected)
    silu_z = jax.nn.silu(gate_z)
    mixed_norm, factor_m = rms_forward(gated, inner_norm)
    mixed_b = mixed_norm.astype(jnp.bfloat16)
    query = projected[:, at_q:at_u].reshape(sequences, rows, Q_HEADS, HEAD)
    keyval = projected[:, at_kv:at_dt].reshape(sequences, rows, 2 * KV_HEADS, HEAD)
    query_b = rotate(query, cos_b, sin_b).astype(jnp.bfloat16)
    keys_local = rotate(keyval[:, :, :KV_HEADS], cos_b, sin_b)
    kv_local = jnp.concatenate([keys_local, keyval[:, :, KV_HEADS:]], axis=2).astype(jnp.bfloat16)
    kv_flat = kv_local.reshape(sequences, rows, kv_width)
    kv_all = jnp.concatenate(
        [passed_along(kv_flat, "seq", far) for far in range(hops, 0, -1)] + [kv_flat], axis=1
    )
    window = kv_all.shape[1]
    kv_all = kv_all.reshape(sequences, window, 2 * KV_HEADS, HEAD)
    keys = kv_all[:, :, :KV_HEADS]
    values = kv_all[:, :, KV_HEADS:]
    query_g = query_b.reshape(sequences, rows, KV_HEADS, group, HEAD)

    def attention_scores():
        raw = (
            jnp.einsum("stkgd,slkd->skgtl", query_g, keys, preferred_element_type=jnp.float32)
            * inv_root
        )
        return jnp.where(allowed[:, None, None], raw, -1e30)

    scores = attention_scores()
    top = jnp.max(scores, axis=-1, keepdims=True)
    lse = top + jnp.log(jnp.sum(jnp.exp(scores - top), axis=-1, keepdims=True))
    probs_b = jnp.exp(scores - lse).astype(jnp.bfloat16)
    attended = jnp.einsum("skgtl,slkd->stkgd", probs_b, values, preferred_element_type=jnp.float32)
    attended_b = attended.reshape(total_rows, Q_HEADS * HEAD).astype(jnp.bfloat16)
    mixers_b = jnp.concatenate([mixed_b, attended_b], axis=1)
    mid = x_in + matmul_nt(mixers_b, full_mixer)
    fnormed, factor_two = rms_forward(mid, gain_two)
    fnormed_b = fnormed.astype(jnp.bfloat16)
    gateup_h = matmul(fnormed_b, full_gateup)
    gate_h = gateup_h[:, :hidden_width]
    up_h = gateup_h[:, hidden_width:]
    hidden_b = (jax.nn.silu(gate_h) * up_h).astype(jnp.bfloat16)
    block_out = (
        (mid + matmul_nt(hidden_b, full_down)).astype(jnp.bfloat16).reshape(sequences, rows, width)
    )
    grad_flat = grad_out.reshape(total_rows, width)
    d_hidden = matmul(grad_flat, full_down)
    d_gate_b = (d_hidden * up_h * silu_grad(gate_h)).astype(jnp.bfloat16)
    d_up_b = (d_hidden * jax.nn.silu(gate_h)).astype(jnp.bfloat16)
    d_gateup_b = jnp.concatenate([d_gate_b, d_up_b], axis=1)
    part_ffn = scattered_dp(outer_pair(fnormed_b, d_gateup_b, grad_flat, hidden_b)[0])
    d_fnorm = matmul_nt(d_gateup_b, full_gateup)
    d_mid_norm, g_fnorm = rms_backward(mid, factor_two, gain_two, d_fnorm)
    d_mid = grad_flat.astype(jnp.float32) + d_mid_norm
    d_mid_b = d_mid.astype(jnp.bfloat16)
    d_mixers = matmul(d_mid_b, full_mixer)
    d_mnorm = d_mixers[:, :inner_width]
    d_gated, g_inner = rms_backward(gated, factor_m, inner_norm, d_mnorm)
    d_ssm = d_gated * silu_z
    d_z = d_gated * ssm_out * silu_grad(gate_z)
    direct = ssm_direct(d_ssm, act, cols)
    d_att_b = d_mixers[:, inner_width:].astype(jnp.bfloat16)
    d_att_g = d_att_b.reshape(sequences, rows, KV_HEADS, group, HEAD)
    probs = jnp.exp(attention_scores() - lse)
    d_probs = jnp.einsum("stkgd,slkd->skgtl", d_att_g, values, preferred_element_type=jnp.float32)
    d_scores_b = (probs * (d_probs - jnp.sum(probs * d_probs, axis=-1, keepdims=True))).astype(
        jnp.bfloat16
    )
    d_query = (
        jnp.einsum("skgtl,slkd->stkgd", d_scores_b, keys, preferred_element_type=jnp.float32)
        * inv_root
    )
    d_keys = (
        jnp.einsum("skgtl,stkgd->slkd", d_scores_b, query_g, preferred_element_type=jnp.float32)
        * inv_root
    )
    d_values = jnp.einsum("skgtl,stkgd->slkd", probs_b, d_att_g, preferred_element_type=jnp.float32)
    d_kv_all = jnp.concatenate([d_keys, d_values], axis=2).reshape(sequences, window, kv_width)
    d_kv_local = d_kv_all[:, window - rows :]
    for far in range(1, hops + 1):
        start = window - (far + 1) * rows
        term = d_kv_all[:, start : start + rows].astype(jnp.bfloat16)
        d_kv_local = d_kv_local + passed_along(term, "seq", -far).astype(jnp.float32)
    d_kv_local = d_kv_local.reshape(sequences, rows, 2 * KV_HEADS, HEAD)
    d_key_local = rotate_back(d_kv_local[:, :, :KV_HEADS], cos_b, sin_b)
    d_kv_b = (
        jnp.concatenate([d_key_local, d_kv_local[:, :, KV_HEADS:]], axis=2)
        .reshape(total_rows, 2 * KV_HEADS * HEAD)
        .astype(jnp.bfloat16)
    )
    d_q_b = (
        rotate_back(d_query.reshape(sequences, rows, Q_HEADS, HEAD), cos_b, sin_b)
        .reshape(total_rows, Q_HEADS * HEAD)
        .astype(jnp.bfloat16)
    )
    d_early = jnp.concatenate([d_z.astype(jnp.bfloat16), d_q_b], axis=1)
    early_own, early_other = outer_pair(normed_b, d_early, d_mid_b, mixers_b, 2)
    early_pair = paired_cores(early_own, early_other)
    backlog = direct
    for hop in range(hops):
        later_grad = passed_along(backlog.astype(jnp.bfloat16), "seq", -1)
        if hop == 0:
            later_grad, early_pair = lax.optimization_barrier((later_grad, early_pair))
        backlog = direct + carry_rows * later_grad.astype(jnp.float32)
    d_carry = jnp.sum(
        (later_grad.astype(jnp.float32) * incoming.astype(jnp.float32)).reshape(
            SSM_HEADS, SSM_HEAD, STATE
        ),
        axis=(1, 2),
    )
    part_early = scattered_own(early_pair)
    d_xs, d_bmat, d_cmat, d_cols, d_rows = ssm_backward(
        d_ssm, act, ssm_out, cols, turned, bias_turned, incoming, later_grad, skip_row
    )
    d_pairs = d_cols[:, :, :6].reshape(SSM_PAIRS, rows, 3, 2).transpose(2, 1, 0, 3)
    d_pairs = d_pairs.reshape(3, rows, SSM_HEADS)
    d_sums = jnp.sum(d_rows.reshape(SSM_PAIRS, 2, 2, SSM_HEAD), axis=3).transpose(1, 0, 2)
    d_sums = d_sums.reshape(2, SSM_HEADS)
    g_skip = d_sums[1]
    d_decay = d_pairs[0] - d_pairs[2]
    d_rise = jnp.dot(ladder.T, d_decay, precision=lax.Precision.HIGHEST)
    d_rise = d_rise + (d_sums[0] + d_carry * carry)
    d_step = d_pairs[1] + d_rise * rate
    g_alog = jnp.sum(d_rise * step, axis=0) * rate
    d_act = jnp.concatenate([d_xs, d_bmat, d_cmat], axis=1).reshape(sequences, rows, channels)
    d_act, part_ffn = lax.optimization_barrier((d_act, part_ffn))
    owned_ffn, _ = hopped_seq(part_ffn, None)
    d_pre = d_act * silu_grad(conv_pre)
    g_cbias = jnp.sum(d_pre, axis=(0, 1))
    g_cweight = jnp.stack(
        [
            jnp.sum(d_pre * extended[:, tap : tap + rows] * tap_masks[tap], axis=(0, 1))
            for tap in range(taps)
        ]
    )
    d_padded = jnp.zeros_like(extended)
    for tap in range(taps):
        d_padded = d_padded + jnp.pad(
            d_pre * tap_masks[tap] * conv_weight[tap], ((0, 0), (tap, taps - 1 - tap), (0, 0))
        )
    edge_grad = passed_along(d_padded[:, : taps - 1], "seq", -1)
    d_inner = d_padded[:, taps - 1 :] + jnp.pad(edge_grad, ((0, 0), (rows - taps + 1, 0), (0, 0)))
    d_inner = d_inner.reshape(total_rows, channels)
    d_step_raw = d_step.reshape(total_rows, SSM_HEADS) * jax.nn.sigmoid(step_raw + dt_bias)
    g_dtb = jnp.sum(d_step_raw, axis=0)
    d_x_b = d_inner[:, :inner_width].astype(jnp.bfloat16)
    d_bc_b = d_inner[:, inner_width:].astype(jnp.bfloat16)
    d_st_b = d_step_raw.astype(jnp.bfloat16)
    d_late = jnp.concatenate(
        [
            d_x_b,
            d_bc_b,
            d_kv_b,
            d_st_b,
            jnp.zeros((total_rows, spare + 2), jnp.bfloat16),
        ],
        axis=1,
    )
    late_own, late_other = outer_pair(normed_b, d_late, None, None, 2)
    late_pair = paired_cores(late_own, late_other)
    d_norm = matmul_nt(d_early, full_in[:, :at_u]) + matmul_nt(d_late, full_in[:, at_u:])
    d_in_norm, g_mnorm = rms_backward(x_in, factor_one, gain_one, d_norm)
    grad_in = (d_mid + d_in_norm).astype(jnp.bfloat16).reshape(sequences, rows, width)
    smalls = jnp.concatenate([g_dtb, g_alog, g_skip])
    strips = [g_inner, g_mnorm, g_fnorm, smalls]
    packed = jnp.concatenate(
        [g_cweight, g_cbias[None]]
        + [jnp.pad(strip, (0, channels - strip.shape[0]))[None] for strip in strips],
        axis=0,
    )
    packed, late_pair = lax.optimization_barrier((packed, late_pair))
    part_late = scattered_own(late_pair)
    summed = summed_everywhere(packed)
    gain_rows = mixer_norm.shape[0]
    part_early, summed, grad_in = lax.optimization_barrier((part_early, summed, grad_in))
    owned_early, part_late = hopped_seq(part_early, part_late)
    owned_late = scattered_seq(part_late)
    owner = lax.axis_index("dpo") * 2 + lax.axis_index("core")
    first_row = (owner * lax.axis_size("seq") + lax.axis_index("seq")) * gain_rows
    g_mnorm_own = lax.dynamic_slice_in_dim(summed[taps + 2], first_row, gain_rows, 0)
    g_fnorm_own = lax.dynamic_slice_in_dim(summed[taps + 3], first_row, gain_rows, 0)
    at_mixers = at_u
    late_kv = at_kv - at_u
    late_dt = at_dt - at_u
    return (
        block_out,
        grad_in,
        owned_early[:, :at_q],
        owned_late[:, :inner_width],
        owned_late[:, inner_width:late_kv],
        owned_late[:, late_dt : late_dt + SSM_HEADS],
        owned_early[:, at_mixers : at_mixers + inner_width],
        owned_early[:, at_q:at_u],
        owned_late[:, late_kv:late_dt],
        owned_early[:, at_mixers + inner_width :],
        owned_ffn[:, :hidden_width],
        owned_ffn[:, hidden_width : 2 * hidden_width],
        owned_ffn[:, 2 * hidden_width :],
        g_mnorm_own,
        g_fnorm_own,
        summed[:taps],
        summed[taps],
        summed[taps + 4, :SSM_HEADS],
        summed[taps + 4, SSM_HEADS : 2 * SSM_HEADS],
        summed[taps + 4, 2 * SSM_HEADS : 3 * SSM_HEADS],
        summed[taps + 1, :inner_width],
    )


def solution(mesh):
    grid = mesh.devices
    mesh = Mesh(grid.reshape(grid.shape[0] // 2, 2, grid.shape[1]), DP + ("seq",))
    in_specs = (
        P(DP, "seq", None),
        P(DP, None),
        P(DP + ("seq",), None),
        P(DP + ("seq",), None),
        P(DP + ("seq",), None),
        P(DP + ("seq",), None),
        P(DP + ("seq",), None),
        P(DP + ("seq",), None),
        P(DP + ("seq",), None),
        P(DP + ("seq",), None),
        P(DP + ("seq",), None),
        P(DP + ("seq",), None),
        P(DP + ("seq",), None),
        P(DP + ("seq",)),
        P(DP + ("seq",)),
        P(),
        P(),
        P(),
        P(),
        P(),
        P(),
        P(DP, "seq", None),
    )
    out_specs = (
        P(DP, "seq", None),
        P(DP, "seq", None),
        P(DP + ("seq",), None),
        P(DP + ("seq",), None),
        P(DP + ("seq",), None),
        P(DP + ("seq",), None),
        P(DP + ("seq",), None),
        P(DP + ("seq",), None),
        P(DP + ("seq",), None),
        P(DP + ("seq",), None),
        P(DP + ("seq",), None),
        P(DP + ("seq",), None),
        P(DP + ("seq",), None),
        P(DP + ("seq",)),
        P(DP + ("seq",)),
        P(),
        P(),
        P(),
        P(),
        P(),
        P(),
    )
    return jax.shard_map(local, mesh=mesh, in_specs=in_specs, out_specs=out_specs, check_vma=False)
```

```python
import functools
import math

import jax
import jax.numpy as jnp
from jax import lax
from jax.experimental import pallas as pl
from jax.experimental.pallas import tpu as pltpu
from jax.sharding import Mesh
from jax.sharding import PartitionSpec as P

SSM_HEADS = 24
SSM_HEAD = 64
STATE = 128
Q_HEADS = 8
KV_HEADS = 2
HEAD = 64


EPSILON = 1e-05
ROPE_BASE = 100000000000.0
MAX_DOC = 512
LANES = 128
SSM_PAIRS = SSM_HEADS * SSM_HEAD // LANES
PAIR_GROUP = 4
DP = ("dpo", "core")


def passed_along(block, axis, distance):
    devices = range(lax.axis_size(axis))
    route = [(i - distance, i) for i in devices if i - distance in devices]
    return lax.ppermute(block, axis, route)


def scattered_dp(grad):
    return lax.psum_scatter(grad, ("dpo", "core"), scatter_dimension=0, tiled=True)


def swapped(block):
    return lax.ppermute(block, "core", [(0, 1), (1, 0)])


def paired_cores(own, other):
    return (own.astype(jnp.float32) + swapped(other).astype(jnp.float32)).astype(jnp.bfloat16)


def scattered_own(paired):
    return lax.psum_scatter(paired, "dpo", scatter_dimension=0, tiled=True)


def summed_everywhere(block):
    for axis in ("core", "dpo", "seq"):
        count = lax.axis_size(axis)
        bit = 1
        while bit < count:
            block = block + lax.ppermute(block, axis, [(i, i ^ bit) for i in range(count)])
            bit *= 2
    return block


def scattered_seq(part):
    return lax.psum_scatter(part, "seq", scatter_dimension=0, tiled=True).astype(jnp.float32)


def chained_seq(shard):
    count = lax.axis_size("seq")
    before = [shard]
    after = [shard]
    for hop in range(count - 1):
        before.append(passed_along(before[-1], "seq", 1))
        after.append(passed_along(after[-1], "seq", -1))
    line = jnp.concatenate(before[:0:-1] + after, axis=0)
    rows = shard.shape[0]
    start = (count - 1 - lax.axis_index("seq")) * rows
    return lax.dynamic_slice_in_dim(line, start, count * rows, 0)


def hopped_seq(part, rider):
    index = lax.axis_index("seq")
    count = lax.axis_size("seq")
    held = part.reshape(count, part.shape[0] // count, part.shape[1])
    bit = 1
    while bit < count:
        halves = held.reshape(held.shape[0] // 2, 2, *held.shape[1:])
        odd = (index // bit) % 2 == 1
        mine = jnp.where(odd, halves[:, 1], halves[:, 0])
        other = jnp.where(odd, halves[:, 0], halves[:, 1])
        got = lax.ppermute(other, "seq", [(i, i ^ bit) for i in range(count)])
        held = mine.astype(jnp.float32) + got.astype(jnp.float32)
        bit *= 2
        if bit < count:
            held = held.astype(jnp.bfloat16)
        if bit == 2 and rider is not None:
            held, rider = lax.optimization_barrier((held, rider))
    return held[0].astype(jnp.float32), rider


def silu_grad(value):
    sigma = jax.nn.sigmoid(value)
    return sigma * (1.0 + value * (1.0 - sigma))


def rms_forward(value, gain):
    factor = lax.rsqrt(jnp.mean(value * value, axis=-1, keepdims=True) + EPSILON)
    return (value * factor * gain, factor)


def rms_backward(value, factor, gain, upstream):
    weighted = upstream * gain
    gain_grad = jnp.sum(upstream * value * factor, axis=0)
    inward = factor * weighted - value * factor * factor * factor * jnp.mean(
        weighted * value, axis=-1, keepdims=True
    )
    return (inward, gain_grad)


def matmul(left, right):
    return jnp.dot(left, right, preferred_element_type=jnp.float32)


def matmul_nt(left, right):
    return lax.dot_general(
        left, right, (((1,), (1,)), ((), ())), preferred_element_type=jnp.float32
    )


def matmul_tn(left, right):
    return lax.dot_general(
        left, right, (((0,), (0,)), ((), ())), preferred_element_type=jnp.float32
    )


def rope_tables(positions, head_size):
    half = head_size // 2
    freq_scale = ROPE_BASE ** (-jnp.arange(half, dtype=jnp.float32) / half)
    angles = positions.astype(jnp.float32)[:, None] * freq_scale[None, :]
    return (jnp.cos(angles), jnp.sin(angles))


def rotate(value, cosine, sine):
    half = value.shape[-1] // 2
    first = value[..., :half]
    second = value[..., half:]
    return jnp.concatenate(
        [first * cosine - second * sine, second * cosine + first * sine], axis=-1
    )


def rotate_back(grad, cosine, sine):
    half = grad.shape[-1] // 2
    first = grad[..., :half]
    second = grad[..., half:]
    return jnp.concatenate(
        [first * cosine + second * sine, second * cosine - first * sine], axis=-1
    )


def half_lanes(cols, first, shape):
    lane = lax.broadcasted_iota(jnp.int32, shape, 1)
    return jnp.where(lane < SSM_HEAD, cols[:, first : first + 1], cols[:, first + 1 : first + 2])


def dot_nn(left, right):
    return lax.dot_general(
        left, right, (((1,), (0,)), ((), ())), preferred_element_type=jnp.float32
    )


def each_pair(body):
    for k in range(PAIR_GROUP):
        body(k, pl.ds(k * LANES, LANES))


def ssm_state_kernel(xs_ref, b_ref, cols_ref, state_ref):
    b_low = b_ref[...].astype(jnp.bfloat16)

    def one(k, lanes):
        xs = xs_ref[:, lanes]
        cols = cols_ref[k]
        scaled = xs * half_lanes(cols, 2, xs.shape)
        tailed = (scaled * half_lanes(cols, 6, xs.shape)).astype(jnp.bfloat16)
        state_ref[k] = lax.dot_general(
            tailed, b_low, (((0,), (0,)), ((), ())), preferred_element_type=jnp.float32
        )

    each_pair(one)


def ssm_local_kernel(xs_ref, b_ref, c_ref, cols_ref, rows_ref, bias_ref, out_ref, cb_ref):
    bmat = b_ref[...]

    @pl.when(pl.program_id(0) == 0)
    def _():
        cb_ref[...] = lax.dot_general(
            c_ref[...],
            bmat,
            (((1,), (1,)), ((), ())),
            precision=lax.Precision.HIGHEST,
            preferred_element_type=jnp.float32,
        )

    def one(k, lanes):
        xs = xs_ref[:, lanes]
        cols = cols_ref[k]
        rows = rows_ref[k]
        scaled_b = (xs * half_lanes(cols, 2, xs.shape)).astype(jnp.bfloat16)
        parts = []
        for h in range(2):
            kernel = jnp.exp(cols[:, h : h + 1] - rows[h : h + 1, :] + bias_ref[...])
            parts.append(dot_nn((kernel * cb_ref[...]).astype(jnp.bfloat16), scaled_b))
        lane = lax.broadcasted_iota(jnp.int32, xs.shape, 1)
        out_ref[:, lanes] = jnp.where(lane < SSM_HEAD, parts[0], parts[1])

    each_pair(one)


def ssm_carry_kernel(local_ref, xs_ref, c_ref, cols_ref, state_ref, skip_ref, z_ref, out_ref, gated_ref):
    c_low = c_ref[...].astype(jnp.bfloat16)

    def one(k, lanes):
        xs = xs_ref[:, lanes]
        carried = lax.dot_general(
            c_low, state_ref[k], (((1,), (1,)), ((), ())), preferred_element_type=jnp.float32
        )
        entry = half_lanes(cols_ref[k], 4, xs.shape)
        out = local_ref[:, lanes] + entry * carried + skip_ref[:, lanes] * xs
        out_ref[:, lanes] = out
        gate = z_ref[:, lanes]
        gated_ref[:, lanes] = out * (gate * jax.nn.sigmoid(gate))

    each_pair(one)


def ssm_direct_kernel(g_ref, c_ref, cols_ref, direct_ref):
    c_low = c_ref[...].astype(jnp.bfloat16)

    def one(k, lanes):
        g = g_ref[:, lanes]
        entered = (g * half_lanes(cols_ref[k], 4, g.shape)).astype(jnp.bfloat16)
        direct_ref[k] = lax.dot_general(
            entered, c_low, (((0,), (0,)), ((), ())), preferred_element_type=jnp.float32
        )

    each_pair(one)


def ssm_backward_kernel(
    g_ref,
    xs_ref,
    out_ref,
    b_ref,
    c_ref,
    cols_ref,
    rows_ref,
    bias_ref,
    state_ref,
    later_ref,
    skip_ref,
    dxs_ref,
    db_ref,
    dc_ref,
    dcols_ref,
    drows_ref,
    cb_ref,
    dcb_ref,
):
    pair = pl.program_id(0)
    bmat = b_ref[...]
    cmat = c_ref[...]
    b_low = bmat.astype(jnp.bfloat16)
    c_low = cmat.astype(jnp.bfloat16)

    @pl.when(pair == 0)
    def _():
        cb_ref[...] = lax.dot_general(
            bmat,
            cmat,
            (((1,), (1,)), ((), ())),
            precision=lax.Precision.HIGHEST,
            preferred_element_type=jnp.float32,
        )
        dcb_ref[...] = jnp.zeros_like(dcb_ref)
        db_ref[...] = jnp.zeros_like(db_ref)
        dc_ref[...] = jnp.zeros_like(dc_ref)

    def one(at, lanes):
        g = g_ref[:, lanes]
        xs = xs_ref[:, lanes]
        skip = skip_ref[:, lanes]
        cols = cols_ref[at]
        rows = rows_ref[at]
        step = half_lanes(cols, 2, xs.shape)
        tail = half_lanes(cols, 6, xs.shape)
        lane = lax.broadcasted_iota(jnp.int32, xs.shape, 1)
        first = lane < SSM_HEAD
        g_low = g.astype(jnp.bfloat16)
        scaled = xs * step
        parts = []
        total = dcb_ref[...]
        for k in range(2):
            mine = first if k == 0 else jnp.logical_not(first)
            kernel = jnp.exp(rows[k : k + 1, :] - cols[:, k : k + 1] + bias_ref[...])
            parts.append(dot_nn((kernel * cb_ref[...]).astype(jnp.bfloat16), g_low))
            crossed = lax.dot_general(
                jnp.where(mine, scaled, 0.0).astype(jnp.bfloat16),
                g_low,
                (((1,), (1,)), ((), ())),
                preferred_element_type=jnp.float32,
            )
            total = total + crossed * kernel
        dcb_ref[...] = total
        later = later_ref[at]
        swept = tail * lax.dot_general(
            b_low, later, (((1,), (1,)), ((), ())), preferred_element_type=jnp.float32
        )
        inner = jnp.where(first, parts[0], parts[1]) + swept
        dxs_ref[:, lanes] = step * inner + skip * g
        db_ref[...] += dot_nn((scaled * tail).astype(jnp.bfloat16), later)
        entered = (g * half_lanes(cols, 4, g.shape)).astype(jnp.bfloat16)
        dc_ref[...] += dot_nn(entered, state_ref[at])
        rose = g_low.astype(jnp.float32) * (out_ref[:, lanes] - skip * xs)
        stepped = xs * inner
        kept = scaled.astype(jnp.bfloat16).astype(jnp.float32)
        fell = kept * (inner - swept) + scaled * swept
        columns = [
            jnp.sum(jnp.where(first, value, 0.0), axis=1, keepdims=True)
            if k == 0
            else jnp.sum(jnp.where(first, 0.0, value), axis=1, keepdims=True)
            for value in (rose, stepped, fell)
            for k in range(2)
        ]
        spot = lax.broadcasted_iota(jnp.int32, cols.shape, 1)
        packed = jnp.zeros_like(cols)
        for index, column in enumerate(columns):
            packed = jnp.where(spot == index, column, packed)
        dcols_ref[at] = packed
        drows_ref[at, 0:1, :] = jnp.sum(scaled * swept, axis=0, keepdims=True)
        drows_ref[at, 1:2, :] = jnp.sum(g * xs, axis=0, keepdims=True)

    each_pair(one)

    @pl.when(pair == pl.num_programs(0) - 1)
    def _():
        low = dcb_ref[...].astype(jnp.bfloat16)
        db_ref[...] += dot_nn(low, c_low)
        dc_ref[...] += lax.dot_general(
            low, b_low, (((0,), (0,)), ((), ())), preferred_element_type=jnp.float32
        )


def ssm_specs(rows):
    wide = PAIR_GROUP * LANES
    block = pl.BlockSpec((rows, wide), lambda p: (0, p))
    bmat = pl.BlockSpec((rows, LANES), lambda p: (0, SSM_PAIRS))
    cmat = pl.BlockSpec((rows, LANES), lambda p: (0, SSM_PAIRS + 1))
    cols = pl.BlockSpec((PAIR_GROUP, rows, 8), lambda p: (p, 0, 0))
    turned = pl.BlockSpec((PAIR_GROUP, 2, rows), lambda p: (p, 0, 0))
    bias = pl.BlockSpec((rows, rows), lambda p: (0, 0))
    state = pl.BlockSpec((PAIR_GROUP, LANES, STATE), lambda p: (p, 0, 0))
    skip = pl.BlockSpec((1, wide), lambda p: (0, p))
    whole = pl.BlockSpec((rows, LANES), lambda p: (0, 0))
    return block, bmat, cmat, cols, turned, bias, state, skip, whole


def ssm_state(act, cols):
    rows = act.shape[0]
    block, bmat, cmat, col, turn, square, state, skip, whole = ssm_specs(rows)
    return pl.pallas_call(
        ssm_state_kernel,
        grid=(SSM_PAIRS // PAIR_GROUP,),
        in_specs=[block, bmat, col],
        out_specs=state,
        out_shape=jax.ShapeDtypeStruct((SSM_PAIRS, LANES, STATE), jnp.float32),
        name="ssm_state",
        cost_estimate=pl.CostEstimate(flops=10**8, transcendentals=0, bytes_accessed=4 * 10**6),
    )(act, act, cols)


def ssm_local(act, cols, turned, bias):
    rows = act.shape[0]
    block, bmat, cmat, col, turn, square, state, skip, whole = ssm_specs(rows)
    return pl.pallas_call(
        ssm_local_kernel,
        grid=(SSM_PAIRS // PAIR_GROUP,),
        in_specs=[block, bmat, cmat, col, turn, square],
        out_specs=block,
        out_shape=jax.ShapeDtypeStruct((rows, SSM_PAIRS * LANES), jnp.float32),
        scratch_shapes=[pltpu.VMEM((rows, rows), jnp.float32)],
        name="ssm_local",
        cost_estimate=pl.CostEstimate(flops=10**9, transcendentals=24 * rows * rows, bytes_accessed=6 * 10**6),
    )(act, act, act, cols, turned, bias)


def ssm_carried(local_part, act, cols, state, skip_row, projected):
    rows = act.shape[0]
    block, bmat, cmat, col, turn, square, states, skip, whole = ssm_specs(rows)
    shape = jax.ShapeDtypeStruct((rows, SSM_PAIRS * LANES), jnp.float32)
    return pl.pallas_call(
        ssm_carry_kernel,
        grid=(SSM_PAIRS // PAIR_GROUP,),
        in_specs=[block, block, cmat, col, states, skip, block],
        out_specs=[block, block],
        out_shape=[shape, shape],
        name="ssm_carried",
        cost_estimate=pl.CostEstimate(flops=10**8, transcendentals=rows * 1536, bytes_accessed=9 * 10**6),
    )(local_part, act, act, cols, state, skip_row, projected)


def ssm_direct(g, act, cols):
    rows = act.shape[0]
    block, bmat, cmat, col, turn, square, states, skip, whole = ssm_specs(rows)
    return pl.pallas_call(
        ssm_direct_kernel,
        grid=(SSM_PAIRS // PAIR_GROUP,),
        in_specs=[block, cmat, col],
        out_specs=states,
        out_shape=jax.ShapeDtypeStruct((SSM_PAIRS, LANES, STATE), jnp.float32),
        name="ssm_direct",
        cost_estimate=pl.CostEstimate(flops=10**8, transcendentals=0, bytes_accessed=4 * 10**6),
    )(g, act, cols)


def ssm_backward(g, act, out, cols, turned, bias_turned, state, later, skip_row):
    rows = act.shape[0]
    block, bmat, cmat, col, turn, square, states, skip, whole = ssm_specs(rows)
    return pl.pallas_call(
        ssm_backward_kernel,
        grid=(SSM_PAIRS // PAIR_GROUP,),
        in_specs=[block, block, block, bmat, cmat, col, turn, square, states, states, skip],
        out_specs=[block, whole, whole, col, pl.BlockSpec((PAIR_GROUP, 2, LANES), lambda p: (p, 0, 0))],
        out_shape=[
            jax.ShapeDtypeStruct((rows, SSM_PAIRS * LANES), jnp.float32),
            jax.ShapeDtypeStruct((rows, STATE), jnp.float32),
            jax.ShapeDtypeStruct((rows, STATE), jnp.float32),
            jax.ShapeDtypeStruct((SSM_PAIRS, rows, 8), jnp.float32),
            jax.ShapeDtypeStruct((SSM_PAIRS, 2, LANES), jnp.float32),
        ],
        scratch_shapes=[pltpu.VMEM((rows, rows), jnp.float32)] * 2,
        name="ssm_backward",
        cost_estimate=pl.CostEstimate(flops=2 * 10**9, transcendentals=24 * rows * rows, bytes_accessed=12 * 10**6),
    )(g, act, out, act, act, cols, turned, bias_turned, state, later, skip_row)


def outer_kernel(split, blocks, core_ref, left_a_ref, right_a_ref, left_b_ref, right_b_ref, *rest):
    outs, turned_ref = rest[:-1], rest[-1]
    step = pl.program_id(0)

    def turn(left_ref):
        turned = left_ref[...].T
        if len(outs) == 1:
            turned_ref[...] = turned
            return
        tall = turned.shape[0] // (2 * blocks)
        second = core_ref[0] == 1
        for block in range(blocks):
            low = turned[2 * block * tall : (2 * block + 1) * tall]
            high = turned[(2 * block + 1) * tall : (2 * block + 2) * tall]
            turned_ref[pl.ds(block * tall, tall), :] = jnp.where(second, high, low)
            turned_ref[pl.ds((blocks + block) * tall, tall), :] = jnp.where(second, low, high)

    @pl.when(step == 0)
    def _():
        turn(left_a_ref)

    @pl.when(step == split)
    def _():
        turn(left_b_ref)

    def filled(right_ref):
        wide = right_ref.shape[1]
        piece = math.gcd(wide, 256)
        for at in range(0, wide, piece):
            lanes = pl.ds(at, piece)
            product = dot_nn(turned_ref[...], right_ref[:, lanes]).astype(jnp.bfloat16)
            for place, out_ref in enumerate(outs):
                tall = out_ref.shape[0]
                out_ref[:, lanes] = product[place * tall : (place + 1) * tall]

    @pl.when(step < split)
    def _():
        filled(right_a_ref)

    @pl.when(step >= split)
    def _():
        filled(right_b_ref)


def outer_pair(left_a, right_a, left_b, right_b, outputs=1):
    rows, width = left_a.shape
    wide_a = right_a.shape[1]
    wide_b = 0 if right_b is None else right_b.shape[1]
    wide = math.gcd(math.gcd(wide_a, wide_b), 1024) if wide_b else wide_a
    split = wide_a // wide
    total = split + wide_b // wide
    held = pl.BlockSpec((rows, width), lambda j, core: (0, 0))
    core = lax.axis_index("core").astype(jnp.int32).reshape(1)
    if right_b is None:
        left_b, right_b = left_a, right_a
    last = right_b.shape[1] // wide - 1
    return pl.pallas_call(
        functools.partial(outer_kernel, split, lax.axis_size("dpo")),
        grid_spec=pltpu.PrefetchScalarGridSpec(
            num_scalar_prefetch=1,
            grid=(total,),
            in_specs=[
                held,
                pl.BlockSpec((rows, wide), lambda j, core: (0, jnp.minimum(j, split - 1))),
                held,
                pl.BlockSpec((rows, wide), lambda j, core: (0, jnp.clip(j - split, 0, last))),
            ],
            out_specs=[pl.BlockSpec((width // outputs, wide), lambda j, core: (0, j))] * outputs,
            scratch_shapes=[pltpu.VMEM((width, rows), jnp.bfloat16)],
        ),
        out_shape=[jax.ShapeDtypeStruct((width // outputs, wide * total), jnp.bfloat16)]
        * outputs,
        name="outer_pair",
        cost_estimate=pl.CostEstimate(
            flops=2 * rows * width * wide * total,
            transcendentals=0,
            bytes_accessed=2 * width * wide * total,
        ),
    )(core, left_a, right_a, left_b, right_b)


def local(
    block_in,
    segment_ids,
    mamba_z,
    mamba_x,
    mamba_bc,
    mamba_dt,
    mamba_out,
    attn_q,
    attn_kv,
    attn_out,
    ffn_gate,
    ffn_up,
    ffn_down,
    mixer_norm,
    ffn_norm,
    conv_weight,
    conv_bias,
    dt_bias,
    a_log,
    d_skip,
    inner_norm,
    grad_out,
):
    sequences, rows, width = block_in.shape
    length = segment_ids.shape[1]
    taps = conv_weight.shape[0]
    group = Q_HEADS // KV_HEADS
    inner_width = SSM_HEADS * SSM_HEAD
    total_rows = sequences * rows
    inv_root = HEAD ** (-0.5)
    offset = lax.axis_index("seq") * rows
    positions = offset + jnp.arange(rows, dtype=jnp.int32)
    local_ids = lax.dynamic_slice_in_dim(segment_ids, offset, rows, 1)
    padded_ids = jnp.concatenate(
        [jnp.full((sequences, taps - 1), -1, jnp.int32), segment_ids], axis=1
    )
    window_ids = lax.dynamic_slice_in_dim(padded_ids, offset, rows + taps - 1, 1)
    prior_id = window_ids[:, taps - 2]
    tap_masks = [
        (window_ids[:, tap : tap + rows] == local_ids).astype(jnp.float32)[:, :, None]
        for tap in range(taps)
    ]
    cosine, sine = rope_tables(positions, HEAD)
    cos_b = cosine[:, None, :]
    sin_b = sine[:, None, :]
    behind = min(lax.axis_size("seq") - 1, (MAX_DOC - 2) // rows + 1) * rows
    key_ids = lax.dynamic_slice_in_dim(
        jnp.concatenate([jnp.full((sequences, behind), -1, jnp.int32), segment_ids], axis=1),
        offset,
        behind + rows,
        1,
    )
    key_order = jnp.arange(behind + rows, dtype=jnp.int32) - behind
    allowed = (key_order[None, None, :] <= jnp.arange(rows, dtype=jnp.int32)[None, :, None]) & (
        key_ids[:, None, :] == local_ids[:, :, None]
    )
    hops = min(lax.axis_size("seq") - 1, (MAX_DOC - 2) // rows + 1)
    spare = -(mamba_dt.shape[1] + 2) % LANES
    shard_in = jnp.concatenate(
        [
            mamba_z,
            attn_q,
            mamba_x,
            mamba_bc,
            attn_kv,
            mamba_dt,
            mixer_norm[:, None],
            ffn_norm[:, None],
            jnp.zeros((mixer_norm.shape[0], spare), jnp.bfloat16),
        ],
        axis=1,
    )
    shard_out = jnp.concatenate([mamba_out, attn_out, ffn_gate, ffn_up, ffn_down], axis=1)
    held_in, shard_out = lax.optimization_barrier((chained_seq(shard_in), shard_out))
    full_in = lax.all_gather(held_in, ("dpo", "core"), axis=0, tiled=True)
    full_out = lax.all_gather(chained_seq(shard_out), ("dpo", "core"), axis=0, tiled=True)
    bc_width = mamba_bc.shape[1]
    q_width = attn_q.shape[1]
    kv_width = attn_kv.shape[1]
    hidden_width = ffn_gate.shape[1]
    at_q = inner_width
    at_u = at_q + q_width
    at_kv = at_u + inner_width + bc_width
    at_dt = at_kv + kv_width
    at_gain = at_dt + SSM_HEADS
    mixer_width = inner_width + q_width
    full_mixer = full_out[:, :mixer_width]
    full_gateup = full_out[:, mixer_width : mixer_width + 2 * hidden_width]
    full_down = full_out[:, mixer_width + 2 * hidden_width :]
    gain_one = full_in[:, at_gain].astype(jnp.float32)
    gain_two = full_in[:, at_gain + 1].astype(jnp.float32)
    x_in = block_in.reshape(total_rows, width).astype(jnp.float32)
    normed, factor_one = rms_forward(x_in, gain_one)
    normed_b = normed.astype(jnp.bfloat16)
    projected = matmul(normed_b, full_in)
    gate_z = projected[:, :at_q]
    inner_u = projected[:, at_u:at_kv]
    step_raw = projected[:, at_dt:at_gain]
    channels = inner_u.shape[1]
    conv_in = inner_u.reshape(sequences, rows, channels)
    edge_in = passed_along(conv_in[:, rows - taps + 1 :, :], "seq", 1)
    extended = jnp.concatenate([edge_in, conv_in], axis=1)
    conv_pre = jnp.zeros_like(conv_in) + conv_bias
    for tap in range(taps):
        conv_pre = conv_pre + conv_weight[tap] * extended[:, tap : tap + rows] * tap_masks[tap]
    activated = jax.nn.silu(conv_pre)
    act = activated.reshape(total_rows, channels)
    step = jax.nn.softplus(step_raw + dt_bias)
    ids = local_ids.reshape(total_rows)
    order = jnp.arange(rows)
    pair = (order[:, None] >= order[None, :]) & (ids[:, None] == ids[None, :])
    bias = jnp.where(pair, 0.0, -1e30).astype(jnp.float32)
    bias_turned = jnp.where(
        (order[:, None] <= order[None, :]) & (ids[:, None] == ids[None, :]), 0.0, -1e30
    ).astype(jnp.float32)
    inbound = (ids == prior_id[0]).astype(jnp.float32)[:, None]
    outbound = (ids == ids[-1]).astype(jnp.float32)[:, None]
    rate = -jnp.exp(a_log)
    ladder = (order[:, None] >= order[None, :]).astype(jnp.float32)
    decay = jnp.dot(ladder, step * rate, precision=lax.Precision.HIGHEST)
    entry = jnp.exp(decay) * inbound
    tail = jnp.exp(decay[-1:] - decay) * outbound
    carry = jnp.exp(decay[-1]) * inbound[-1, 0]
    cols = jnp.stack([decay, step, entry, tail], axis=1)
    cols = cols.reshape(rows, 4, SSM_PAIRS, 2).transpose(2, 0, 1, 3).reshape(SSM_PAIRS, rows, 8)
    turned = decay.T.reshape(SSM_PAIRS, 2, rows)
    skip_row = jnp.repeat(d_skip, SSM_HEAD)[None, :]
    carry_rows = jnp.repeat(carry, SSM_HEAD).reshape(SSM_PAIRS, LANES, 1)
    state_local = ssm_state(act, cols)
    outgoing = state_local
    for hop in range(hops):
        incoming = passed_along(outgoing.astype(jnp.bfloat16), "seq", 1)
        outgoing = carry_rows * incoming.astype(jnp.float32) + state_local
    local_part = ssm_local(act, cols, turned, bias)
    ssm_out, gated = ssm_carried(local_part, act, cols, incoming, skip_row, projected)
    silu_z = jax.nn.silu(gate_z)
    mixed_norm, factor_m = rms_forward(gated, inner_norm)
    mixed_b = mixed_norm.astype(jnp.bfloat16)
    query = projected[:, at_q:at_u].reshape(sequences, rows, Q_HEADS, HEAD)
    keyval = projected[:, at_kv:at_dt].reshape(sequences, rows, 2 * KV_HEADS, HEAD)
    query_b = rotate(query, cos_b, sin_b).astype(jnp.bfloat16)
    keys_local = rotate(keyval[:, :, :KV_HEADS], cos_b, sin_b)
    kv_local = jnp.concatenate([keys_local, keyval[:, :, KV_HEADS:]], axis=2).astype(jnp.bfloat16)
    kv_flat = kv_local.reshape(sequences, rows, kv_width)
    kv_all = jnp.concatenate(
        [passed_along(kv_flat, "seq", far) for far in range(hops, 0, -1)] + [kv_flat], axis=1
    )
    window = kv_all.shape[1]
    kv_all = kv_all.reshape(sequences, window, 2 * KV_HEADS, HEAD)
    keys = kv_all[:, :, :KV_HEADS]
    values = kv_all[:, :, KV_HEADS:]
    query_g = query_b.reshape(sequences, rows, KV_HEADS, group, HEAD)

    def attention_scores():
        raw = (
            jnp.einsum("stkgd,slkd->skgtl", query_g, keys, preferred_element_type=jnp.float32)
            * inv_root
        )
        return jnp.where(allowed[:, None, None], raw, -1e30)

    scores = attention_scores()
    top = jnp.max(scores, axis=-1, keepdims=True)
    lse = top + jnp.log(jnp.sum(jnp.exp(scores - top), axis=-1, keepdims=True))
    probs_b = jnp.exp(scores - lse).astype(jnp.bfloat16)
    attended = jnp.einsum("skgtl,slkd->stkgd", probs_b, values, preferred_element_type=jnp.float32)
    attended_b = attended.reshape(total_rows, Q_HEADS * HEAD).astype(jnp.bfloat16)
    mixers_b = jnp.concatenate([mixed_b, attended_b], axis=1)
    mid = x_in + matmul_nt(mixers_b, full_mixer)
    fnormed, factor_two = rms_forward(mid, gain_two)
    fnormed_b = fnormed.astype(jnp.bfloat16)
    gateup_h = matmul(fnormed_b, full_gateup)
    gate_h = gateup_h[:, :hidden_width]
    up_h = gateup_h[:, hidden_width:]
    hidden_b = (jax.nn.silu(gate_h) * up_h).astype(jnp.bfloat16)
    block_out = (
        (mid + matmul_nt(hidden_b, full_down)).astype(jnp.bfloat16).reshape(sequences, rows, width)
    )
    grad_flat = grad_out.reshape(total_rows, width)
    d_hidden = matmul(grad_flat, full_down)
    d_gate_b = (d_hidden * up_h * silu_grad(gate_h)).astype(jnp.bfloat16)
    d_up_b = (d_hidden * jax.nn.silu(gate_h)).astype(jnp.bfloat16)
    d_gateup_b = jnp.concatenate([d_gate_b, d_up_b], axis=1)
    part_ffn = scattered_dp(outer_pair(fnormed_b, d_gateup_b, grad_flat, hidden_b)[0])
    d_fnorm = matmul_nt(d_gateup_b, full_gateup)
    d_mid_norm, g_fnorm = rms_backward(mid, factor_two, gain_two, d_fnorm)
    d_mid = grad_flat.astype(jnp.float32) + d_mid_norm
    d_mid_b = d_mid.astype(jnp.bfloat16)
    d_mixers = matmul(d_mid_b, full_mixer)
    d_mnorm = d_mixers[:, :inner_width]
    d_gated, g_inner = rms_backward(gated, factor_m, inner_norm, d_mnorm)
    d_ssm = d_gated * silu_z
    d_z = d_gated * ssm_out * silu_grad(gate_z)
    direct = ssm_direct(d_ssm, act, cols)
    d_att_b = d_mixers[:, inner_width:].astype(jnp.bfloat16)
    d_att_g = d_att_b.reshape(sequences, rows, KV_HEADS, group, HEAD)
    probs = jnp.exp(attention_scores() - lse)
    d_probs = jnp.einsum("stkgd,slkd->skgtl", d_att_g, values, preferred_element_type=jnp.float32)
    d_scores_b = (probs * (d_probs - jnp.sum(probs * d_probs, axis=-1, keepdims=True))).astype(
        jnp.bfloat16
    )
    d_query = (
        jnp.einsum("skgtl,slkd->stkgd", d_scores_b, keys, preferred_element_type=jnp.float32)
        * inv_root
    )
    d_keys = (
        jnp.einsum("skgtl,stkgd->slkd", d_scores_b, query_g, preferred_element_type=jnp.float32)
        * inv_root
    )
    d_values = jnp.einsum("skgtl,stkgd->slkd", probs_b, d_att_g, preferred_element_type=jnp.float32)
    d_kv_all = jnp.concatenate([d_keys, d_values], axis=2).reshape(sequences, window, kv_width)
    d_kv_local = d_kv_all[:, window - rows :]
    for far in range(1, hops + 1):
        start = window - (far + 1) * rows
        term = d_kv_all[:, start : start + rows].astype(jnp.bfloat16)
        d_kv_local = d_kv_local + passed_along(term, "seq", -far).astype(jnp.float32)
    d_kv_local = d_kv_local.reshape(sequences, rows, 2 * KV_HEADS, HEAD)
    d_key_local = rotate_back(d_kv_local[:, :, :KV_HEADS], cos_b, sin_b)
    d_kv_b = (
        jnp.concatenate([d_key_local, d_kv_local[:, :, KV_HEADS:]], axis=2)
        .reshape(total_rows, 2 * KV_HEADS * HEAD)
        .astype(jnp.bfloat16)
    )
    d_q_b = (
        rotate_back(d_query.reshape(sequences, rows, Q_HEADS, HEAD), cos_b, sin_b)
        .reshape(total_rows, Q_HEADS * HEAD)
        .astype(jnp.bfloat16)
    )
    d_early = jnp.concatenate([d_z.astype(jnp.bfloat16), d_q_b], axis=1)
    early_own, early_other = outer_pair(normed_b, d_early, d_mid_b, mixers_b, 2)
    early_pair = paired_cores(early_own, early_other)
    backlog = direct
    for hop in range(hops):
        later_grad = passed_along(backlog.astype(jnp.bfloat16), "seq", -1)
        if hop == 0:
            later_grad, early_pair, d_kv_all = lax.optimization_barrier(
                (later_grad, early_pair, d_kv_all)
            )
        backlog = direct + carry_rows * later_grad.astype(jnp.float32)
    d_carry = jnp.sum(
        (later_grad.astype(jnp.float32) * incoming.astype(jnp.float32)).reshape(
            SSM_HEADS, SSM_HEAD, STATE
        ),
        axis=(1, 2),
    )
    part_early = scattered_own(early_pair)
    d_xs, d_bmat, d_cmat, d_cols, d_rows = ssm_backward(
        d_ssm, act, ssm_out, cols, turned, bias_turned, incoming, later_grad, skip_row
    )
    d_pairs = d_cols[:, :, :6].reshape(SSM_PAIRS, rows, 3, 2).transpose(2, 1, 0, 3)
    d_pairs = d_pairs.reshape(3, rows, SSM_HEADS)
    d_sums = jnp.sum(d_rows.reshape(SSM_PAIRS, 2, 2, SSM_HEAD), axis=3).transpose(1, 0, 2)
    d_sums = d_sums.reshape(2, SSM_HEADS)
    g_skip = d_sums[1]
    d_decay = d_pairs[0] - d_pairs[2]
    d_rise = jnp.dot(ladder.T, d_decay, precision=lax.Precision.HIGHEST)
    d_rise = d_rise + (d_sums[0] + d_carry * carry)
    d_step = d_pairs[1] + d_rise * rate
    g_alog = jnp.sum(d_rise * step, axis=0) * rate
    d_act = jnp.concatenate([d_xs, d_bmat, d_cmat], axis=1).reshape(sequences, rows, channels)
    d_act, part_ffn = lax.optimization_barrier((d_act, part_ffn))
    owned_ffn, _ = hopped_seq(part_ffn, None)
    d_pre = d_act * silu_grad(conv_pre)
    g_cbias = jnp.sum(d_pre, axis=(0, 1))
    g_cweight = jnp.stack(
        [
            jnp.sum(d_pre * extended[:, tap : tap + rows] * tap_masks[tap], axis=(0, 1))
            for tap in range(taps)
        ]
    )
    d_padded = jnp.zeros_like(extended)
    for tap in range(taps):
        d_padded = d_padded + jnp.pad(
            d_pre * tap_masks[tap] * conv_weight[tap], ((0, 0), (tap, taps - 1 - tap), (0, 0))
        )
    edge_grad = passed_along(d_padded[:, : taps - 1], "seq", -1)
    d_inner = d_padded[:, taps - 1 :] + jnp.pad(edge_grad, ((0, 0), (rows - taps + 1, 0), (0, 0)))
    d_inner = d_inner.reshape(total_rows, channels)
    d_step_raw = d_step.reshape(total_rows, SSM_HEADS) * jax.nn.sigmoid(step_raw + dt_bias)
    g_dtb = jnp.sum(d_step_raw, axis=0)
    d_x_b = d_inner[:, :inner_width].astype(jnp.bfloat16)
    d_bc_b = d_inner[:, inner_width:].astype(jnp.bfloat16)
    d_st_b = d_step_raw.astype(jnp.bfloat16)
    d_late = jnp.concatenate(
        [
            d_x_b,
            d_bc_b,
            d_kv_b,
            d_st_b,
            jnp.zeros((total_rows, spare + 2), jnp.bfloat16),
        ],
        axis=1,
    )
    late_own, late_other = outer_pair(normed_b, d_late, None, None, 2)
    late_pair = paired_cores(late_own, late_other)
    d_norm = matmul_nt(d_early, full_in[:, :at_u]) + matmul_nt(d_late, full_in[:, at_u:])
    d_in_norm, g_mnorm = rms_backward(x_in, factor_one, gain_one, d_norm)
    grad_in = (d_mid + d_in_norm).astype(jnp.bfloat16).reshape(sequences, rows, width)
    smalls = jnp.concatenate([g_dtb, g_alog, g_skip])
    strips = [g_inner, g_mnorm, g_fnorm, smalls]
    packed = jnp.concatenate(
        [g_cweight, g_cbias[None]]
        + [jnp.pad(strip, (0, channels - strip.shape[0]))[None] for strip in strips],
        axis=0,
    )
    packed, late_pair = lax.optimization_barrier((packed, late_pair))
    part_late = scattered_own(late_pair)
    summed = summed_everywhere(packed)
    gain_rows = mixer_norm.shape[0]
    part_early, summed, grad_in = lax.optimization_barrier((part_early, summed, grad_in))
    owned_early, part_late = hopped_seq(part_early, part_late)
    owned_late = scattered_seq(part_late)
    owner = lax.axis_index("dpo") * 2 + lax.axis_index("core")
    first_row = (owner * lax.axis_size("seq") + lax.axis_index("seq")) * gain_rows
    g_mnorm_own = lax.dynamic_slice_in_dim(summed[taps + 2], first_row, gain_rows, 0)
    g_fnorm_own = lax.dynamic_slice_in_dim(summed[taps + 3], first_row, gain_rows, 0)
    at_mixers = at_u
    late_kv = at_kv - at_u
    late_dt = at_dt - at_u
    return (
        block_out,
        grad_in,
        owned_early[:, :at_q],
        owned_late[:, :inner_width],
        owned_late[:, inner_width:late_kv],
        owned_late[:, late_dt : late_dt + SSM_HEADS],
        owned_early[:, at_mixers : at_mixers + inner_width],
        owned_early[:, at_q:at_u],
        owned_late[:, late_kv:late_dt],
        owned_early[:, at_mixers + inner_width :],
        owned_ffn[:, :hidden_width],
        owned_ffn[:, hidden_width : 2 * hidden_width],
        owned_ffn[:, 2 * hidden_width :],
        g_mnorm_own,
        g_fnorm_own,
        summed[:taps],
        summed[taps],
        summed[taps + 4, :SSM_HEADS],
        summed[taps + 4, SSM_HEADS : 2 * SSM_HEADS],
        summed[taps + 4, 2 * SSM_HEADS : 3 * SSM_HEADS],
        summed[taps + 1, :inner_width],
    )


def solution(mesh):
    grid = mesh.devices
    mesh = Mesh(grid.reshape(grid.shape[0] // 2, 2, grid.shape[1]), DP + ("seq",))
    in_specs = (
        P(DP, "seq", None),
        P(DP, None),
        P(DP + ("seq",), None),
        P(DP + ("seq",), None),
        P(DP + ("seq",), None),
        P(DP + ("seq",), None),
        P(DP + ("seq",), None),
        P(DP + ("seq",), None),
        P(DP + ("seq",), None),
        P(DP + ("seq",), None),
        P(DP + ("seq",), None),
        P(DP + ("seq",), None),
        P(DP + ("seq",), None),
        P(DP + ("seq",)),
        P(DP + ("seq",)),
        P(),
        P(),
        P(),
        P(),
        P(),
        P(),
        P(DP, "seq", None),
    )
    out_specs = (
        P(DP, "seq", None),
        P(DP, "seq", None),
        P(DP + ("seq",), None),
        P(DP + ("seq",), None),
        P(DP + ("seq",), None),
        P(DP + ("seq",), None),
        P(DP + ("seq",), None),
        P(DP + ("seq",), None),
        P(DP + ("seq",), None),
        P(DP + ("seq",), None),
        P(DP + ("seq",), None),
        P(DP + ("seq",), None),
        P(DP + ("seq",), None),
        P(DP + ("seq",)),
        P(DP + ("seq",)),
        P(),
        P(),
        P(),
        P(),
        P(),
        P(),
    )
    return jax.shard_map(local, mesh=mesh, in_specs=in_specs, out_specs=out_specs, check_vma=False)
```
